32 devices in a mesh: row: 4 (over z), col: 8 (over y, x, core).
Axes of the slice: x: 2, y: 2, z: 4, core: 2. Of those that a mesh axis runs over, the one named last changes fastest.
Arguments:
- tokens: bfloat16 [16384, 2048], P('row', 'col'), may hold values from -8 to 8
- norm_gain: float32 [2048], P('col'), may hold values from 0.5 to 1.5
- norm_bias: float32 [2048], P('col'), may hold values from -3 to 3
- qkv_weight: bfloat16 [2048, 3, 2048], P('row', None, 'col'), may hold values from -0.125 to 0.125
- gate_up_weight: bfloat16 [2048, 2, 5632], P('row', None, 'col'), may hold values from -0.125 to 0.125
- out_weight: bfloat16 [2048, 2048], P('row', 'col'), may hold values from -1 to 1
- down_weight: bfloat16 [2048, 5632], P('row', 'col'), may hold values from -0.078125 to 0.078125
- image_start: int32 [16], P('row'), may hold values from 0 to 768
- doc_ids: int32 [16, 1024], P('row'), may hold values from 0 to 3, never falling along the last dimension, each value on 1 to 512 neighbouring positions
- out_grad: bfloat16 [16384, 2048], P('row', 'col'), may hold values from -8 to 8
Outputs:
- layer_out: bfloat16 [16384, 2048], P('row', 'col')
- input_grad: float32 [16384, 2048], P('row', 'col')
- norm_gain_grad: float32 [2048], P('col')
- norm_bias_grad: float32 [2048], P('col')
- qkv_weight_grad: float32 [2048, 3, 2048], P('row', None, 'col')
- gate_up_weight_grad: float32 [2048, 2, 5632], P('row', None, 'col')
- out_weight_grad: float32 [2048, 2048], P('row', 'col')
- down_weight_grad: float32 [2048, 5632], P('row', 'col')
The draws below stay inside these ranges and needn't reach their ends.
Inputs may be any that keep to these rules, and one draw needn't show every extreme that they name: `image_start`: the image piece lies inside its sequence. `doc_ids`: never falls along a sequence; a document holds 1 to 512 tokens.
All inputs are finite; a program needn't handle non-finite values.
Results may differ from the reference program's by a relative error of at most 0.012.
Values may be sent and summed in bfloat16 or wider, within the bound.
A program may use at most 256 MiB of HBM per device.

```python
import math
import jax
import jax.numpy as jnp
import numpy as np
from jax import lax

D = 2048
H = 32
HD = 64
ROT = 16
FF = 5632
LEN = 1024
IMG = 256
SEQ_ROW = 4
SEQS = 16
TOKENS = 16384


def draw_tokens(key, part):
    noise_key = jax.random.fold_in(jax.random.fold_in(key, 11), 0)
    feature_scale = 0.6 * 3.0 ** (jnp.arange(D).astype(jnp.float32) / D)
    values = jax.random.normal(noise_key, (TOKENS, D), jnp.float32) * feature_scale[None, :]
    return jnp.clip(values, -8.0, 8.0).astype(jnp.bfloat16)


def draw_out_grad(key, part):
    noise_key = jax.random.fold_in(jax.random.fold_in(key, 23), 0)
    token_scale = 3.0 ** (jnp.arange(TOKENS).astype(jnp.float32) / TOKENS - 0.5)
    feature_scale = 3.0 ** (0.5 - jnp.arange(D).astype(jnp.float32) / D)
    scale = token_scale[:, None] * feature_scale[None, :]
    values = jax.random.normal(noise_key, (TOKENS, D), jnp.float32) * scale
    return jnp.clip(values, -8.0, 8.0).astype(jnp.bfloat16)


def set_ends(values, own_key, smallest, top_value):
    dims = values.shape
    place = [jax.random.randint(jax.random.fold_in(own_key, axis), (), 0, dims[axis]) for axis in range(len(dims))]
    values = values.at[tuple(place)].set(smallest)
    longest = dims.index(max(dims))
    place[longest] = (place[longest] + 1) % dims[longest]
    return values.at[tuple(place)].set(top_value)


def steps_of(own_key, shape, cuts, least, largest):
    loudness, own = 1.0, jax.random.fold_in(own_key, 6)
    for position, parts in cuts:
        draws = jnp.exp(jax.random.uniform(jax.random.fold_in(own, position), (parts,), jnp.float32, least / len(cuts), largest / len(cuts)))
        loudness = loudness * jnp.repeat(draws, shape[position] // parts).reshape([-1 if axis == position else 1 for axis in range(len(shape))])
    return loudness


def profile(number_of, total, limit, slope):
    portions = [(1 << 20) // math.isqrt(grade ** slope) + 1 for grade in range(2, number_of + 1)]
    spare, counts = total - limit - (number_of - 1), [1] * (number_of - 1)
    while spare > 0:
        movable = [i for i in range(number_of - 1) if counts[i] < limit]
        pool, left = sum([portions[i] for i in movable]), spare
        for i in movable:
            more = min(limit - counts[i], max(1, left * portions[i] // pool), spare)
            counts[i] = counts[i] + more
            spare = spare - more
    return np.array([limit] + counts)


def ragged(stream_key, number_of, total, reach, skew):
    if number_of == 2:
        one = jax.random.randint(stream_key, (), max(1, total - reach), min(reach, total - 1) + 1)
        return jnp.stack([one, total - one])
    tallies = jnp.asarray(profile(number_of, total, reach, skew), jnp.int32)
    pairs = (number_of - 1) // 2
    donor, receiver = tallies[1:1 + 2 * pairs:2], tallies[2:2 + 2 * pairs:2]
    slack = jnp.minimum(donor - 1, reach - receiver)
    passed = jax.random.randint(jax.random.fold_in(stream_key, 1), (pairs,), 0, 1 << 20) % (slack + 1)
    tallies = tallies.at[1:1 + 2 * pairs:2].set(donor - passed).at[2:2 + 2 * pairs:2].set(receiver + passed)
    return tallies[jax.random.permutation(jax.random.fold_in(stream_key, 2), number_of)]


def centred(own_key, dims, deviation, reach, cuts=(), kind=jnp.bfloat16):
    values = deviation * jax.random.normal(own_key, dims, jnp.float32)
    if cuts:
        values = values * steps_of(own_key, dims, cuts, -0.22, 0.18)
    return jnp.clip(values, -reach, reach).astype(kind)


def setup_inputs(seed: int = 0) -> dict:
    arg_keys = jax.random.split(jax.random.key(seed), 11)
    tokens = draw_tokens(jax.random.fold_in(arg_keys[10], 71), 0)
    norm_gain = jnp.clip(1.0 + 0.1 * jax.random.normal(arg_keys[1], (D,), jnp.float32), 0.5, 1.5)
    norm_bias = centred(arg_keys[2], (D,), 0.5, 3.0, ((0, 8),), jnp.float32)
    qkv_weight = centred(arg_keys[3], (D, 3, D), D ** -0.5, 0.125, ((0, 4), (2, 8)))
    gate_up_weight = centred(arg_keys[4], (D, 2, FF), D ** -0.5, 0.125, ((0, 4), (2, 8)))
    out_weight = centred(arg_keys[5], (D, D), (D // 64) ** -0.5, 1.0, ((0, 4), (1, 8)))
    down_weight = centred(arg_keys[6], (D, FF), FF ** -0.5, 0.078125, ((0, 4), (1, 8)))
    image_start = set_ends(jax.random.randint(arg_keys[7], (SEQS,), 0, LEN - IMG + 1), jax.random.fold_in(arg_keys[7], 1), 0, LEN - IMG).astype(jnp.int32)
    doc_ids = jax.vmap(lambda own: jnp.searchsorted(jnp.cumsum(ragged(own, 4, LEN, LEN // 2, 1)), jnp.arange(LEN), side="right"))(jax.random.split(arg_keys[8], SEQS)).reshape((SEQS, LEN)).astype(jnp.int32)
    out_grad = draw_out_grad(jax.random.fold_in(arg_keys[10], 71), 0)
    return {"tokens": tokens, "norm_gain": norm_gain, "norm_bias": norm_bias, "qkv_weight": qkv_weight, "gate_up_weight": gate_up_weight, "out_weight": out_weight, "down_weight": down_weight, "image_start": image_start, "doc_ids": doc_ids, "out_grad": out_grad}


NORM_EPS = 1e-05
MASKED_SCORE = -1e+30
ROPE_BASE = 10000.0
HIGHEST = lax.Precision.HIGHEST

@jax.custom_vjp
def low(v):
    return lax.optimization_barrier(v.astype(jnp.bfloat16)).astype(jnp.float32)

@jax.custom_vjp
def low_back(v):
    return v

def low_keep(v):
    return (low(v), None)

def low_pass(kept, grad):
    return (grad,)

def back_keep(v):
    return (v, None)

def back_low(kept, grad):
    return (low(grad),)
low.defvjp(low_keep, low_pass)
low_back.defvjp(back_keep, back_low)

def rotate(values):
    half_rot = ROT // 2
    places = jnp.arange(LEN).astype(jnp.float32)
    inv_freq = ROPE_BASE ** (-2.0 * jnp.arange(half_rot).astype(jnp.float32) / ROT)
    angles = places[:, None] * inv_freq[None, :]
    cosines = jnp.cos(angles)[:, None, :]
    sines = jnp.sin(angles)[:, None, :]
    first_half = values[..., :half_rot]
    second_half = values[..., half_rot:ROT]
    return jnp.concatenate([first_half * cosines - second_half * sines, second_half * cosines + first_half * sines, values[..., ROT:]], axis=-1)

def allowed_pairs(doc_row, img_start):
    places = jnp.arange(LEN)
    causal = places[:, None] >= places[None, :]
    inside = (places >= img_start) & (places < img_start + IMG)
    same_doc = doc_row[:, None] == doc_row[None, :]
    return same_doc & (causal | inside[:, None] & inside[None, :])

def block_forward(inputs, norm_gain, norm_bias, qkv_weight, gate_up_weight, out_weight, down_weight, starts, documents):
    row_mean = lax.optimization_barrier(jnp.mean(inputs, axis=1, keepdims=True))
    centered = inputs - row_mean
    row_var = lax.optimization_barrier(jnp.mean(centered * centered, axis=1, keepdims=True))
    normed = low(centered * lax.rsqrt(row_var + NORM_EPS) * norm_gain + norm_bias)
    projected = low_back(jnp.dot(normed, qkv_weight.reshape(D, 3 * D), precision=HIGHEST))
    count = inputs.shape[0] // LEN
    queries = low(rotate(projected[:, :D].reshape(count, LEN, H, HD)))
    key_rows = low(rotate(projected[:, D:2 * D].reshape(count, LEN, H, HD)))
    value_rows = low(projected[:, 2 * D:].reshape(count, LEN, H, HD))

    def one_sequence(items):
        seq_queries, seq_keys, seq_values, img_start, doc_row = items
        scores = low_back(jnp.einsum('qhd,khd->hqk', seq_queries, seq_keys, precision=HIGHEST) * HD ** (-0.5))
        scores = jnp.where(allowed_pairs(doc_row, img_start)[None], scores, MASKED_SCORE)
        attn_probs = low(jax.nn.softmax(scores, axis=-1))
        return jnp.einsum('hqk,khd->qhd', attn_probs, seq_values, precision=HIGHEST)
    attended = lax.map(jax.checkpoint(one_sequence), (queries, key_rows, value_rows, starts, documents))
    attended = low_back(low(attended.reshape(inputs.shape[0], D)))
    gate_up = jnp.dot(normed, gate_up_weight.reshape(D, 2 * FF), precision=HIGHEST)
    gate_pre = low_back(gate_up[:, :FF])
    up_pre = low_back(gate_up[:, FF:])
    hidden = low(jax.nn.silu(gate_pre) * up_pre)
    attn_branch = jnp.dot(attended, out_weight.T, precision=HIGHEST)
    ffn_branch = jnp.dot(hidden, down_weight.T, precision=HIGHEST)
    return inputs + attn_branch + ffn_branch

def reference(tokens, norm_gain, norm_bias, qkv_weight, gate_up_weight, out_weight, down_weight, image_start, doc_ids, out_grad):
    params = (norm_gain.astype(jnp.float32), norm_bias.astype(jnp.float32), qkv_weight.astype(jnp.float32), gate_up_weight.astype(jnp.float32), out_weight.astype(jnp.float32), down_weight.astype(jnp.float32))
    block_rows = SEQ_ROW * LEN
    groups = TOKENS // block_rows
    inputs = tokens.astype(jnp.float32).reshape(groups, block_rows, D)
    grads_in = out_grad.astype(jnp.float32).reshape(groups, block_rows, D)
    starts = image_start.reshape(groups, SEQ_ROW)
    documents = doc_ids.reshape(groups, SEQ_ROW, LEN)

    def one_group(totals, items):
        group_inputs, group_grad, group_starts, group_docs = items

        def forward(block_inputs, weights):
            return block_forward(block_inputs, weights[0], weights[1], weights[2], weights[3], weights[4], weights[5], group_starts, group_docs)
        outputs, pullback = jax.vjp(forward, group_inputs, params)
        block_input_grad, weight_grads = pullback(group_grad)
        totals = jax.tree.map(lambda first, second: first + second, totals, weight_grads)
        return (totals, (outputs.astype(jnp.bfloat16), block_input_grad))
    zeros = jax.tree.map(jnp.zeros_like, params)
    totals, (outputs, input_grads) = lax.scan(one_group, zeros, (inputs, grads_in, starts, documents))
    return (outputs.reshape(TOKENS, D), input_grads.reshape(TOKENS, D), totals[0], totals[1], totals[2], totals[3], totals[4], totals[5])
```

```python
import functools

import jax
import jax.numpy as jnp
from jax import lax
from jax.experimental import pallas as pl
from jax.experimental.pallas import tpu as pltpu
from jax.sharding import PartitionSpec as P

D = 2048
HD = 64
ROT = 16
LEN = 1024
IMG = 256
QB = 256
MB = 512


NORM_EPS = 1e-05
MESH = pl.DeviceIdType.MESH
MASKED_SCORE = -1e30
ROPE_BASE = 10000.0


def contract(left, right, left_dim, right_dim):
    return lax.dot_general(
        left, right, (((left_dim,), (right_dim,)), ((), ())), preferred_element_type=jnp.float32
    )


def rope_tables(width):
    half = ROT // 2
    places = jnp.arange(LEN).astype(jnp.float32)
    inv_freq = ROPE_BASE ** (-2.0 * jnp.arange(half).astype(jnp.float32) / ROT)
    angles = places[:, None] * inv_freq[None, :]
    cosines, sines = jnp.cos(angles), jnp.sin(angles)
    rest = HD - ROT
    c = jnp.concatenate([cosines, cosines, jnp.ones((LEN, rest), jnp.float32)], axis=1)
    a = jnp.concatenate([-sines, jnp.zeros((LEN, HD - half), jnp.float32)], axis=1)
    b = jnp.concatenate(
        [jnp.zeros((LEN, half), jnp.float32), sines, jnp.zeros((LEN, rest), jnp.float32)], axis=1
    )
    heads = width // HD
    return tuple(jnp.tile(t, (1, heads)) for t in (c, a, b))


def spans(doc_ids, image_start):
    places = jnp.arange(LEN, dtype=jnp.int32)
    first = jnp.sum(doc_ids[:, None, :] < doc_ids[:, :, None], axis=2, dtype=jnp.int32)
    last = jnp.sum(doc_ids[:, None, :] <= doc_ids[:, :, None], axis=2, dtype=jnp.int32) - 1
    start = image_start[:, None]
    inside = (places[None] >= start) & (places[None] < start + IMG)
    final = jnp.where(inside, jnp.minimum(last, start + IMG - 1), places[None])
    return first, final


def attention_kernel(
    heads,
    low_ref,
    high_ref,
    x_ref,
    g_ref,
    w_ref,
    first_ref,
    final_ref,
    c_ref,
    a_ref,
    b_ref,
    att_ref,
    gp_ref,
    ga_scr,
    q_scr,
    k_scr,
    v_scr,
    qt_scr,
    gt_scr,
    ks_scr,
    vs_scr,
    s_scr,
    d_scr,
    p_scr,
    ds_scr,
    bias_scr,
    m_scr,
    l_scr,
    e_scr,
    o_scr,
    dq_scr,
    dkt_scr,
    dvt_scr,
):
    f32, bf16 = jnp.float32, jnp.bfloat16
    width = heads * HD
    blocks = LEN // QB
    seq = pl.program_id(0)
    nt = (((1,), (1,)), ((), ()))
    lane = lax.broadcasted_iota(jnp.int32, (1, width), 1) // HD

    def turn(x, sl, sign):
        left = pltpu.roll(x, width - ROT // 2, 1)
        right = pltpu.roll(x, ROT // 2, 1)
        return x * c_ref[sl, :] + (left * a_ref[sl, :] + right * b_ref[sl, :]) * sign

    for i in range(blocks):
        sl = pl.ds(i * QB, QB)
        x = x_ref[sl, :]
        q, k, v = (
            jnp.dot(x, w_ref[:, kind * width : (kind + 1) * width], preferred_element_type=f32)
            for kind in range(3)
        )
        g = jnp.dot(g_ref[sl, :], w_ref[:, 3 * width :], preferred_element_type=f32)
        ga_scr[sl, :] = g.astype(bf16)
        g = ga_scr[sl, :]
        q = turn(q, sl, 1.0).astype(bf16).astype(f32) * (HD**-0.5)
        q_scr[sl, :] = q.astype(bf16)
        qt_scr[:, sl] = q.T.astype(bf16)
        k = turn(k, sl, 1.0).astype(bf16)
        v = v.astype(bf16)
        k_scr[sl, :] = k
        v_scr[sl, :] = v
        gt_scr[:, sl] = g.astype(f32).T.astype(bf16)
        for h in range(heads):
            keep = lane == h
            ks_scr[i, pl.ds(h * QB, QB), :] = jnp.where(keep, k, jnp.zeros_like(k))
            vs_scr[i, pl.ds(h * QB, QB), :] = jnp.where(keep, v, jnp.zeros_like(v))
    dkt_scr[...] = jnp.zeros_like(dkt_scr)
    dvt_scr[...] = jnp.zeros_like(dvt_scr)

    def query_block(i, _):
        rows = pl.ds(pl.multiple_of(i * QB, QB), QB)
        low, high = low_ref[seq, i], high_ref[seq, i]
        q = q_scr[rows, :]
        g = ga_scr[rows, :]
        zero = jnp.zeros_like(q)
        q_all = jnp.concatenate([jnp.where(lane == h, q, zero) for h in range(heads)], axis=0)
        g_all = jnp.concatenate([jnp.where(lane == h, g, zero) for h in range(heads)], axis=0)
        m_scr[...] = jnp.full_like(m_scr, MASKED_SCORE)
        first = first_ref[rows, :]
        final = final_ref[rows, :]

        def score(kb, _):
            keys = pl.ds(pl.multiple_of(kb * QB, QB), QB)
            s = lax.dot_general(q_all, k_scr[keys, :], nt, preferred_element_type=f32)
            d = lax.dot_general(g_all, v_scr[keys, :], nt, preferred_element_type=f32)
            col = lax.broadcasted_iota(jnp.int32, (QB, QB), 1) + kb * QB
            bias_scr[...] = jnp.where((col >= first) & (col <= final), 0.0, MASKED_SCORE)
            d_scr[kb] = d
            for h in range(heads):
                hs = slice(h * QB, (h + 1) * QB)
                x = s[hs] + bias_scr[...]
                s_scr[kb, hs, :] = x
                top = m_scr[hs, :]
                for j in range(QB // 128):
                    top = jnp.maximum(top, x[:, j * 128 : (j + 1) * 128])
                m_scr[hs, :] = top
            return 0

        lax.fori_loop(low, high + 1, score, 0)
        for h in range(heads):
            hs = slice(h * QB, (h + 1) * QB)
            m_scr[hs, :] = jnp.broadcast_to(jnp.max(m_scr[hs, :], axis=1, keepdims=True), (QB, 128))
        l_scr[...] = jnp.zeros_like(l_scr)
        e_scr[...] = jnp.zeros_like(e_scr)

        def expo(kb, _):
            for h in range(heads):
                hs = slice(h * QB, (h + 1) * QB)
                top, tot, dot = m_scr[hs, :], l_scr[hs, :], e_scr[hs, :]
                for j in range(QB // 128):
                    js = slice(j * 128, (j + 1) * 128)
                    e = jnp.exp(s_scr[kb, hs, js] - top)
                    s_scr[kb, hs, js] = e
                    tot = tot + e
                    dot = dot + e * d_scr[kb, hs, js]
                l_scr[hs, :] = tot
                e_scr[hs, :] = dot
            return 0

        lax.fori_loop(low, high + 1, expo, 0)
        for h in range(heads):
            hs = slice(h * QB, (h + 1) * QB)
            inv = 1.0 / jnp.sum(l_scr[hs, :], axis=1, keepdims=True)
            delta = jnp.sum(e_scr[hs, :], axis=1, keepdims=True) * inv
            l_scr[hs, :] = jnp.broadcast_to(inv, (QB, 128))
            e_scr[hs, :] = jnp.broadcast_to(delta, (QB, 128))
        o_scr[...] = jnp.zeros_like(o_scr)
        dq_scr[...] = jnp.zeros_like(dq_scr)

        def back(kb, _):
            keys = pl.ds(pl.multiple_of(kb * QB, QB), QB)
            for h in range(heads):
                hs = slice(h * QB, (h + 1) * QB)
                inv, delta = l_scr[hs, :], e_scr[hs, :]
                for j in range(QB // 128):
                    js = slice(j * 128, (j + 1) * 128)
                    out = slice(h * QB + j * 128, h * QB + (j + 1) * 128)
                    p = s_scr[kb, hs, js] * inv
                    p_scr[:, out] = p.astype(bf16)
                    ds_scr[:, out] = (p * (d_scr[kb, hs, js] - delta)).astype(bf16)
            o_scr[...] += jnp.dot(p_scr[...], vs_scr[kb], preferred_element_type=f32)
            dq_scr[...] += jnp.dot(ds_scr[...], ks_scr[kb], preferred_element_type=f32)
            for h in range(heads):
                hs = slice(h * HD, (h + 1) * HD)
                cs = slice(h * QB, (h + 1) * QB)
                dkt_scr[hs, keys] += jnp.dot(
                    qt_scr[hs, rows], ds_scr[:, cs], preferred_element_type=f32
                )
                dvt_scr[hs, keys] += jnp.dot(
                    gt_scr[hs, rows], p_scr[:, cs], preferred_element_type=f32
                )
            return 0

        lax.fori_loop(low, high + 1, back, 0)
        att_ref[rows, :] = o_scr[...].astype(bf16)
        gp_ref[rows, :width] = turn(dq_scr[...] * (HD**-0.5), rows, -1.0).astype(bf16)
        return 0

    lax.fori_loop(0, blocks, query_block, 0)
    for i in range(blocks):
        sl = pl.ds(i * QB, QB)
        gp_ref[sl, width : 2 * width] = turn(dkt_scr[:, sl].T, sl, -1.0).astype(bf16)
        gp_ref[sl, 2 * width :] = dvt_scr[:, sl].T.astype(bf16)


def attention(normed, grad, weights, doc_ids, image_start):
    rows, width = normed.shape[0], weights.shape[1] // 4
    count = rows // LEN
    heads = width // HD
    blocks = LEN // QB
    first, final = spans(doc_ids, image_start)
    low = jnp.min(first.reshape(count, blocks, QB), axis=2) // QB
    high = jnp.max(final.reshape(count, blocks, QB), axis=2) // QB
    f32, bf16 = jnp.float32, jnp.bfloat16
    seq_rows = lambda s, *_: (s, 0)
    fixed = lambda s, *_: (0, 0)
    return pl.pallas_call(
        functools.partial(attention_kernel, heads),
        out_shape=(
            jax.ShapeDtypeStruct((rows, width), bf16),
            jax.ShapeDtypeStruct((rows, 3 * width), bf16),
        ),
        grid_spec=pltpu.PrefetchScalarGridSpec(
            num_scalar_prefetch=2,
            grid=(count,),
            in_specs=[
                pl.BlockSpec((LEN, D), seq_rows),
                pl.BlockSpec((LEN, D), seq_rows),
                pl.BlockSpec((D, 4 * width), fixed, pipeline_mode=pl.Buffered(1)),
                pl.BlockSpec((LEN, 1), seq_rows),
                pl.BlockSpec((LEN, 1), seq_rows),
                pl.BlockSpec((LEN, width), fixed, pipeline_mode=pl.Buffered(1)),
                pl.BlockSpec((LEN, width), fixed, pipeline_mode=pl.Buffered(1)),
                pl.BlockSpec((LEN, width), fixed, pipeline_mode=pl.Buffered(1)),
            ],
            out_specs=[
                pl.BlockSpec((LEN, width), seq_rows),
                pl.BlockSpec((LEN, 3 * width), seq_rows),
            ],
            scratch_shapes=[
                pltpu.VMEM((LEN, width), bf16),
                pltpu.VMEM((LEN, width), bf16),
                pltpu.VMEM((LEN, width), bf16),
                pltpu.VMEM((LEN, width), bf16),
                pltpu.VMEM((width, LEN), bf16),
                pltpu.VMEM((width, LEN), bf16),
                pltpu.VMEM((blocks, heads * QB, width), bf16),
                pltpu.VMEM((blocks, heads * QB, width), bf16),
                pltpu.VMEM((blocks, heads * QB, QB), f32),
                pltpu.VMEM((blocks, heads * QB, QB), f32),
                pltpu.VMEM((QB, heads * QB), bf16),
                pltpu.VMEM((QB, heads * QB), bf16),
                pltpu.VMEM((QB, QB), f32),
                pltpu.VMEM((heads * QB, 128), f32),
                pltpu.VMEM((heads * QB, 128), f32),
                pltpu.VMEM((heads * QB, 128), f32),
                pltpu.VMEM((QB, width), f32),
                pltpu.VMEM((QB, width), f32),
                pltpu.VMEM((width, LEN), f32),
                pltpu.VMEM((width, LEN), f32),
            ],
        ),
        compiler_params=pltpu.CompilerParams(
            dimension_semantics=("arbitrary",), vmem_limit_bytes=58 << 20
        ),
        cost_estimate=pl.CostEstimate(
            flops=12 * rows * 640 * width * 3 + 8 * rows * D * width,
            bytes_accessed=rows * (width * 8 + D * 4) + 8 * D * width,
            transcendentals=rows * 640 * heads,
        ),
        name="attention",
    )(
        low,
        high,
        normed,
        grad,
        weights,
        first.reshape(rows, 1),
        final.reshape(rows, 1),
        *rope_tables(width),
    )


NT = (((1,), (1,)), ((), ()))


def ffn_kernel(x_ref, g_ref, wgu_ref, wd_ref, hidden_ref, gg_ref, gu_ref):
    f32, bf16 = jnp.float32, jnp.bfloat16
    x = x_ref[...]
    gate = lax.dot_general(x, wgu_ref[0], NT, preferred_element_type=f32)
    up = lax.dot_general(x, wgu_ref[1], NT, preferred_element_type=f32)
    grad = lax.dot_general(g_ref[...], wd_ref[...], NT, preferred_element_type=f32)
    sigma = jax.nn.sigmoid(gate)
    silu = gate * sigma
    hidden_ref[...] = (silu * up).astype(bf16)
    gg_ref[...] = (grad * up * (sigma + silu * (1.0 - sigma))).astype(bf16)
    gu_ref[...] = (grad * silu).astype(bf16)


def feed_forward(normed, grad, wgu, wd):
    rows, ffn = normed.shape[0], wd.shape[0]
    block = lambda i: (i, 0)
    return pl.pallas_call(
        ffn_kernel,
        out_shape=[jax.ShapeDtypeStruct((rows, ffn), jnp.bfloat16)] * 3,
        grid=(rows // MB,),
        in_specs=[
            pl.BlockSpec((MB, D), block),
            pl.BlockSpec((MB, D), block),
            pl.BlockSpec((2, ffn, D), lambda i: (0, 0, 0), pipeline_mode=pl.Buffered(1)),
            pl.BlockSpec((ffn, D), lambda i: (0, 0), pipeline_mode=pl.Buffered(1)),
        ],
        out_specs=[pl.BlockSpec((MB, ffn), block)] * 3,
        compiler_params=pltpu.CompilerParams(
            dimension_semantics=("arbitrary",), vmem_limit_bytes=56 << 20
        ),
        cost_estimate=pl.CostEstimate(
            flops=6 * rows * D * ffn,
            bytes_accessed=rows * (4 * D + 6 * ffn) + 6 * D * ffn,
            transcendentals=rows * ffn,
        ),
        name="feed_forward",
    )(normed, grad, wgu, wd)


def flip(index, bits):
    bit = 1
    while bit <= bits:
        if bits & bit:
            index = index + bit - 2 * bit * ((index // bit) % 2)
        bit *= 2
    return index


def chip_orders(ways):
    bits = [1 << k for k in range(1, ways.bit_length() - 1)]
    return bits, bits[::-1]


def held(bits):
    found = [0]
    for bit in bits:
        found += [o ^ bit for o in found]
    return found


def meet(peers):
    barrier = pltpu.get_barrier_semaphore()
    for peer in peers:
        pl.semaphore_signal(barrier, inc=1, device_id=peer, device_id_type=MESH)
    pl.semaphore_wait(barrier, len(peers))


def gather_kernel(
    ways,
    pairs,
    token_ref,
    grad_ref,
    vector_ref,
    normed_ref,
    full_ref,
    stat_ref,
    vectors_ref,
    both,
    ready,
    load_sem,
    store_sem,
    full_sem,
    send_sem,
    recv_sem,
    vsend_sem,
    vrecv_sem,
):
    f32, bf16 = jnp.float32, jnp.bfloat16
    me = lax.axis_index("col")
    rows, width = token_ref.shape
    part = rows // pairs
    orders = chip_orders(ways)
    phases = len(orders[0])
    loads = [
        pltpu.make_async_copy(token_ref, both.at[me, :, pl.ds(0, width)], load_sem.at[0]),
        pltpu.make_async_copy(grad_ref, both.at[me, :, pl.ds(width, width)], load_sem.at[1]),
    ]
    for load in loads:
        load.start()
    mine = pl.ds(pl.multiple_of(me * width, width), width)
    vectors_ref[:, mine] = vector_ref[...]
    peers = [flip(me, k) for k in range(1, ways)]
    meet([{"col": peer} for peer in peers])

    def vector_copy(k):
        return pltpu.make_async_remote_copy(
            src_ref=vectors_ref.at[:, mine],
            dst_ref=vectors_ref.at[:, mine],
            send_sem=vsend_sem.at[k],
            recv_sem=vrecv_sem.at[k],
            device_id={"col": peers[k]},
            device_id_type=MESH,
        )

    for k in range(ways - 1):
        vector_copy(k).start()
    for load in loads:
        load.wait()

    def copies(p, phase):
        for k, order in enumerate(orders):
            bit = order[phase] if phase < phases else 1
            place = pl.ds(p * part + k * (part // 2), part // 2)
            for o in held(order[:phase]):
                index = (p * 2 + k) * ways + (o ^ bit)
                owner = flip(me, o)
                yield pltpu.make_async_remote_copy(
                    src_ref=both.at[owner, place],
                    dst_ref=both.at[owner, place],
                    send_sem=send_sem.at[index],
                    recv_sem=recv_sem.at[index],
                    device_id={"col": flip(me, bit)},
                    device_id_type=MESH,
                )

    def start(p, phase):
        if p < pairs:
            for copy in copies(p, phase):
                copy.start()

    def arrive(p, phase):
        for copy in copies(p, phase):
            copy.wait_recv()

    def stored(p):
        return pltpu.make_async_copy(
            ready.at[p % 2], normed_ref.at[pl.ds(p * part, part)], store_sem.at[p % 2]
        )

    def full_done(p):
        rows_p = full_ref.at[pl.ds(p * part, part)]
        return pltpu.make_async_copy(rows_p, rows_p, full_sem.at[p])

    def work(p):
        place = pl.ds(p * part, part)
        for b in range(ways):
            pltpu.make_async_copy(
                both.at[b, place, pl.ds(width, width)],
                full_ref.at[place, pl.ds(b * width, width)],
                full_sem.at[p],
            ).start()
        if p >= 2:
            stored(p - 2).wait()

        def block(j, _):
            own = pl.ds(pl.multiple_of(j * QB, QB), QB)
            at = pl.ds(pl.multiple_of(p * part + j * QB, QB), QB)
            sums = sum(both[b, at, :width].astype(f32) for b in range(ways))
            mean = jnp.sum(sums, axis=1, keepdims=True) / D
            squares = jnp.zeros((QB, width), f32)
            for b in range(ways):
                x = both[b, at, :width].astype(f32) - mean
                squares += x * x
            inv = lax.rsqrt(jnp.sum(squares, axis=1, keepdims=True) / D + NORM_EPS)
            stat_ref[at, :1] = mean
            stat_ref[at, 1:] = inv
            for b in range(ways):
                cols = slice(b * width, (b + 1) * width)
                x = (both[b, at, :width].astype(f32) - mean) * inv
                ready[p % 2, own, cols] = (
                    x * vectors_ref[0:1, cols] + vectors_ref[1:2, cols]
                ).astype(bf16)
            return 0

        lax.fori_loop(0, part // QB, block, 0)
        stored(p).start()

    start(0, 0)
    start(1, 0)
    for k in range(ways - 1):
        vector_copy(k).wait_recv()
    for p in range(pairs):
        for phase in range(phases):
            arrive(p, phase)
            start(p, phase + 1)
            if phase == 0:
                start(p + 2, 0)
                if p >= 1:
                    arrive(p - 1, phases)
                    work(p - 1)
    arrive(pairs - 1, phases)
    work(pairs - 1)
    for p in range(pairs):
        full_done(p).wait()
        for phase in range(phases + 1):
            for copy in copies(p, phase):
                copy.wait_send()
    for p in range(max(pairs - 2, 0), pairs):
        stored(p).wait()
    for k in range(ways - 1):
        vector_copy(k).wait_send()


def gather(tokens, out_grad, vectors, ways):
    rows, width = tokens.shape
    pairs = rows // LEN
    bf16, f32 = jnp.bfloat16, jnp.float32
    anywhere = pl.BlockSpec(memory_space=pl.ANY)
    vmem = pl.BlockSpec(memory_space=pltpu.VMEM)
    dma = pltpu.SemaphoreType.DMA
    return pl.pallas_call(
        functools.partial(gather_kernel, ways, pairs),
        out_shape=[
            jax.ShapeDtypeStruct((rows, D), bf16),
            jax.ShapeDtypeStruct((rows, D), bf16),
            jax.ShapeDtypeStruct((rows, 2), f32),
            jax.ShapeDtypeStruct((8, D), f32),
        ],
        in_specs=[anywhere, anywhere, vmem],
        out_specs=[anywhere, anywhere, vmem, vmem],
        scratch_shapes=[
            pltpu.VMEM((ways, rows, 2 * width), bf16),
            pltpu.VMEM((2, rows // pairs, D), bf16),
            dma((2,)),
            dma((2,)),
            dma((pairs,)),
            dma((pairs * 2 * ways,)),
            dma((pairs * 2 * ways,)),
            dma((ways - 1,)),
            dma((ways - 1,)),
        ],
        compiler_params=pltpu.CompilerParams(
            collective_id=0, has_side_effects=True, vmem_limit_bytes=56 << 20
        ),
        cost_estimate=pl.CostEstimate(
            flops=200 * rows * D * D // ways, bytes_accessed=rows * D * 8, transcendentals=0
        ),
        name="gather",
    )(tokens, out_grad, vectors)


class Reducer:
    def __init__(self, ways, parts, inbox, send_sem, recv_sem):
        self.ways, self.parts, self.inbox = ways, parts, inbox
        self.send_sem, self.recv_sem = send_sem, recv_sem
        self.me = lax.axis_index("col")
        self.orders = chip_orders(ways)
        self.phases = 1 + len(self.orders[0])

    def moves(self, step, phase):
        halves = [None] if phase == 0 else [0, 1]
        for k in halves:
            order = [1] if phase == 0 else [1, *self.orders[k]]
            bit = order[phase]
            done = sum(order[:phase])
            count = MB if k is None else MB // 2
            rows = pl.ds(pl.multiple_of(step * MB + (k or 0) * count, count), count)
            for o in range(self.ways):
                if o & done or not o & bit:
                    continue
                goal = o ^ bit
                slot = slot_of(self.ways, self.orders, phase, k, goal)
                sem = 2 * slot + (k or 0)
                copy = pltpu.make_async_remote_copy(
                    src_ref=self.parts.at[o, rows],
                    dst_ref=self.inbox.at[slot, rows],
                    send_sem=self.send_sem.at[step, sem],
                    recv_sem=self.recv_sem.at[step, sem],
                    device_id={"col": flip(self.me, bit)},
                    device_id_type=MESH,
                )
                yield copy, goal, slot, rows

    def send(self, step, phase):
        for copy, *_ in self.moves(step, phase):
            copy.start()

    def absorb(self, step, phase):
        out = []
        for copy, goal, slot, rows in self.moves(step, phase):
            copy.wait_recv()
            value = self.parts[goal, rows, :].astype(jnp.float32)
            value += self.inbox[slot, rows, :].astype(jnp.float32)
            if phase == self.phases - 1:
                out.append(value)
            else:
                self.parts[goal, rows, :] = value.astype(jnp.bfloat16)
        return out

    def finish(self, step):
        for phase in range(self.phases):
            for copy, *_ in self.moves(step, phase):
                copy.wait_send()

    def advance(self, t, steps, lags):
        pl.when(t < steps)(lambda: self.send(t, 0))
        for phase in range(self.phases - 1):
            s = t - lags[phase]

            @pl.when((s >= 0) & (s < steps))
            def _():
                self.absorb(s, phase)
                self.send(s, phase + 1)


def slot_of(ways, orders, phase, half, goal):
    if phase == 0:
        return goal // 2
    order = [1, *orders[half]]
    base = ways // 2
    for p in range(1, phase):
        base += ways >> (p + 1)
    goals = [g for g in range(ways) if not g & sum(order[: phase + 1])]
    return base + goals.index(goal)


def lags_of(ways):
    return [1 + 2 * p for p in range(len(chip_orders(ways)[0]) + 1)]


def reducer_scratch(ways, rows, width):
    steps = rows // MB
    return [
        pltpu.VMEM((ways, rows, width), jnp.bfloat16),
        pltpu.VMEM((ways - 1, rows, width), jnp.bfloat16),
        pltpu.SemaphoreType.DMA((steps, 2 * ways)),
        pltpu.SemaphoreType.DMA((steps, 2 * ways)),
    ]


def branch_kernel(
    ways,
    steps,
    att_ref,
    hidden_ref,
    grad_ref,
    token_ref,
    wout_ref,
    wd_ref,
    out_ref,
    wgrad_ref,
    parts,
    inbox,
    send_sem,
    recv_sem,
    acc,
):
    f32, bf16 = jnp.float32, jnp.bfloat16
    t = pl.program_id(0)
    me, width = lax.axis_index("col"), D // ways
    lags = lags_of(ways)
    ring = Reducer(ways, parts, inbox, send_sem, recv_sem)

    @pl.when(t == 0)
    def _():
        acc[...] = jnp.zeros_like(acc)
        meet([{"col": flip(me, 1 << k)} for k in range(ways.bit_length() - 1)])

    @pl.when(t < steps)
    def _():
        rows = pl.ds(pl.multiple_of(t * MB, MB), MB)
        att, hidden = att_ref[...], hidden_ref[...]
        for o in range(ways):
            cols = pl.ds(pl.multiple_of(flip(me, o) * width, width), width)
            total = lax.dot_general(att, wout_ref[cols, :], NT, preferred_element_type=f32)
            total += jnp.dot(hidden, wd_ref[:, cols], preferred_element_type=f32)
            parts[o, rows, :] = total.astype(bf16)

    ring.advance(t, steps, lags)

    @pl.when(t < steps)
    def _():
        acc[...] += contract(hidden_ref[...], grad_ref[...], 0, 0)

    @pl.when(t == steps)
    def _():
        wgrad_ref[...] = acc[...].astype(bf16)

    s = t - lags[-1]

    @pl.when(s >= 0)
    def _():
        for k, value in enumerate(ring.absorb(s, ring.phases - 1)):
            half = slice(k * (MB // 2), (k + 1) * (MB // 2))
            out_ref[half, :] = (token_ref[half, :].astype(f32) + value).astype(bf16)
        ring.finish(s)


def branches(att, hidden, grad, tokens, weights, wd, ways):
    rows, width = tokens.shape
    ffn = wd.shape[0]
    steps = rows // MB
    lag = lags_of(ways)[-1]
    now = lambda t: (jnp.minimum(t, steps - 1), 0)
    late = lambda t: (jnp.maximum(t - lag, 0), 0)
    fixed = lambda t: (0, 0)
    once = pl.Buffered(1)
    return pl.pallas_call(
        functools.partial(branch_kernel, ways, steps),
        out_shape=[
            jax.ShapeDtypeStruct((rows, width), jnp.bfloat16),
            jax.ShapeDtypeStruct((ffn, D), jnp.bfloat16),
        ],
        grid=(steps + lag,),
        in_specs=[
            pl.BlockSpec((MB, width), now),
            pl.BlockSpec((MB, ffn), now),
            pl.BlockSpec((MB, D), now),
            pl.BlockSpec((MB, width), late),
            pl.BlockSpec((D, width), lambda t: (0, 3), pipeline_mode=once),
            pl.BlockSpec((ffn, D), fixed, pipeline_mode=once),
        ],
        out_specs=[
            pl.BlockSpec((MB, width), late),
            pl.BlockSpec((ffn, D), fixed, pipeline_mode=once),
        ],
        scratch_shapes=[*reducer_scratch(ways, rows, width), pltpu.VMEM((ffn, D), jnp.float32)],
        compiler_params=pltpu.CompilerParams(
            collective_id=1,
            has_side_effects=True,
            dimension_semantics=("arbitrary",),
            vmem_limit_bytes=60 << 20,
        ),
        cost_estimate=pl.CostEstimate(
            flops=8 * rows * D * (2 * ffn + width), bytes_accessed=4 * rows * D, transcendentals=0
        ),
        name="branches",
    )(att, hidden, grad, tokens, weights, wd)


def back_kernel(
    ways,
    lines,
    steps,
    gp_ref,
    gg_ref,
    gu_ref,
    x_ref,
    token_ref,
    cot_ref,
    stat_ref,
    w_ref,
    wgu_ref,
    vectors_ref,
    gain_ref,
    out_ref,
    vgrad_ref,
    parts,
    inbox,
    send_sem,
    recv_sem,
    sums,
    ssend_sem,
    srecv_sem,
    acc,
    vsend_sem,
    vrecv_sem,
):
    f32, bf16 = jnp.float32, jnp.bfloat16
    t = pl.program_id(0)
    me, width = lax.axis_index("col"), D // ways
    line = lax.axis_index("row")
    lags = lags_of(ways)
    ring = Reducer(ways, parts, inbox, send_sem, recv_sem)

    @pl.when(t == 0)
    def _():
        acc[...] = jnp.zeros_like(acc)
        meet(
            [{"col": flip(me, k)} for k in range(1, ways)]
            + [{"row": (line + k) % lines} for k in range(1, lines)]
        )

    def sum_copies(step):
        rows = pl.ds(pl.multiple_of(step * MB, MB), MB)
        for k in range(1, ways):
            yield pltpu.make_async_remote_copy(
                src_ref=sums.at[0, :, rows],
                dst_ref=sums.at[k, :, rows],
                send_sem=ssend_sem.at[step, k - 1],
                recv_sem=srecv_sem.at[step, k - 1],
                device_id={"col": flip(me, k)},
                device_id_type=MESH,
            )

    @pl.when(t < steps)
    def _():
        rows = pl.ds(pl.multiple_of(t * MB, MB), MB)
        gp, gg, gu = gp_ref[...], gg_ref[...], gu_ref[...]
        plain = jnp.zeros((MB, 1), f32)
        cross = jnp.zeros((MB, 1), f32)
        for o in range(ways):
            cols = pl.ds(pl.multiple_of(flip(me, o) * width, width), width)
            total = jnp.dot(gg, wgu_ref[0, :, cols], preferred_element_type=f32)
            total += jnp.dot(gu, wgu_ref[1, :, cols], preferred_element_type=f32)
            total += lax.dot_general(gp, w_ref[cols, :], NT, preferred_element_type=f32)
            parts[o, rows, :] = total.astype(bf16)
            scaled = x_ref[:, cols].astype(f32) - vectors_ref[1:2, cols]
            plain += jnp.sum(total * vectors_ref[0:1, cols], axis=1, keepdims=True)
            cross += jnp.sum(total * scaled, axis=1, keepdims=True)
        lane = lax.broadcasted_iota(jnp.int32, (MB, 128), 1)
        pair = jnp.where(lane == 0, plain, jnp.where(lane == 1, cross, 0.0))
        sums[0, :, rows] = pair.T[:8]
        for copy in sum_copies(t):
            copy.start()

    ring.advance(t, steps, lags)
    s = t - lags[-1]

    @pl.when(s >= 0)
    def _():
        rows = pl.ds(pl.multiple_of(s * MB, MB), MB)
        for copy in sum_copies(s):
            copy.wait_recv()
        both = sum(sums[k, :, rows] for k in range(ways)).T
        for k, value in enumerate(ring.absorb(s, ring.phases - 1)):
            half = slice(k * (MB // 2), (k + 1) * (MB // 2))
            inv = stat_ref[half, 1:]
            unit = (token_ref[half, :].astype(f32) - stat_ref[half, :1]) * inv
            scaled = value * gain_ref[0:1, :]
            out_ref[half, :] = cot_ref[half, :].astype(f32) + inv * (
                scaled - both[half, 0:1] / D - unit * (both[half, 1:2] / D)
            )
            acc[0, 0:1, :] += jnp.sum(value * unit, axis=0, keepdims=True)
            acc[0, 1:2, :] += jnp.sum(value, axis=0, keepdims=True)
        for copy in sum_copies(s):
            copy.wait_send()
        ring.finish(s)

    @pl.when(t == pl.num_programs(0) - 1)
    def _():
        copies = [
            pltpu.make_async_remote_copy(
                src_ref=acc.at[0],
                dst_ref=acc.at[k],
                send_sem=vsend_sem.at[k - 1],
                recv_sem=vrecv_sem.at[k - 1],
                device_id={"row": (line + k) % lines},
                device_id_type=MESH,
            )
            for k in range(1, lines)
        ]
        for copy in copies:
            copy.start()
        for copy in copies:
            copy.wait()
        vgrad_ref[...] = sum(acc[k] for k in range(lines))


def norm_back(gp, gg, gu, normed, tokens, cot, stats, weights, wgu, vectors, own, ways, lines):
    rows, width = tokens.shape
    ffn = gg.shape[1]
    steps = rows // MB
    lag = lags_of(ways)[-1]
    now = lambda t: (jnp.minimum(t, steps - 1), 0)
    late = lambda t: (jnp.maximum(t - lag, 0), 0)
    fixed = lambda t: (0, 0)
    once = pl.Buffered(1)
    dma = pltpu.SemaphoreType.DMA
    return pl.pallas_call(
        functools.partial(back_kernel, ways, lines, steps),
        out_shape=[
            jax.ShapeDtypeStruct((rows, width), jnp.float32),
            jax.ShapeDtypeStruct((8, width), jnp.float32),
        ],
        grid=(steps + lag,),
        in_specs=[
            pl.BlockSpec((MB, 3 * width), now),
            pl.BlockSpec((MB, ffn), now),
            pl.BlockSpec((MB, ffn), now),
            pl.BlockSpec((MB, D), now),
            pl.BlockSpec((MB, width), late),
            pl.BlockSpec((MB, width), late),
            pl.BlockSpec((MB, 2), late),
            pl.BlockSpec((D, 3 * width), fixed, pipeline_mode=once),
            pl.BlockSpec((2, ffn, D), lambda t: (0, 0, 0), pipeline_mode=once),
            pl.BlockSpec((8, D), fixed),
            pl.BlockSpec((8, width), fixed),
        ],
        out_specs=[pl.BlockSpec((MB, width), late), pl.BlockSpec((8, width), fixed)],
        scratch_shapes=[
            *reducer_scratch(ways, rows, width),
            pltpu.VMEM((ways, 8, rows), jnp.float32),
            dma((steps, ways - 1)),
            dma((steps, ways - 1)),
            pltpu.VMEM((lines, 8, width), jnp.float32),
            dma((lines - 1,)),
            dma((lines - 1,)),
        ],
        compiler_params=pltpu.CompilerParams(
            collective_id=2,
            has_side_effects=True,
            dimension_semantics=("arbitrary",),
            vmem_limit_bytes=61 << 20,
        ),
        cost_estimate=pl.CostEstimate(
            flops=4 * rows * D * (2 * ffn + 3 * width), bytes_accessed=6 * rows * D, transcendentals=0
        ),
        name="norm_back",
    )(gp, gg, gu, normed, tokens, cot, stats, weights, wgu, vectors, own)


def after(value, *others):
    return lax.optimization_barrier((value, others))[0]


def local(
    tokens,
    norm_gain,
    norm_bias,
    qkv_weight,
    gate_up_weight,
    out_weight,
    down_weight,
    image_start,
    doc_ids,
    out_grad,
):
    f32, bf16 = jnp.float32, jnp.bfloat16
    block_rows, width = tokens.shape
    ways = D // width
    lines = D // qkv_weight.shape[0]

    own = jnp.concatenate([qkv_weight[:, k] for k in range(3)] + [out_weight], axis=1)
    weights = lax.all_gather(own, "row", axis=0, tiled=True)
    full_gate_up = lax.all_gather(gate_up_weight, "row", axis=0, tiled=True)
    full_down = lax.all_gather(down_weight, "row", axis=0, tiled=True)
    wgu = jnp.transpose(full_gate_up, (1, 2, 0))
    wd = jnp.transpose(full_down, (1, 0))
    own_vectors = jnp.pad(jnp.stack([norm_gain, norm_bias]), ((0, 6), (0, 0)))

    normed, grad, stats, vectors = gather(tokens, out_grad, own_vectors, ways)
    attended, grad_projected = attention(normed, grad, weights, doc_ids, image_start)

    def weight_sum(grad):
        return lax.psum_scatter(grad, "row", scatter_dimension=0, tiled=True)

    def weight_grad(left, right):
        return contract(left, right, 0, 0).astype(bf16)

    grad_qkv = weight_grad(normed, grad_projected)
    grad_out = weight_grad(grad, attended)
    hidden, grad_gate, grad_up = feed_forward(after(normed, grad_qkv, grad_out), grad, wgu, wd)
    weight_gate = weight_grad(normed, grad_gate)
    weight_up = weight_grad(normed, after(grad_up, weight_gate))
    outputs, weight_down = branches(
        after(attended, weight_up), hidden, grad, tokens, weights, wd, ways
    )
    input_grad, vector_grads = norm_back(
        after(grad_projected, outputs),
        grad_gate,
        grad_up,
        normed,
        tokens,
        out_grad,
        stats,
        weights,
        wgu,
        vectors,
        own_vectors,
        ways,
        lines,
    )
    qkv_sum = weight_sum(grad_qkv.reshape(D, 3, width)).astype(f32)
    out_sum = weight_sum(grad_out).astype(f32)
    gate_sum = weight_sum(weight_gate)
    up_sum = weight_sum(weight_up)
    down_sum = weight_sum(jnp.transpose(weight_down, (1, 0))).astype(f32)
    gate_up_sum = jnp.stack([gate_sum.astype(f32), up_sum.astype(f32)], axis=1)
    return (
        outputs,
        input_grad,
        vector_grads[0],
        vector_grads[1],
        qkv_sum,
        gate_up_sum,
        out_sum,
        down_sum,
    )


def solution(mesh):
    placed = (
        P("row", "col"),
        P("col"),
        P("col"),
        P("row", None, "col"),
        P("row", None, "col"),
        P("row", "col"),
        P("row", "col"),
        P("row"),
        P("row", None),
        P("row", "col"),
    )
    return jax.shard_map(
        local,
        mesh=mesh,
        in_specs=placed,
        out_specs=(
            P("row", "col"),
            P("row", "col"),
            P("col"),
            P("col"),
            P("row", None, "col"),
            P("row", None, "col"),
            P("row", "col"),
            P("row", "col"),
        ),
        check_vma=False,
    )
```

```python
import functools

import jax
import jax.numpy as jnp
import numpy as np
from jax import lax
from jax.experimental import pallas as pl
from jax.experimental.pallas import tpu as pltpu
from jax.sharding import PartitionSpec as P

D = 2048
HD = 64
ROT = 16
LEN = 1024
IMG = 256
QB = 256
MB = 512
RB = 256
GB = 512
SUMS = 4


NORM_EPS = 1e-05
MESH = pl.DeviceIdType.MESH
MASKED_SCORE = -1e30
ROPE_BASE = 10000.0
NT = (((1,), (1,)), ((), ()))


def contract(left, right, left_dim, right_dim):
    return lax.dot_general(
        left, right, (((left_dim,), (right_dim,)), ((), ())), preferred_element_type=jnp.float32
    )


def rope_rows():
    half = ROT // 2
    inv_freq = np.float32(ROPE_BASE) ** (np.float32(-2.0 / ROT) * np.arange(half, dtype=np.float32))
    angles = np.arange(LEN, dtype=np.float32)[None, :] * inv_freq[:, None]
    wide = angles.astype(np.float64)
    return np.concatenate([np.cos(wide), np.sin(wide)]).astype(np.float32)


def fill_tables(rows_ref, tables):
    half = ROT // 2
    for i in range(LEN // QB):
        sl = pl.ds(i * QB, QB)
        cosines, sines = rows_ref[:half, sl], rows_ref[half:, sl]
        zero = jnp.zeros_like(sines)
        rest = [zero] * (HD // half - 2)
        ones = [jnp.ones_like(sines)] * (HD // half - 2)
        tables[0, sl, :] = jnp.concatenate([cosines, cosines, *ones] * (128 // HD), axis=0).T
        tables[1, sl, :] = jnp.concatenate([-sines, zero, *rest] * (128 // HD), axis=0).T
        tables[2, sl, :] = jnp.concatenate([zero, sines, *rest] * (128 // HD), axis=0).T


def turn(x, tables, sl, sign):
    width = x.shape[1]
    c, a, b = (jnp.concatenate([tables[k, sl, :]] * (width // 128), axis=1) for k in range(3))
    left = pltpu.roll(x, width - ROT // 2, 1)
    right = pltpu.roll(x, ROT // 2, 1)
    return x * c + (left * a + right * b) * sign


class Attention:
    def __init__(self, heads, scratch):
        self.heads, self.width = heads, heads * HD
        (
            self.tables,
            self.span,
            self.data,
            self.kt,
            self.vt,
            self.s,
            self.d,
            self.e,
            self.bias,
            self.m,
            self.l,
            self.x,
            self.ot,
            self.dqt,
            self.dk,
            self.dv,
        ) = scratch

    @staticmethod
    def scratch(heads):
        f32, bf16, blocks, width = jnp.float32, jnp.bfloat16, LEN // QB, heads * HD
        return [
            pltpu.VMEM((3, LEN, 128), f32),
            pltpu.VMEM((blocks, 8, QB), jnp.int32),
            pltpu.VMEM((LEN, 4 * width), bf16),
            pltpu.VMEM((blocks, width, QB), bf16),
            pltpu.VMEM((blocks, width, QB), bf16),
            pltpu.VMEM((blocks, heads, QB, QB), f32),
            pltpu.VMEM((blocks, heads, QB, QB), f32),
            pltpu.VMEM((blocks, heads, QB, QB), bf16),
            pltpu.VMEM((QB, QB), f32),
            pltpu.VMEM((heads, 8, QB), f32),
            pltpu.VMEM((heads, 8, QB), f32),
            pltpu.VMEM((heads, 8, QB), f32),
            pltpu.VMEM((width, QB), f32),
            pltpu.VMEM((width, QB), f32),
            pltpu.VMEM((LEN, width), f32),
            pltpu.VMEM((LEN, width), f32),
        ]

    def part(self, kind):
        return pl.ds(kind * self.width, self.width)

    def begin(self, doc_ref, seq, start, x_ref, g_ref, w_ref):
        f32, bf16, width = jnp.float32, jnp.bfloat16, self.width
        docs = doc_ref[pl.ds(seq, 1), :].astype(f32)
        down = jnp.broadcast_to(docs, (128, LEN)).T[:, :1]
        for i in range(LEN // QB):
            own = docs[:, i * QB : (i + 1) * QB]
            first = jnp.sum((down < own).astype(jnp.int32), axis=0, keepdims=True)
            last = jnp.sum((down <= own).astype(jnp.int32), axis=0, keepdims=True) - 1
            at = lax.broadcasted_iota(jnp.int32, (1, QB), 1) + i * QB
            inside = (at >= start) & (at < start + IMG)
            self.span[i, 0:1, :] = first
            self.span[i, 1:2, :] = jnp.where(inside, jnp.minimum(last, start + IMG - 1), at)

        def block(i, _):
            sl = pl.ds(pl.multiple_of(i * QB, QB), QB)
            x = x_ref[sl, :]
            q = jnp.dot(x, w_ref[:, :width], preferred_element_type=f32)
            k = jnp.dot(x, w_ref[:, width : 2 * width], preferred_element_type=f32)
            v = jnp.dot(x, w_ref[:, 2 * width : 3 * width], preferred_element_type=f32)
            g = jnp.dot(g_ref[sl, :], w_ref[:, 3 * width :], preferred_element_type=f32)
            q = turn(q, self.tables, sl, 1.0).astype(bf16).astype(f32) * HD**-0.5
            k = turn(k, self.tables, sl, 1.0).astype(bf16)
            self.data[sl, self.part(0)] = q.astype(bf16)
            self.data[sl, self.part(1)] = k
            self.data[sl, self.part(2)] = v.astype(bf16)
            self.data[sl, self.part(3)] = g.astype(bf16)
            self.kt[i] = k.astype(f32).T.astype(bf16)
            self.vt[i] = v.T.astype(bf16)
            return 0

        lax.fori_loop(0, LEN // QB, block, 0)
        self.dk[...] = jnp.zeros_like(self.dk)
        self.dv[...] = jnp.zeros_like(self.dv)

    def bounds(self, i):
        return jnp.min(self.span[i, 0:1, :]) // QB, jnp.max(self.span[i, 1:2, :]) // QB

    def query_block(self, i, low, high, att_ref, gp_ref):
        f32, bf16, heads, width = jnp.float32, jnp.bfloat16, self.heads, self.width
        rows = pl.ds(pl.multiple_of(i * QB, QB), QB)
        lane = lax.broadcasted_iota(jnp.int32, (1, width), 1) // HD
        first, final = self.span[i, 0:1, :], self.span[i, 1:2, :]
        q, g = self.data[rows, self.part(0)], self.data[rows, self.part(3)]
        zero = jnp.zeros_like(q)
        q_own = [jnp.where(lane == h, q, zero) for h in range(heads)]
        g_own = [jnp.where(lane == h, g, zero) for h in range(heads)]
        self.m[...] = jnp.full_like(self.m, MASKED_SCORE)

        def fold(x, op):
            out = x[:8]
            for r in range(8, QB, 8):
                out = op(out, x[r : r + 8])
            return out

        def score(kb, _):
            keys = pl.ds(pl.multiple_of(kb * QB, QB), QB)
            k, v = self.data[keys, self.part(1)], self.data[keys, self.part(2)]
            at = lax.broadcasted_iota(jnp.int32, (QB, QB), 0) + kb * QB
            self.bias[...] = jnp.where((at >= first) & (at <= final), 0.0, MASKED_SCORE)
            for h in range(heads):
                s = lax.dot_general(k, q_own[h], NT, preferred_element_type=f32) + self.bias[...]
                self.s[kb, h] = s
                self.m[h] = jnp.maximum(self.m[h], fold(s, jnp.maximum))
                self.d[kb, h] = lax.dot_general(v, g_own[h], NT, preferred_element_type=f32)
            return 0

        lax.fori_loop(low, high + 1, score, 0)
        for h in range(heads):
            self.m[h] = jnp.broadcast_to(jnp.max(self.m[h], axis=0, keepdims=True), (8, QB))
        self.l[...] = jnp.zeros_like(self.l)
        self.x[...] = jnp.zeros_like(self.x)
        self.ot[...] = jnp.zeros_like(self.ot)
        self.dqt[...] = jnp.zeros_like(self.dqt)

        def expo(kb, _):
            for h in range(heads):
                hs = slice(h * HD, (h + 1) * HD)
                e = jnp.exp(self.s[kb, h] - self.m[h, 0:1, :])
                self.l[h] += fold(e, jnp.add)
                self.x[h] += fold(e * self.d[kb, h], jnp.add)
                e = e.astype(bf16)
                self.e[kb, h] = e
                self.ot[hs, :] += jnp.dot(self.vt[kb, hs, :], e, preferred_element_type=f32)
            return 0

        lax.fori_loop(low, high + 1, expo, 0)
        for h in range(heads):
            inv = 1.0 / jnp.sum(self.l[h], axis=0, keepdims=True)
            self.l[h] = jnp.broadcast_to(inv, (8, QB))
            delta = jnp.sum(self.x[h], axis=0, keepdims=True) * inv
            self.x[h] = jnp.broadcast_to(delta, (8, QB))

        def back(kb, _):
            keys = pl.ds(pl.multiple_of(kb * QB, QB), QB)
            dk = self.dk[keys, :]
            dv = self.dv[keys, :]
            for h in range(heads):
                hs = slice(h * HD, (h + 1) * HD)
                p = self.e[kb, h].astype(f32) * self.l[h, 0:1, :]
                ds = (p * (self.d[kb, h] - self.x[h, 0:1, :])).astype(bf16)
                dv += jnp.dot(p.astype(bf16), g_own[h], preferred_element_type=f32)
                dk += jnp.dot(ds, q_own[h], preferred_element_type=f32)
                self.dqt[hs, :] += jnp.dot(self.kt[kb, hs, :], ds, preferred_element_type=f32)
            self.dk[keys, :] = dk
            self.dv[keys, :] = dv
            return 0

        lax.fori_loop(low, high + 1, back, 0)
        for h in range(heads):
            hs = slice(h * HD, (h + 1) * HD)
            self.ot[hs, :] = self.ot[hs, :] * self.l[h, 0:1, :]
        att_ref[rows, :] = self.ot[...].T.astype(bf16)
        dq = self.dqt[...].T * HD**-0.5
        gp_ref[rows, :width] = turn(dq, self.tables, rows, -1.0).astype(bf16)

    def finish(self, gp_ref):
        width = self.width

        def block(i, _):
            sl = pl.ds(pl.multiple_of(i * QB, QB), QB)
            dk = turn(self.dk[sl, :], self.tables, sl, -1.0)
            gp_ref[sl, width : 2 * width] = dk.astype(jnp.bfloat16)
            gp_ref[sl, 2 * width :] = self.dv[sl, :].astype(jnp.bfloat16)
            return 0

        lax.fori_loop(0, LEN // QB, block, 0)


def attention_kernel(
    heads, first, start_ref, x_ref, g_ref, w_ref, doc_ref, rope_ref, *refs
):
    att_ref, gp_ref = refs[2:4]
    seq = pl.program_id(0) + first
    attend = Attention(heads, refs[4:])

    @pl.when(pl.program_id(0) == 0)
    def _():
        fill_tables(rope_ref, attend.tables)

    attend.begin(doc_ref, seq, start_ref[seq], x_ref, g_ref, w_ref)

    def query_block(i, _):
        attend.query_block(i, *attend.bounds(i), att_ref, gp_ref)
        return 0

    lax.fori_loop(0, LEN // QB, query_block, 0)
    attend.finish(gp_ref)


def attention(first, normed, grad, weights, image_start, doc_ids, earlier):
    rows, width = normed.shape[0], weights.shape[1] // 4
    count, heads = rows // LEN, width // HD
    bf16 = jnp.bfloat16
    seq_rows = lambda s, *_: (s + first, 0)
    fixed = lambda s, *_: (0, 0)
    return pl.pallas_call(
        functools.partial(attention_kernel, heads, first),
        out_shape=[jax.ShapeDtypeStruct(e.shape, bf16) for e in earlier],
        grid_spec=pltpu.PrefetchScalarGridSpec(
            num_scalar_prefetch=1,
            grid=(count - first,),
            in_specs=[
                pl.BlockSpec((LEN, D), seq_rows),
                pl.BlockSpec((LEN, D), seq_rows),
                pl.BlockSpec((D, 4 * width), fixed, pipeline_mode=pl.Buffered(1)),
                pl.BlockSpec((count, LEN), fixed),
                pl.BlockSpec((ROT, LEN), fixed),
                pl.BlockSpec(memory_space=pl.ANY),
                pl.BlockSpec(memory_space=pl.ANY),
            ],
            out_specs=[
                pl.BlockSpec((LEN, width), seq_rows),
                pl.BlockSpec((LEN, 3 * width), seq_rows),
            ],
            scratch_shapes=Attention.scratch(heads),
        ),
        input_output_aliases={6: 0, 7: 1},
        compiler_params=pltpu.CompilerParams(
            dimension_semantics=("arbitrary",), vmem_limit_bytes=56 << 20
        ),
        cost_estimate=pl.CostEstimate(
            flops=(count - first) * LEN * (36 * 640 * width + 8 * D * width),
            bytes_accessed=(count - first) * LEN * (width * 8 + 4 * D) + 8 * D * width,
            transcendentals=(count - first) * LEN * 640 * heads,
        ),
        name="attention",
    )(image_start, normed, grad, weights, doc_ids, jnp.asarray(rope_rows()), *earlier)


def ffn_kernel(x_ref, g_ref, wgu_ref, wd_ref, hidden_ref, gg_ref, gu_ref):
    f32, bf16 = jnp.float32, jnp.bfloat16
    x = x_ref[...]
    gate = lax.dot_general(x, wgu_ref[0], NT, preferred_element_type=f32)
    up = lax.dot_general(x, wgu_ref[1], NT, preferred_element_type=f32)
    grad = lax.dot_general(g_ref[...], wd_ref[...], NT, preferred_element_type=f32)
    sigma = jax.nn.sigmoid(gate)
    silu = gate * sigma
    hidden_ref[...] = (silu * up).astype(bf16)
    gg_ref[...] = (grad * up * (sigma + silu * (1.0 - sigma))).astype(bf16)
    gu_ref[...] = (grad * silu).astype(bf16)


def feed_forward(normed, grad, wgu, wd):
    rows, ffn = normed.shape[0], wd.shape[0]
    block = lambda i: (i, 0)
    return pl.pallas_call(
        ffn_kernel,
        out_shape=[jax.ShapeDtypeStruct((rows, ffn), jnp.bfloat16)] * 3,
        grid=(rows // MB,),
        in_specs=[
            pl.BlockSpec((MB, D), block),
            pl.BlockSpec((MB, D), block),
            pl.BlockSpec((2, ffn, D), lambda i: (0, 0, 0), pipeline_mode=pl.Buffered(1)),
            pl.BlockSpec((ffn, D), lambda i: (0, 0), pipeline_mode=pl.Buffered(1)),
        ],
        out_specs=[pl.BlockSpec((MB, ffn), block)] * 3,
        compiler_params=pltpu.CompilerParams(
            dimension_semantics=("arbitrary",), vmem_limit_bytes=56 << 20
        ),
        cost_estimate=pl.CostEstimate(
            flops=6 * rows * D * ffn,
            bytes_accessed=rows * (4 * D + 6 * ffn) + 6 * D * ffn,
            transcendentals=rows * ffn,
        ),
        name="feed_forward",
    )(normed, grad, wgu, wd)


def flip(index, bits):
    bit = 1
    while bit <= bits:
        if bits & bit:
            index = index + bit - 2 * bit * ((index // bit) % 2)
        bit *= 2
    return index


def chip_orders(ways):
    bits = [1 << k for k in range(1, ways.bit_length() - 1)]
    return bits, bits[::-1]


def held(bits):
    found = [0]
    for bit in bits:
        found += [o ^ bit for o in found]
    return found


def meet(peers):
    barrier = pltpu.get_barrier_semaphore()
    for peer in peers:
        pl.semaphore_signal(barrier, inc=1, device_id=peer, device_id_type=MESH)
    pl.semaphore_wait(barrier, len(peers))


def gather_kernel(ways, base, attended, *refs):
    f32, bf16 = jnp.float32, jnp.bfloat16
    me = lax.axis_index("col")
    if attended:
        (token_ref, cot_ref, vectors_ref, w_ref, rope_ref, doc_ref, image_ref, old_ref) = refs[:8]
        (old_normed, old_grad, normed_ref, full_ref, stat_ref, att_ref, gp_ref) = refs[8:15]
        refs = refs[15:]
    else:
        (token_ref, cot_ref, vector_ref, normed_ref, full_ref, stat_ref, vectors_ref) = refs[:7]
        refs = refs[7:]
    (both, load_sem, store_sem, full_sem, send_sem, recv_sem) = refs[:6]
    refs = refs[6:]
    width = token_ref.shape[1]
    rows = both.shape[1]
    pairs = rows // GB
    orders = chip_orders(ways)
    phases = len(orders[0])
    mine = pl.ds(pl.multiple_of(me * width, width), width)
    source = pl.ds(base, rows)
    loads = [
        pltpu.make_async_copy(token_ref.at[source], both.at[me, :, pl.ds(0, width)], load_sem.at[0]),
        pltpu.make_async_copy(cot_ref.at[source], both.at[me, :, pl.ds(width, width)], load_sem.at[1]),
    ]
    for load in loads:
        load.start()
    peers = [flip(me, k) for k in range(1, ways)]
    if attended:
        meet([{"col": flip(me, 1 << k)} for k in range(ways.bit_length() - 1)])
    else:
        vectors_ref[:, mine] = vector_ref[...]
        meet([{"col": peer} for peer in peers])

    def vector_copy(k):
        return pltpu.make_async_remote_copy(
            src_ref=vectors_ref.at[:, mine],
            dst_ref=vectors_ref.at[:, mine],
            send_sem=refs[0].at[k],
            recv_sem=refs[1].at[k],
            device_id={"col": peers[k]},
            device_id_type=MESH,
        )

    def copies(p, phase):
        for k, order in enumerate(orders):
            bit = order[phase] if phase < phases else 1
            place = pl.ds(pl.multiple_of(p * GB + k * (GB // 2), GB // 2), GB // 2)
            for o in held(order[:phase]):
                index = k * ways + (o ^ bit)
                owner = flip(me, o)
                yield pltpu.make_async_remote_copy(
                    src_ref=both.at[owner, place],
                    dst_ref=both.at[owner, place],
                    send_sem=send_sem.at[p, index],
                    recv_sem=recv_sem.at[p, index],
                    device_id={"col": flip(me, bit)},
                    device_id_type=MESH,
                )

    def start(p, phase):
        for copy in copies(p, phase):
            copy.start()

    def arrive(p, phase):
        for copy in copies(p, phase):
            copy.wait_recv()

    def filed(p, first, out_ref, sem):
        place = pl.ds(pl.multiple_of(p * GB, GB), GB)
        goal = pl.ds(pl.multiple_of(base + p * GB, GB), GB)
        for b in range(ways):
            pltpu.make_async_copy(
                both.at[b, place, pl.ds(first, width)],
                out_ref.at[goal, pl.ds(b * width, width)],
                sem.at[p],
            ).start()

    def filed_wait(p, out_ref, sem):
        place = out_ref.at[pl.ds(base + p * GB, GB)]
        pltpu.make_async_copy(place, place, sem.at[p]).wait()

    def norm(p):
        filed(p, width, full_ref, full_sem)
        for phase in range(phases + 1):
            for copy in copies(p, phase):
                copy.wait_send()

        def block(j, _):
            at = pl.ds(pl.multiple_of(p * GB + j * QB, QB), QB)
            goal = pl.ds(pl.multiple_of(base + p * GB + j * QB, QB), QB)
            sums = sum(both[b, at, :width].astype(f32) for b in range(ways))
            mean = jnp.sum(sums, axis=1, keepdims=True) / D
            squares = jnp.zeros((QB, width), f32)
            for b in range(ways):
                x = both[b, at, :width].astype(f32) - mean
                squares += x * x
            inv = lax.rsqrt(jnp.sum(squares, axis=1, keepdims=True) / D + NORM_EPS)
            stat_ref[goal, :1] = mean
            stat_ref[goal, 1:] = inv
            for b in range(ways):
                cols = slice(b * width, (b + 1) * width)
                x = (both[b, at, :width].astype(f32) - mean) * inv
                x = x * vectors_ref[0:1, cols] + vectors_ref[1:2, cols]
                both[b, at, :width] = x.astype(bf16)
            return 0

        lax.fori_loop(0, GB // QB, block, 0)
        filed(p, 0, normed_ref, store_sem)

    if attended:
        x_scr, g_scr, att_scr, gp_scr, in_sem, out_sem = refs[:6]
        attend = Attention(width // HD, refs[6:])
        stat_ref[pl.ds(0, base), :] = old_ref[pl.ds(0, base), :]

        def fetch(seq):
            place = pl.ds(pl.multiple_of(seq * LEN, LEN), LEN)
            return [
                pltpu.make_async_copy(old_normed.at[place], x_scr, in_sem.at[seq, 0]),
                pltpu.make_async_copy(old_grad.at[place], g_scr, in_sem.at[seq, 1]),
            ]

        def give(seq):
            place = pl.ds(pl.multiple_of(seq * LEN, LEN), LEN)
            return [
                pltpu.make_async_copy(att_scr.at[seq], att_ref.at[place], out_sem.at[seq, 0]),
                pltpu.make_async_copy(gp_scr.at[seq], gp_ref.at[place], out_sem.at[seq, 1]),
            ]

        for move in fetch(0):
            move.start()

    for load in loads:
        load.wait()
    start(0, 0)
    start(1, 0)
    if attended:
        fill_tables(rope_ref, attend.tables)
    else:
        for k in range(ways - 1):
            vector_copy(k).start()
        for k in range(ways - 1):
            vector_copy(k).wait_recv()
    blocks = LEN // QB
    turns = attended * blocks // pairs if attended else 0

    def step(p, _):
        for phase in range(phases):
            arrive(p, phase)
            start(p, phase + 1)
            if phase == 0:
                pl.when(p + 2 < pairs)(lambda: start(p + 2, 0))

                @pl.when(p >= 1)
                def _():
                    arrive(p - 1, phases)
                    norm(p - 1)

                if attended:
                    seq = p * turns // blocks
                    spot = p * turns % blocks

                    @pl.when(spot == 0)
                    def _():
                        for move in fetch(seq):
                            move.wait()
                        attend.begin(doc_ref, seq, image_ref[seq], x_scr, g_scr, w_ref)

                        @pl.when(seq + 1 < attended)
                        def _():
                            for move in fetch(seq + 1):
                                move.start()

                    def query_block(i, _):
                        low = i // (blocks - 1)
                        attend.query_block(i, low, i + 1 - low, att_scr.at[seq], gp_scr.at[seq])
                        return 0

                    lax.fori_loop(spot, spot + turns, query_block, 0)

                    @pl.when(spot + turns == blocks)
                    def _():
                        attend.finish(gp_scr.at[seq])
                        for move in give(seq):
                            move.start()
        return 0

    lax.fori_loop(0, pairs, step, 0)
    arrive(pairs - 1, phases)
    norm(pairs - 1)
    for p in range(pairs):
        filed_wait(p, full_ref, full_sem)
        filed_wait(p, normed_ref, store_sem)
    if attended:
        for seq in range(attended):
            for move in give(seq):
                move.wait()
    else:
        for k in range(ways - 1):
            vector_copy(k).wait_send()


def gather_scratch(ways, rows, width):
    dma = pltpu.SemaphoreType.DMA
    pairs = rows // GB
    return [
        pltpu.VMEM((ways, rows, 2 * width), jnp.bfloat16),
        dma((2,)),
        dma((pairs,)),
        dma((pairs,)),
        dma((pairs, 2 * ways)),
        dma((pairs, 2 * ways)),
    ]


def gather_first(tokens, out_grad, vectors, count, ways):
    rows, width = tokens.shape
    bf16, f32 = jnp.bfloat16, jnp.float32
    anywhere = pl.BlockSpec(memory_space=pl.ANY)
    vmem = pl.BlockSpec(memory_space=pltpu.VMEM)
    dma = pltpu.SemaphoreType.DMA
    return pl.pallas_call(
        functools.partial(gather_kernel, ways, 0, 0),
        out_shape=[
            jax.ShapeDtypeStruct((rows, D), bf16),
            jax.ShapeDtypeStruct((rows, D), bf16),
            jax.ShapeDtypeStruct((rows, 2), f32),
            jax.ShapeDtypeStruct((8, D), f32),
        ],
        in_specs=[anywhere, anywhere, vmem],
        out_specs=[anywhere, anywhere, vmem, vmem],
        scratch_shapes=[*gather_scratch(ways, count, width), dma((ways - 1,)), dma((ways - 1,))],
        compiler_params=pltpu.CompilerParams(
            collective_id=0, has_side_effects=True, vmem_limit_bytes=40 << 20
        ),
        cost_estimate=pl.CostEstimate(
            flops=100 * count * D * D // ways, bytes_accessed=count * D * 8, transcendentals=0
        ),
        name="gather_first",
    )(tokens, out_grad, vectors)


def gather_rest(tokens, out_grad, vectors, weights, doc_ids, image_start, stats, normed, grad, ways):
    rows, width = tokens.shape
    count = rows // 2
    bf16, f32 = jnp.bfloat16, jnp.float32
    anywhere = pl.BlockSpec(memory_space=pl.ANY)
    vmem = pl.BlockSpec(memory_space=pltpu.VMEM)
    dma = pltpu.SemaphoreType.DMA
    seqs = count // LEN
    return pl.pallas_call(
        functools.partial(gather_kernel, ways, count, seqs),
        out_shape=[
            jax.ShapeDtypeStruct((rows, D), bf16),
            jax.ShapeDtypeStruct((rows, D), bf16),
            jax.ShapeDtypeStruct((rows, 2), f32),
            jax.ShapeDtypeStruct((rows, width), bf16),
            jax.ShapeDtypeStruct((rows, 3 * width), bf16),
        ],
        in_specs=[
            anywhere,
            anywhere,
            vmem,
            vmem,
            vmem,
            vmem,
            pl.BlockSpec(memory_space=pltpu.SMEM),
            vmem,
            anywhere,
            anywhere,
        ],
        out_specs=[anywhere, anywhere, vmem, anywhere, anywhere],
        input_output_aliases={8: 0, 9: 1},
        scratch_shapes=[
            *gather_scratch(ways, rows - count, width),
            pltpu.VMEM((LEN, D), bf16),
            pltpu.VMEM((LEN, D), bf16),
            pltpu.VMEM((seqs, LEN, width), bf16),
            pltpu.VMEM((seqs, LEN, 3 * width), bf16),
            dma((seqs, 2)),
            dma((seqs, 2)),
            *Attention.scratch(width // HD),
        ],
        compiler_params=pltpu.CompilerParams(
            collective_id=3, has_side_effects=True, vmem_limit_bytes=60 << 20
        ),
        cost_estimate=pl.CostEstimate(
            flops=100 * count * D * D // ways, bytes_accessed=count * D * 8, transcendentals=0
        ),
        name="gather_rest",
    )(tokens, out_grad, vectors, weights, jnp.asarray(rope_rows()), doc_ids, image_start, stats, normed, grad)


class Reducer:
    def __init__(self, ways, parts, inbox, send_sem, recv_sem):
        self.ways, self.parts, self.inbox = ways, parts, inbox
        self.send_sem, self.recv_sem = send_sem, recv_sem
        self.me = lax.axis_index("col")
        self.orders = chip_orders(ways)
        self.phases = 1 + len(self.orders[0])

    def moves(self, step, phase):
        halves = [None] if phase == 0 else [0, 1]
        for k in halves:
            order = [1] if phase == 0 else [1, *self.orders[k]]
            bit = order[phase]
            done = sum(order[:phase])
            count = RB if k is None else RB // 2
            rows = pl.ds(pl.multiple_of(step * RB + (k or 0) * count, count), count)
            for o in range(self.ways):
                if o & done or not o & bit:
                    continue
                goal = o ^ bit
                slot = slot_of(self.ways, self.orders, phase, k, goal)
                sem = 2 * slot + (k or 0)
                copy = pltpu.make_async_remote_copy(
                    src_ref=self.parts.at[o, rows],
                    dst_ref=self.inbox.at[slot, rows],
                    send_sem=self.send_sem.at[step, sem],
                    recv_sem=self.recv_sem.at[step, sem],
                    device_id={"col": flip(self.me, bit)},
                    device_id_type=MESH,
                )
                yield copy, goal, slot, rows

    def send(self, step, phase):
        for copy, *_ in self.moves(step, phase):
            copy.start()

    def absorb(self, step, phase):
        out = []
        for copy, goal, slot, rows in self.moves(step, phase):
            copy.wait_recv()
            value = self.parts[goal, rows, :].astype(jnp.float32)
            value += self.inbox[slot, rows, :].astype(jnp.float32)
            if phase == self.phases - 1:
                out.append(value)
            else:
                self.parts[goal, rows, :] = value.astype(jnp.bfloat16)
        return out

    def finish(self, step):
        for phase in range(self.phases):
            for copy, *_ in self.moves(step, phase):
                copy.wait_send()

    def advance(self, t, steps, lags):
        pl.when(t < steps)(lambda: self.send(t, 0))
        for phase in range(self.phases - 1):
            s = t - lags[phase]

            @pl.when((s >= 0) & (s < steps))
            def _():
                self.absorb(s, phase)
                self.send(s, phase + 1)


def slot_of(ways, orders, phase, half, goal):
    if phase == 0:
        return goal // 2
    order = [1, *orders[half]]
    base = ways // 2
    for p in range(1, phase):
        base += ways >> (p + 1)
    goals = [g for g in range(ways) if not g & sum(order[: phase + 1])]
    return base + goals.index(goal)


def lags_of(ways):
    return [1 + 2 * p for p in range(len(chip_orders(ways)[0]) + 1)]


def reducer_scratch(ways, rows, width):
    steps = rows // RB
    return [
        pltpu.VMEM((ways, rows, width), jnp.bfloat16),
        pltpu.VMEM((ways - 1, rows, width), jnp.bfloat16),
        pltpu.SemaphoreType.DMA((steps, 2 * ways)),
        pltpu.SemaphoreType.DMA((steps, 2 * ways)),
    ]


def branch_kernel(
    ways,
    steps,
    att_ref,
    hidden_ref,
    grad_ref,
    token_ref,
    wout_ref,
    wd_ref,
    out_ref,
    wgrad_ref,
    parts,
    inbox,
    send_sem,
    recv_sem,
    acc,
):
    f32, bf16 = jnp.float32, jnp.bfloat16
    t = pl.program_id(0)
    me, width = lax.axis_index("col"), D // ways
    lags = lags_of(ways)
    ring = Reducer(ways, parts, inbox, send_sem, recv_sem)

    @pl.when(t == 0)
    def _():
        acc[...] = jnp.zeros_like(acc)
        meet([{"col": flip(me, 1 << k)} for k in range(ways.bit_length() - 1)])

    @pl.when(t < steps)
    def _():
        rows = pl.ds(pl.multiple_of(t * RB, RB), RB)
        att, hidden = att_ref[...], hidden_ref[...]
        for o in range(ways):
            cols = pl.ds(pl.multiple_of(flip(me, o) * width, width), width)
            total = lax.dot_general(att, wout_ref[cols, :], NT, preferred_element_type=f32)
            total += jnp.dot(hidden, wd_ref[:, cols], preferred_element_type=f32)
            parts[o, rows, :] = total.astype(bf16)

    ring.advance(t, steps, lags)

    @pl.when(t < steps)
    def _():
        acc[...] += contract(hidden_ref[...], grad_ref[...], 0, 0)

    @pl.when(t == steps)
    def _():
        wgrad_ref[...] = acc[...].astype(bf16)

    s = t - lags[-1]

    @pl.when(s >= 0)
    def _():
        for k, value in enumerate(ring.absorb(s, ring.phases - 1)):
            half = slice(k * (RB // 2), (k + 1) * (RB // 2))
            out_ref[half, :] = (token_ref[half, :].astype(f32) + value).astype(bf16)
        ring.finish(s)


def branches(att, hidden, grad, tokens, weights, wd, ways):
    rows, width = tokens.shape
    ffn = wd.shape[0]
    steps = rows // RB
    lag = lags_of(ways)[-1]
    now = lambda t: (jnp.minimum(t, steps - 1), 0)
    late = lambda t: (jnp.maximum(t - lag, 0), 0)
    fixed = lambda t: (0, 0)
    once = pl.Buffered(1)
    return pl.pallas_call(
        functools.partial(branch_kernel, ways, steps),
        out_shape=[
            jax.ShapeDtypeStruct((rows, width), jnp.bfloat16),
            jax.ShapeDtypeStruct((ffn, D), jnp.bfloat16),
        ],
        grid=(steps + lag,),
        in_specs=[
            pl.BlockSpec((RB, width), now),
            pl.BlockSpec((RB, ffn), now),
            pl.BlockSpec((RB, D), now),
            pl.BlockSpec((RB, width), late),
            pl.BlockSpec((D, width), lambda t: (0, 3), pipeline_mode=once),
            pl.BlockSpec((ffn, D), fixed, pipeline_mode=once),
        ],
        out_specs=[
            pl.BlockSpec((RB, width), late),
            pl.BlockSpec((ffn, D), fixed, pipeline_mode=once),
        ],
        scratch_shapes=[*reducer_scratch(ways, rows, width), pltpu.VMEM((ffn, D), jnp.float32)],
        compiler_params=pltpu.CompilerParams(
            collective_id=1,
            has_side_effects=True,
            dimension_semantics=("arbitrary",),
            vmem_limit_bytes=60 << 20,
        ),
        cost_estimate=pl.CostEstimate(
            flops=8 * rows * D * (2 * ffn + width), bytes_accessed=4 * rows * D, transcendentals=0
        ),
        name="branches",
    )(att, hidden, grad, tokens, weights, wd)


def back_kernel(
    ways,
    lines,
    steps,
    gp_ref,
    gg_ref,
    gu_ref,
    x_ref,
    token_ref,
    cot_ref,
    stat_ref,
    w_ref,
    wgu_ref,
    vectors_ref,
    gain_ref,
    out_ref,
    vgrad_ref,
    parts,
    inbox,
    send_sem,
    recv_sem,
    sums,
    ssend_sem,
    srecv_sem,
    acc,
    vsend_sem,
    vrecv_sem,
):
    f32, bf16 = jnp.float32, jnp.bfloat16
    t = pl.program_id(0)
    me, width = lax.axis_index("col"), D // ways
    line = lax.axis_index("row")
    lags = lags_of(ways)
    ring = Reducer(ways, parts, inbox, send_sem, recv_sem)

    @pl.when(t == 0)
    def _():
        acc[...] = jnp.zeros_like(acc)
        meet(
            [{"col": flip(me, k)} for k in range(1, ways)]
            + [{"row": (line + k) % lines} for k in range(1, lines)]
        )

    def sum_copies(group):
        rows = pl.ds(pl.multiple_of(group * (SUMS * RB), SUMS * RB), SUMS * RB)
        for k in range(1, ways):
            yield pltpu.make_async_remote_copy(
                src_ref=sums.at[0, :, rows],
                dst_ref=sums.at[k, :, rows],
                send_sem=ssend_sem.at[group, k - 1],
                recv_sem=srecv_sem.at[group, k - 1],
                device_id={"col": flip(me, k)},
                device_id_type=MESH,
            )

    @pl.when(t < steps)
    def _():
        rows = pl.ds(pl.multiple_of(t * RB, RB), RB)
        gp, gg, gu = gp_ref[...], gg_ref[...], gu_ref[...]
        plain = jnp.zeros((RB, 1), f32)
        cross = jnp.zeros((RB, 1), f32)
        for o in range(ways):
            cols = pl.ds(pl.multiple_of(flip(me, o) * width, width), width)
            total = jnp.dot(gg, wgu_ref[0, :, cols], preferred_element_type=f32)
            total += jnp.dot(gu, wgu_ref[1, :, cols], preferred_element_type=f32)
            total += lax.dot_general(gp, w_ref[cols, :], NT, preferred_element_type=f32)
            parts[o, rows, :] = total.astype(bf16)
            scaled = x_ref[:, cols].astype(f32) - vectors_ref[1:2, cols]
            plain += jnp.sum(total * vectors_ref[0:1, cols], axis=1, keepdims=True)
            cross += jnp.sum(total * scaled, axis=1, keepdims=True)
        lane = lax.broadcasted_iota(jnp.int32, (RB, 128), 1)
        pair = jnp.where(lane == 0, plain, jnp.where(lane == 1, cross, 0.0))
        sums[0, :, rows] = pair.T[:8]

        @pl.when(t % SUMS == SUMS - 1)
        def _():
            for copy in sum_copies(t // SUMS):
                copy.start()

    ring.advance(t, steps, lags)
    s = t - lags[-1]

    @pl.when(s >= 0)
    def _():
        rows = pl.ds(pl.multiple_of(s * RB, RB), RB)

        @pl.when(s % SUMS == 0)
        def _():
            for copy in sum_copies(s // SUMS):
                copy.wait_recv()

        both = sum(sums[k, :, rows] for k in range(ways)).T
        for k, value in enumerate(ring.absorb(s, ring.phases - 1)):
            half = slice(k * (RB // 2), (k + 1) * (RB // 2))
            inv = stat_ref[half, 1:]
            unit = (token_ref[half, :].astype(f32) - stat_ref[half, :1]) * inv
            scaled = value * gain_ref[0:1, :]
            out_ref[half, :] = cot_ref[half, :].astype(f32) + inv * (
                scaled - both[half, 0:1] / D - unit * (both[half, 1:2] / D)
            )
            acc[0, 0:1, :] += jnp.sum(value * unit, axis=0, keepdims=True)
            acc[0, 1:2, :] += jnp.sum(value, axis=0, keepdims=True)

        @pl.when(s % SUMS == 0)
        def _():
            for copy in sum_copies(s // SUMS):
                copy.wait_send()

        ring.finish(s)

    @pl.when(t == pl.num_programs(0) - 1)
    def _():
        copies = [
            pltpu.make_async_remote_copy(
                src_ref=acc.at[0],
                dst_ref=acc.at[k],
                send_sem=vsend_sem.at[k - 1],
                recv_sem=vrecv_sem.at[k - 1],
                device_id={"row": (line + k) % lines},
                device_id_type=MESH,
            )
            for k in range(1, lines)
        ]
        for copy in copies:
            copy.start()
        for copy in copies:
            copy.wait()
        vgrad_ref[...] = sum(acc[k] for k in range(lines))


def norm_back(gp, gg, gu, normed, tokens, cot, stats, weights, wgu, vectors, own, ways, lines):
    rows, width = tokens.shape
    ffn = gg.shape[1]
    steps = rows // RB
    lag = lags_of(ways)[-1]
    now = lambda t: (jnp.minimum(t, steps - 1), 0)
    late = lambda t: (jnp.maximum(t - lag, 0), 0)
    fixed = lambda t: (0, 0)
    once = pl.Buffered(1)
    dma = pltpu.SemaphoreType.DMA
    return pl.pallas_call(
        functools.partial(back_kernel, ways, lines, steps),
        out_shape=[
            jax.ShapeDtypeStruct((rows, width), jnp.float32),
            jax.ShapeDtypeStruct((8, width), jnp.float32),
        ],
        grid=(steps + lag,),
        in_specs=[
            pl.BlockSpec((RB, 3 * width), now),
            pl.BlockSpec((RB, ffn), now),
            pl.BlockSpec((RB, ffn), now),
            pl.BlockSpec((RB, D), now),
            pl.BlockSpec((RB, width), late),
            pl.BlockSpec((RB, width), late),
            pl.BlockSpec((RB, 2), late),
            pl.BlockSpec((D, 3 * width), fixed, pipeline_mode=once),
            pl.BlockSpec((2, ffn, D), lambda t: (0, 0, 0), pipeline_mode=once),
            pl.BlockSpec((8, D), fixed),
            pl.BlockSpec((8, width), fixed),
        ],
        out_specs=[pl.BlockSpec((RB, width), late), pl.BlockSpec((8, width), fixed)],
        scratch_shapes=[
            *reducer_scratch(ways, rows, width),
            pltpu.VMEM((ways, 8, rows), jnp.float32),
            dma((steps // SUMS, ways - 1)),
            dma((steps // SUMS, ways - 1)),
            pltpu.VMEM((lines, 8, width), jnp.float32),
            dma((lines - 1,)),
            dma((lines - 1,)),
        ],
        compiler_params=pltpu.CompilerParams(
            collective_id=2,
            has_side_effects=True,
            dimension_semantics=("arbitrary",),
            vmem_limit_bytes=61 << 20,
        ),
        cost_estimate=pl.CostEstimate(
            flops=4 * rows * D * (2 * ffn + 3 * width), bytes_accessed=6 * rows * D, transcendentals=0
        ),
        name="norm_back",
    )(gp, gg, gu, normed, tokens, cot, stats, weights, wgu, vectors, own)


def after(value, *others):
    return lax.optimization_barrier((value, others))[0]


def local(
    tokens,
    norm_gain,
    norm_bias,
    qkv_weight,
    gate_up_weight,
    out_weight,
    down_weight,
    image_start,
    doc_ids,
    out_grad,
):
    f32, bf16 = jnp.float32, jnp.bfloat16
    block_rows, width = tokens.shape
    ways = D // width
    lines = D // qkv_weight.shape[0]

    own = jnp.concatenate([qkv_weight[:, k] for k in range(3)] + [out_weight], axis=1)
    weights = lax.all_gather(own, "row", axis=0, tiled=True)
    full_gate_up = lax.all_gather(gate_up_weight, "row", axis=0, tiled=True)
    full_down = lax.all_gather(down_weight, "row", axis=0, tiled=True)
    wgu = jnp.transpose(full_gate_up, (1, 2, 0))
    wd = jnp.transpose(full_down, (1, 0))
    own_vectors = jnp.pad(jnp.stack([norm_gain, norm_bias]), ((0, 6), (0, 0)))

    half = block_rows // 2
    normed, grad, stats, vectors = gather_first(tokens, out_grad, own_vectors, half, ways)
    normed, grad, stats, *earlier = gather_rest(
        tokens, out_grad, vectors, weights, doc_ids, image_start, stats, normed, grad, ways
    )
    attended, grad_projected = attention(
        half // LEN, normed, grad, weights, image_start, doc_ids, earlier
    )

    def weight_sum(grad):
        return lax.psum_scatter(grad, "row", scatter_dimension=0, tiled=True)

    def weight_grad(left, right):
        return contract(left, right, 0, 0).astype(bf16)

    grad_qkv = weight_grad(normed, grad_projected)
    grad_out = weight_grad(grad, attended)
    hidden, grad_gate, grad_up = feed_forward(after(normed, grad_qkv, grad_out), grad, wgu, wd)
    weight_gate = weight_grad(normed, grad_gate)
    weight_up = weight_grad(normed, after(grad_up, weight_gate))
    outputs, weight_down = branches(
        after(attended, weight_up), hidden, grad, tokens, weights, wd, ways
    )
    input_grad, vector_grads = norm_back(
        after(grad_projected, outputs),
        grad_gate,
        grad_up,
        normed,
        tokens,
        out_grad,
        stats,
        weights,
        wgu,
        vectors,
        own_vectors,
        ways,
        lines,
    )
    qkv_sum = after(weight_sum(grad_qkv.reshape(D, 3, width)), input_grad).astype(f32)
    out_sum = after(weight_sum(grad_out), input_grad).astype(f32)
    gate_sum = after(weight_sum(weight_gate), input_grad)
    up_sum = weight_sum(weight_up)
    down_sum = weight_sum(jnp.transpose(weight_down, (1, 0))).astype(f32)
    gate_up_sum = jnp.stack([gate_sum.astype(f32), up_sum.astype(f32)], axis=1)
    return (
        outputs,
        input_grad,
        vector_grads[0],
        vector_grads[1],
        qkv_sum,
        gate_up_sum,
        out_sum,
        down_sum,
    )


def solution(mesh):
    placed = (
        P("row", "col"),
        P("col"),
        P("col"),
        P("row", None, "col"),
        P("row", None, "col"),
        P("row", "col"),
        P("row", "col"),
        P("row"),
        P("row", None),
        P("row", "col"),
    )
    return jax.shard_map(
        local,
        mesh=mesh,
        in_specs=placed,
        out_specs=(
            P("row", "col"),
            P("row", "col"),
            P("col"),
            P("col"),
            P("row", None, "col"),
            P("row", None, "col"),
            P("row", "col"),
            P("row", "col"),
        ),
        check_vma=False,
    )
```

```python
import functools

import jax
import jax.numpy as jnp
import numpy as np
from jax import lax
from jax.experimental import pallas as pl
from jax.experimental.pallas import tpu as pltpu
from jax.sharding import PartitionSpec as P

D = 2048
HD = 64
ROT = 16
LEN = 1024
IMG = 256
QB = 256
MB = 512
RB = 256
GB = 512
SUMS = 4


NORM_EPS = 1e-05
MESH = pl.DeviceIdType.MESH
MASKED_SCORE = -1e30
ROPE_BASE = 10000.0
NT = (((1,), (1,)), ((), ()))


def contract(left, right, left_dim, right_dim):
    return lax.dot_general(
        left, right, (((left_dim,), (right_dim,)), ((), ())), preferred_element_type=jnp.float32
    )


def rope_rows():
    half = ROT // 2
    inv_freq = np.float32(ROPE_BASE) ** (np.float32(-2.0 / ROT) * np.arange(half, dtype=np.float32))
    angles = np.arange(LEN, dtype=np.float32)[None, :] * inv_freq[:, None]
    wide = angles.astype(np.float64)
    return np.concatenate([np.cos(wide), np.sin(wide)]).astype(np.float32)


def fill_tables(rows_ref, tables):
    half = ROT // 2
    for i in range(LEN // QB):
        sl = pl.ds(i * QB, QB)
        cosines, sines = rows_ref[:half, sl], rows_ref[half:, sl]
        zero = jnp.zeros_like(sines)
        rest = [zero] * (HD // half - 2)
        ones = [jnp.ones_like(sines)] * (HD // half - 2)
        tables[0, sl, :] = jnp.concatenate([cosines, cosines, *ones] * (128 // HD), axis=0).T
        tables[1, sl, :] = jnp.concatenate([-sines, zero, *rest] * (128 // HD), axis=0).T
        tables[2, sl, :] = jnp.concatenate([zero, sines, *rest] * (128 // HD), axis=0).T


def turn(x, tables, sl, sign):
    width = x.shape[1]
    c, a, b = (jnp.concatenate([tables[k, sl, :]] * (width // 128), axis=1) for k in range(3))
    left = pltpu.roll(x, width - ROT // 2, 1)
    right = pltpu.roll(x, ROT // 2, 1)
    return x * c + (left * a + right * b) * sign


class Attention:
    def __init__(self, heads, scratch):
        self.heads, self.width = heads, heads * HD
        (
            self.tables,
            self.span,
            self.data,
            self.kt,
            self.vt,
            self.s,
            self.d,
            self.e,
            self.bias,
            self.m,
            self.l,
            self.x,
            self.ot,
            self.dqt,
            self.dk,
            self.dv,
        ) = scratch

    @staticmethod
    def scratch(heads):
        f32, bf16, blocks, width = jnp.float32, jnp.bfloat16, LEN // QB, heads * HD
        return [
            pltpu.VMEM((3, LEN, 128), f32),
            pltpu.VMEM((blocks, 8, QB), jnp.int32),
            pltpu.VMEM((LEN, 4 * width), bf16),
            pltpu.VMEM((blocks, width, QB), bf16),
            pltpu.VMEM((blocks, width, QB), bf16),
            pltpu.VMEM((blocks, heads, QB, QB), f32),
            pltpu.VMEM((blocks, heads, QB, QB), f32),
            pltpu.VMEM((blocks, heads, QB, QB), bf16),
            pltpu.VMEM((QB, QB), f32),
            pltpu.VMEM((heads, 8, QB), f32),
            pltpu.VMEM((heads, 8, QB), f32),
            pltpu.VMEM((heads, 8, QB), f32),
            pltpu.VMEM((width, QB), f32),
            pltpu.VMEM((width, QB), f32),
            pltpu.VMEM((LEN, width), f32),
            pltpu.VMEM((LEN, width), f32),
        ]

    def part(self, kind):
        return pl.ds(kind * self.width, self.width)

    def begin(self, doc_ref, seq, start, x_ref, g_ref, w_ref):
        f32, bf16, width = jnp.float32, jnp.bfloat16, self.width
        docs = doc_ref[pl.ds(seq, 1), :].astype(f32)
        down = jnp.broadcast_to(docs, (128, LEN)).T[:, :1]
        for i in range(LEN // QB):
            own = docs[:, i * QB : (i + 1) * QB]
            first = jnp.sum((down < own).astype(jnp.int32), axis=0, keepdims=True)
            last = jnp.sum((down <= own).astype(jnp.int32), axis=0, keepdims=True) - 1
            at = lax.broadcasted_iota(jnp.int32, (1, QB), 1) + i * QB
            inside = (at >= start) & (at < start + IMG)
            self.span[i, 0:1, :] = first
            self.span[i, 1:2, :] = jnp.where(inside, jnp.minimum(last, start + IMG - 1), at)

        def block(i, _):
            sl = pl.ds(pl.multiple_of(i * QB, QB), QB)
            x = x_ref[sl, :]
            q = jnp.dot(x, w_ref[:, :width], preferred_element_type=f32)
            k = jnp.dot(x, w_ref[:, width : 2 * width], preferred_element_type=f32)
            v = jnp.dot(x, w_ref[:, 2 * width : 3 * width], preferred_element_type=f32)
            g = jnp.dot(g_ref[sl, :], w_ref[:, 3 * width :], preferred_element_type=f32)
            q = turn(q, self.tables, sl, 1.0).astype(bf16).astype(f32) * HD**-0.5
            k = turn(k, self.tables, sl, 1.0).astype(bf16)
            self.data[sl, self.part(0)] = q.astype(bf16)
            self.data[sl, self.part(1)] = k
            self.data[sl, self.part(2)] = v.astype(bf16)
            self.data[sl, self.part(3)] = g.astype(bf16)
            self.kt[i] = k.astype(f32).T.astype(bf16)
            self.vt[i] = v.T.astype(bf16)
            return 0

        lax.fori_loop(0, LEN // QB, block, 0)
        self.dk[...] = jnp.zeros_like(self.dk)
        self.dv[...] = jnp.zeros_like(self.dv)

    def bounds(self, i):
        return jnp.min(self.span[i, 0:1, :]) // QB, jnp.max(self.span[i, 1:2, :]) // QB

    def query_block(self, i, low, high, att_ref, gp_ref):
        f32, bf16, heads, width = jnp.float32, jnp.bfloat16, self.heads, self.width
        rows = pl.ds(pl.multiple_of(i * QB, QB), QB)
        lane = lax.broadcasted_iota(jnp.int32, (1, width), 1) // HD
        first, final = self.span[i, 0:1, :], self.span[i, 1:2, :]
        q, g = self.data[rows, self.part(0)], self.data[rows, self.part(3)]
        zero = jnp.zeros_like(q)
        q_own = [jnp.where(lane == h, q, zero) for h in range(heads)]
        g_own = [jnp.where(lane == h, g, zero) for h in range(heads)]
        self.m[...] = jnp.full_like(self.m, MASKED_SCORE)

        def fold(x, op):
            out = x[:8]
            for r in range(8, QB, 8):
                out = op(out, x[r : r + 8])
            return out

        def score(kb, _):
            keys = pl.ds(pl.multiple_of(kb * QB, QB), QB)
            k, v = self.data[keys, self.part(1)], self.data[keys, self.part(2)]
            at = lax.broadcasted_iota(jnp.int32, (QB, QB), 0) + kb * QB
            self.bias[...] = jnp.where((at >= first) & (at <= final), 0.0, MASKED_SCORE)
            for h in range(heads):
                s = lax.dot_general(k, q_own[h], NT, preferred_element_type=f32) + self.bias[...]
                self.s[kb, h] = s
                self.m[h] = jnp.maximum(self.m[h], fold(s, jnp.maximum))
                self.d[kb, h] = lax.dot_general(v, g_own[h], NT, preferred_element_type=f32)
            return 0

        lax.fori_loop(low, high + 1, score, 0)
        for h in range(heads):
            self.m[h] = jnp.broadcast_to(jnp.max(self.m[h], axis=0, keepdims=True), (8, QB))
        self.l[...] = jnp.zeros_like(self.l)
        self.x[...] = jnp.zeros_like(self.x)
        self.ot[...] = jnp.zeros_like(self.ot)
        self.dqt[...] = jnp.zeros_like(self.dqt)

        def expo(kb, _):
            for h in range(heads):
                hs = slice(h * HD, (h + 1) * HD)
                e = jnp.exp(self.s[kb, h] - self.m[h, 0:1, :])
                self.l[h] += fold(e, jnp.add)
                self.x[h] += fold(e * self.d[kb, h], jnp.add)
                e = e.astype(bf16)
                self.e[kb, h] = e
                self.ot[hs, :] += jnp.dot(self.vt[kb, hs, :], e, preferred_element_type=f32)
            return 0

        lax.fori_loop(low, high + 1, expo, 0)
        for h in range(heads):
            inv = 1.0 / jnp.sum(self.l[h], axis=0, keepdims=True)
            self.l[h] = jnp.broadcast_to(inv, (8, QB))
            delta = jnp.sum(self.x[h], axis=0, keepdims=True) * inv
            self.x[h] = jnp.broadcast_to(delta, (8, QB))

        def back(kb, _):
            keys = pl.ds(pl.multiple_of(kb * QB, QB), QB)
            dk = self.dk[keys, :]
            dv = self.dv[keys, :]
            for h in range(heads):
                hs = slice(h * HD, (h + 1) * HD)
                p = self.e[kb, h].astype(f32) * self.l[h, 0:1, :]
                ds = (p * (self.d[kb, h] - self.x[h, 0:1, :])).astype(bf16)
                dv += jnp.dot(p.astype(bf16), g_own[h], preferred_element_type=f32)
                dk += jnp.dot(ds, q_own[h], preferred_element_type=f32)
                self.dqt[hs, :] += jnp.dot(self.kt[kb, hs, :], ds, preferred_element_type=f32)
            self.dk[keys, :] = dk
            self.dv[keys, :] = dv
            return 0

        lax.fori_loop(low, high + 1, back, 0)
        for h in range(heads):
            hs = slice(h * HD, (h + 1) * HD)
            self.ot[hs, :] = self.ot[hs, :] * self.l[h, 0:1, :]
        att_ref[rows, :] = self.ot[...].T.astype(bf16)
        dq = self.dqt[...].T * HD**-0.5
        gp_ref[rows, :width] = turn(dq, self.tables, rows, -1.0).astype(bf16)

    def finish(self, gp_ref):
        width = self.width

        def block(i, _):
            sl = pl.ds(pl.multiple_of(i * QB, QB), QB)
            dk = turn(self.dk[sl, :], self.tables, sl, -1.0)
            gp_ref[sl, width : 2 * width] = dk.astype(jnp.bfloat16)
            gp_ref[sl, 2 * width :] = self.dv[sl, :].astype(jnp.bfloat16)
            return 0

        lax.fori_loop(0, LEN // QB, block, 0)


def attention_kernel(
    heads, first, start_ref, x_ref, g_ref, w_ref, doc_ref, rope_ref, *refs
):
    att_ref, gp_ref = refs[2:4]
    seq = pl.program_id(0) + first
    attend = Attention(heads, refs[4:])

    @pl.when(pl.program_id(0) == 0)
    def _():
        fill_tables(rope_ref, attend.tables)

    attend.begin(doc_ref, seq, start_ref[seq], x_ref, g_ref, w_ref)

    def query_block(i, _):
        attend.query_block(i, *attend.bounds(i), att_ref, gp_ref)
        return 0

    lax.fori_loop(0, LEN // QB, query_block, 0)
    attend.finish(gp_ref)


def attention(first, normed, grad, weights, image_start, doc_ids, earlier):
    rows, width = normed.shape[0], weights.shape[1] // 4
    count, heads = rows // LEN, width // HD
    bf16 = jnp.bfloat16
    seq_rows = lambda s, *_: (s + first, 0)
    fixed = lambda s, *_: (0, 0)
    return pl.pallas_call(
        functools.partial(attention_kernel, heads, first),
        out_shape=[jax.ShapeDtypeStruct(e.shape, bf16) for e in earlier],
        grid_spec=pltpu.PrefetchScalarGridSpec(
            num_scalar_prefetch=1,
            grid=(count - first,),
            in_specs=[
                pl.BlockSpec((LEN, D), seq_rows),
                pl.BlockSpec((LEN, D), seq_rows),
                pl.BlockSpec((D, 4 * width), fixed, pipeline_mode=pl.Buffered(1)),
                pl.BlockSpec((count, LEN), fixed),
                pl.BlockSpec((ROT, LEN), fixed),
                pl.BlockSpec(memory_space=pl.ANY),
                pl.BlockSpec(memory_space=pl.ANY),
            ],
            out_specs=[
                pl.BlockSpec((LEN, width), seq_rows),
                pl.BlockSpec((LEN, 3 * width), seq_rows),
            ],
            scratch_shapes=Attention.scratch(heads),
        ),
        input_output_aliases={6: 0, 7: 1},
        compiler_params=pltpu.CompilerParams(
            dimension_semantics=("arbitrary",), vmem_limit_bytes=56 << 20
        ),
        cost_estimate=pl.CostEstimate(
            flops=(count - first) * LEN * (36 * 640 * width + 8 * D * width),
            bytes_accessed=(count - first) * LEN * (width * 8 + 4 * D) + 8 * D * width,
            transcendentals=(count - first) * LEN * 640 * heads,
        ),
        name="attention",
    )(image_start, normed, grad, weights, doc_ids, jnp.asarray(rope_rows()), *earlier)


def ffn_kernel(x_ref, g_ref, wgu_ref, wd_ref, hidden_ref, gg_ref, gu_ref):
    f32, bf16 = jnp.float32, jnp.bfloat16
    x = x_ref[...]
    gate = lax.dot_general(x, wgu_ref[0], NT, preferred_element_type=f32)
    up = lax.dot_general(x, wgu_ref[1], NT, preferred_element_type=f32)
    grad = lax.dot_general(g_ref[...], wd_ref[...], NT, preferred_element_type=f32)
    sigma = jax.nn.sigmoid(gate)
    silu = gate * sigma
    hidden_ref[...] = (silu * up).astype(bf16)
    gg_ref[...] = (grad * up * (sigma + silu * (1.0 - sigma))).astype(bf16)
    gu_ref[...] = (grad * silu).astype(bf16)


def feed_forward(normed, grad, wgu, wd):
    rows, ffn = normed.shape[0], wd.shape[0]
    block = lambda i: (i, 0)
    return pl.pallas_call(
        ffn_kernel,
        out_shape=[jax.ShapeDtypeStruct((rows, ffn), jnp.bfloat16)] * 3,
        grid=(rows // MB,),
        in_specs=[
            pl.BlockSpec((MB, D), block),
            pl.BlockSpec((MB, D), block),
            pl.BlockSpec((2, ffn, D), lambda i: (0, 0, 0), pipeline_mode=pl.Buffered(1)),
            pl.BlockSpec((ffn, D), lambda i: (0, 0), pipeline_mode=pl.Buffered(1)),
        ],
        out_specs=[pl.BlockSpec((MB, ffn), block)] * 3,
        compiler_params=pltpu.CompilerParams(
            dimension_semantics=("arbitrary",), vmem_limit_bytes=56 << 20
        ),
        cost_estimate=pl.CostEstimate(
            flops=6 * rows * D * ffn,
            bytes_accessed=rows * (4 * D + 6 * ffn) + 6 * D * ffn,
            transcendentals=rows * ffn,
        ),
        name="feed_forward",
    )(normed, grad, wgu, wd)


def flip(index, bits):
    bit = 1
    while bit <= bits:
        if bits & bit:
            index = index + bit - 2 * bit * ((index // bit) % 2)
        bit *= 2
    return index


def chip_orders(ways):
    bits = [1 << k for k in range(1, ways.bit_length() - 1)]
    return bits, bits[::-1]


def held(bits):
    found = [0]
    for bit in bits:
        found += [o ^ bit for o in found]
    return found


def meet(peers):
    barrier = pltpu.get_barrier_semaphore()
    for peer in peers:
        pl.semaphore_signal(barrier, inc=1, device_id=peer, device_id_type=MESH)
    pl.semaphore_wait(barrier, len(peers))


def gather_kernel(ways, base, attended, *refs):
    f32, bf16 = jnp.float32, jnp.bfloat16
    me = lax.axis_index("col")
    if attended:
        (token_ref, cot_ref, vectors_ref, w_ref, rope_ref, doc_ref, image_ref, old_ref) = refs[:8]
        (old_normed, old_grad, normed_ref, full_ref, stat_ref, att_ref, gp_ref) = refs[8:15]
        refs = refs[15:]
    else:
        (token_ref, cot_ref, vector_ref, normed_ref, full_ref, stat_ref, vectors_ref) = refs[:7]
        refs = refs[7:]
    (both, load_sem, store_sem, full_sem, send_sem, recv_sem) = refs[:6]
    refs = refs[6:]
    width = token_ref.shape[1]
    rows = both.shape[1]
    pairs = rows // GB
    orders = chip_orders(ways)
    phases = len(orders[0])
    mine = pl.ds(pl.multiple_of(me * width, width), width)
    source = pl.ds(base, rows)
    loads = [
        pltpu.make_async_copy(token_ref.at[source], both.at[me, :, pl.ds(0, width)], load_sem.at[0]),
        pltpu.make_async_copy(cot_ref.at[source], both.at[me, :, pl.ds(width, width)], load_sem.at[1]),
    ]
    for load in loads:
        load.start()
    peers = [flip(me, k) for k in range(1, ways)]
    if attended:
        meet([{"col": flip(me, 1 << k)} for k in range(ways.bit_length() - 1)])
    else:
        vectors_ref[:, mine] = vector_ref[...]
        meet([{"col": peer} for peer in peers])

    def vector_copy(k):
        return pltpu.make_async_remote_copy(
            src_ref=vectors_ref.at[:, mine],
            dst_ref=vectors_ref.at[:, mine],
            send_sem=refs[0].at[k],
            recv_sem=refs[1].at[k],
            device_id={"col": peers[k]},
            device_id_type=MESH,
        )

    def copies(p, phase):
        for k, order in enumerate(orders):
            bit = order[phase] if phase < phases else 1
            place = pl.ds(pl.multiple_of(p * GB + k * (GB // 2), GB // 2), GB // 2)
            for o in held(order[:phase]):
                index = k * ways + (o ^ bit)
                owner = flip(me, o)
                yield pltpu.make_async_remote_copy(
                    src_ref=both.at[owner, place],
                    dst_ref=both.at[owner, place],
                    send_sem=send_sem.at[p, index],
                    recv_sem=recv_sem.at[p, index],
                    device_id={"col": flip(me, bit)},
                    device_id_type=MESH,
                )

    def start(p, phase):
        for copy in copies(p, phase):
            copy.start()

    def arrive(p, phase):
        for copy in copies(p, phase):
            copy.wait_recv()

    def filed(p, first, out_ref, sem):
        place = pl.ds(pl.multiple_of(p * GB, GB), GB)
        goal = pl.ds(pl.multiple_of(base + p * GB, GB), GB)
        for b in range(ways):
            pltpu.make_async_copy(
                both.at[b, place, pl.ds(first, width)],
                out_ref.at[goal, pl.ds(b * width, width)],
                sem.at[p],
            ).start()

    def filed_wait(p, out_ref, sem):
        place = out_ref.at[pl.ds(base + p * GB, GB)]
        pltpu.make_async_copy(place, place, sem.at[p]).wait()

    def norm(p):
        filed(p, width, full_ref, full_sem)
        for phase in range(phases + 1):
            for copy in copies(p, phase):
                copy.wait_send()

        def block(j, _):
            at = pl.ds(pl.multiple_of(p * GB + j * QB, QB), QB)
            goal = pl.ds(pl.multiple_of(base + p * GB + j * QB, QB), QB)
            sums = sum(both[b, at, :width].astype(f32) for b in range(ways))
            mean = jnp.sum(sums, axis=1, keepdims=True) / D
            squares = jnp.zeros((QB, width), f32)
            for b in range(ways):
                x = both[b, at, :width].astype(f32) - mean
                squares += x * x
            inv = lax.rsqrt(jnp.sum(squares, axis=1, keepdims=True) / D + NORM_EPS)
            stat_ref[goal, :1] = mean
            stat_ref[goal, 1:] = inv
            for b in range(ways):
                cols = slice(b * width, (b + 1) * width)
                x = (both[b, at, :width].astype(f32) - mean) * inv
                x = x * vectors_ref[0:1, cols] + vectors_ref[1:2, cols]
                both[b, at, :width] = x.astype(bf16)
            return 0

        lax.fori_loop(0, GB // QB, block, 0)
        filed(p, 0, normed_ref, store_sem)

    if attended:
        x_scr, g_scr, att_scr, gp_scr, in_sem, out_sem = refs[:6]
        attend = Attention(width // HD, refs[6:])
        stat_ref[pl.ds(0, base), :] = old_ref[pl.ds(0, base), :]

        def fetch(seq):
            place = pl.ds(pl.multiple_of(seq * LEN, LEN), LEN)
            return [
                pltpu.make_async_copy(old_normed.at[place], x_scr, in_sem.at[seq, 0]),
                pltpu.make_async_copy(old_grad.at[place], g_scr, in_sem.at[seq, 1]),
            ]

        def give(seq):
            place = pl.ds(pl.multiple_of(seq * LEN, LEN), LEN)
            return [
                pltpu.make_async_copy(att_scr.at[seq], att_ref.at[place], out_sem.at[seq, 0]),
                pltpu.make_async_copy(gp_scr.at[seq], gp_ref.at[place], out_sem.at[seq, 1]),
            ]

        for move in fetch(0):
            move.start()

    for load in loads:
        load.wait()
    start(0, 0)
    start(1, 0)
    if attended:
        fill_tables(rope_ref, attend.tables)
    else:
        for k in range(ways - 1):
            vector_copy(k).start()
        for k in range(ways - 1):
            vector_copy(k).wait_recv()
    blocks = LEN // QB
    turns = attended * blocks // pairs if attended else 0

    def step(p, _):
        for phase in range(phases):
            if phase or attended:
                arrive(p, phase)
                start(p, phase + 1)
            if phase == 0:
                if attended:
                    pl.when(p + 2 < pairs)(lambda: start(p + 2, 0))
                else:

                    @pl.when(p + 1 < pairs)
                    def _():
                        arrive(p + 1, 0)
                        start(p + 1, 1)

                    pl.when(p + 3 < pairs)(lambda: start(p + 3, 0))

                @pl.when(p >= 1)
                def _():
                    arrive(p - 1, phases)
                    norm(p - 1)

                if attended:
                    seq = p * turns // blocks
                    spot = p * turns % blocks

                    @pl.when(spot == 0)
                    def _():
                        for move in fetch(seq):
                            move.wait()
                        attend.begin(doc_ref, seq, image_ref[seq], x_scr, g_scr, w_ref)

                        @pl.when(seq + 1 < attended)
                        def _():
                            for move in fetch(seq + 1):
                                move.start()

                    def query_block(i, _):
                        low = i // (blocks - 1)
                        attend.query_block(i, low, i + 1 - low, att_scr.at[seq], gp_scr.at[seq])
                        return 0

                    lax.fori_loop(spot, spot + turns, query_block, 0)

                    @pl.when(spot + turns == blocks)
                    def _():
                        attend.finish(gp_scr.at[seq])
                        for move in give(seq):
                            move.start()
        return 0

    if not attended:
        arrive(0, 0)
        start(0, 1)
        start(2, 0)
    lax.fori_loop(0, pairs, step, 0)
    arrive(pairs - 1, phases)
    norm(pairs - 1)
    for p in range(pairs):
        filed_wait(p, full_ref, full_sem)
        filed_wait(p, normed_ref, store_sem)
    if attended:
        for seq in range(attended):
            for move in give(seq):
                move.wait()
    else:
        for k in range(ways - 1):
            vector_copy(k).wait_send()


def gather_scratch(ways, rows, width):
    dma = pltpu.SemaphoreType.DMA
    pairs = rows // GB
    return [
        pltpu.VMEM((ways, rows, 2 * width), jnp.bfloat16),
        dma((2,)),
        dma((pairs,)),
        dma((pairs,)),
        dma((pairs, 2 * ways)),
        dma((pairs, 2 * ways)),
    ]


def gather_first(tokens, out_grad, vectors, count, ways):
    rows, width = tokens.shape
    bf16, f32 = jnp.bfloat16, jnp.float32
    anywhere = pl.BlockSpec(memory_space=pl.ANY)
    vmem = pl.BlockSpec(memory_space=pltpu.VMEM)
    dma = pltpu.SemaphoreType.DMA
    return pl.pallas_call(
        functools.partial(gather_kernel, ways, 0, 0),
        out_shape=[
            jax.ShapeDtypeStruct((rows, D), bf16),
            jax.ShapeDtypeStruct((rows, D), bf16),
            jax.ShapeDtypeStruct((rows, 2), f32),
            jax.ShapeDtypeStruct((8, D), f32),
        ],
        in_specs=[anywhere, anywhere, vmem],
        out_specs=[anywhere, anywhere, vmem, vmem],
        scratch_shapes=[*gather_scratch(ways, count, width), dma((ways - 1,)), dma((ways - 1,))],
        compiler_params=pltpu.CompilerParams(
            collective_id=0, has_side_effects=True, vmem_limit_bytes=40 << 20
        ),
        cost_estimate=pl.CostEstimate(
            flops=100 * count * D * D // ways, bytes_accessed=count * D * 8, transcendentals=0
        ),
        name="gather_first",
    )(tokens, out_grad, vectors)


def gather_rest(tokens, out_grad, vectors, weights, doc_ids, image_start, stats, normed, grad, ways):
    rows, width = tokens.shape
    count = rows // 2
    bf16, f32 = jnp.bfloat16, jnp.float32
    anywhere = pl.BlockSpec(memory_space=pl.ANY)
    vmem = pl.BlockSpec(memory_space=pltpu.VMEM)
    dma = pltpu.SemaphoreType.DMA
    seqs = count // LEN
    return pl.pallas_call(
        functools.partial(gather_kernel, ways, count, seqs),
        out_shape=[
            jax.ShapeDtypeStruct((rows, D), bf16),
            jax.ShapeDtypeStruct((rows, D), bf16),
            jax.ShapeDtypeStruct((rows, 2), f32),
            jax.ShapeDtypeStruct((rows, width), bf16),
            jax.ShapeDtypeStruct((rows, 3 * width), bf16),
        ],
        in_specs=[
            anywhere,
            anywhere,
            vmem,
            vmem,
            vmem,
            vmem,
            pl.BlockSpec(memory_space=pltpu.SMEM),
            vmem,
            anywhere,
            anywhere,
        ],
        out_specs=[anywhere, anywhere, vmem, anywhere, anywhere],
        input_output_aliases={8: 0, 9: 1},
        scratch_shapes=[
            *gather_scratch(ways, rows - count, width),
            pltpu.VMEM((LEN, D), bf16),
            pltpu.VMEM((LEN, D), bf16),
            pltpu.VMEM((seqs, LEN, width), bf16),
            pltpu.VMEM((seqs, LEN, 3 * width), bf16),
            dma((seqs, 2)),
            dma((seqs, 2)),
            *Attention.scratch(width // HD),
        ],
        compiler_params=pltpu.CompilerParams(
            collective_id=3, has_side_effects=True, vmem_limit_bytes=60 << 20
        ),
        cost_estimate=pl.CostEstimate(
            flops=100 * count * D * D // ways, bytes_accessed=count * D * 8, transcendentals=0
        ),
        name="gather_rest",
    )(tokens, out_grad, vectors, weights, jnp.asarray(rope_rows()), doc_ids, image_start, stats, normed, grad)


class Reducer:
    def __init__(self, ways, parts, inbox, send_sem, recv_sem):
        self.ways, self.parts, self.inbox = ways, parts, inbox
        self.send_sem, self.recv_sem = send_sem, recv_sem
        self.me = lax.axis_index("col")
        self.orders = chip_orders(ways)
        self.phases = 1 + len(self.orders[0])

    def moves(self, step, phase):
        halves = [None] if phase == 0 else [0, 1]
        for k in halves:
            order = [1] if phase == 0 else [1, *self.orders[k]]
            bit = order[phase]
            done = sum(order[:phase])
            count = RB if k is None else RB // 2
            rows = pl.ds(pl.multiple_of(step * RB + (k or 0) * count, count), count)
            for o in range(self.ways):
                if o & done or not o & bit:
                    continue
                goal = o ^ bit
                slot = slot_of(self.ways, self.orders, phase, k, goal)
                sem = 2 * slot + (k or 0)
                copy = pltpu.make_async_remote_copy(
                    src_ref=self.parts.at[o, rows],
                    dst_ref=self.inbox.at[slot, rows],
                    send_sem=self.send_sem.at[step, sem],
                    recv_sem=self.recv_sem.at[step, sem],
                    device_id={"col": flip(self.me, bit)},
                    device_id_type=MESH,
                )
                yield copy, goal, slot, rows

    def send(self, step, phase):
        for copy, *_ in self.moves(step, phase):
            copy.start()

    def absorb(self, step, phase):
        out = []
        for copy, goal, slot, rows in self.moves(step, phase):
            copy.wait_recv()
            value = self.parts[goal, rows, :].astype(jnp.float32)
            value += self.inbox[slot, rows, :].astype(jnp.float32)
            if phase == self.phases - 1:
                out.append(value)
            else:
                self.parts[goal, rows, :] = value.astype(jnp.bfloat16)
        return out

    def finish(self, step):
        for phase in range(self.phases):
            for copy, *_ in self.moves(step, phase):
                copy.wait_send()

    def advance(self, t, steps, lags):
        pl.when(t < steps)(lambda: self.send(t, 0))
        for phase in range(self.phases - 1):
            s = t - lags[phase]

            @pl.when((s >= 0) & (s < steps))
            def _():
                self.absorb(s, phase)
                self.send(s, phase + 1)


def slot_of(ways, orders, phase, half, goal):
    if phase == 0:
        return goal // 2
    order = [1, *orders[half]]
    base = ways // 2
    for p in range(1, phase):
        base += ways >> (p + 1)
    goals = [g for g in range(ways) if not g & sum(order[: phase + 1])]
    return base + goals.index(goal)


def lags_of(ways):
    return [1 + 2 * p for p in range(len(chip_orders(ways)[0]) + 1)]


def reducer_scratch(ways, rows, width):
    steps = rows // RB
    return [
        pltpu.VMEM((ways, rows, width), jnp.bfloat16),
        pltpu.VMEM((ways - 1, rows, width), jnp.bfloat16),
        pltpu.SemaphoreType.DMA((steps, 2 * ways)),
        pltpu.SemaphoreType.DMA((steps, 2 * ways)),
    ]


def branch_kernel(
    ways,
    steps,
    att_ref,
    hidden_ref,
    grad_ref,
    token_ref,
    wout_ref,
    wd_ref,
    out_ref,
    wgrad_ref,
    wout_grad_ref,
    parts,
    inbox,
    send_sem,
    recv_sem,
    acc,
    acc_out,
):
    f32, bf16 = jnp.float32, jnp.bfloat16
    t = pl.program_id(0)
    me, width = lax.axis_index("col"), D // ways
    lags = lags_of(ways)
    ring = Reducer(ways, parts, inbox, send_sem, recv_sem)

    @pl.when(t == 0)
    def _():
        acc[...] = jnp.zeros_like(acc)
        acc_out[...] = jnp.zeros_like(acc_out)
        meet([{"col": flip(me, 1 << k)} for k in range(ways.bit_length() - 1)])

    @pl.when(t < steps)
    def _():
        rows = pl.ds(pl.multiple_of(t * RB, RB), RB)
        att, hidden = att_ref[...], hidden_ref[...]
        for o in range(ways):
            cols = pl.ds(pl.multiple_of(flip(me, o) * width, width), width)
            total = lax.dot_general(att, wout_ref[cols, :], NT, preferred_element_type=f32)
            total += jnp.dot(hidden, wd_ref[:, cols], preferred_element_type=f32)
            parts[o, rows, :] = total.astype(bf16)

    ring.advance(t, steps, lags)

    @pl.when(t < steps)
    def _():
        acc[...] += contract(hidden_ref[...], grad_ref[...], 0, 0)
        acc_out[...] += contract(att_ref[...], grad_ref[...], 0, 0)

    @pl.when(t == steps)
    def _():
        wgrad_ref[...] = acc[...].astype(bf16)
        wout_grad_ref[...] = acc_out[...].astype(bf16)

    s = t - lags[-1]

    @pl.when(s >= 0)
    def _():
        for k, value in enumerate(ring.absorb(s, ring.phases - 1)):
            half = slice(k * (RB // 2), (k + 1) * (RB // 2))
            out_ref[half, :] = (token_ref[half, :].astype(f32) + value).astype(bf16)
        ring.finish(s)


def branches(att, hidden, grad, tokens, weights, wd, ways):
    rows, width = tokens.shape
    ffn = wd.shape[0]
    steps = rows // RB
    lag = lags_of(ways)[-1]
    now = lambda t: (jnp.minimum(t, steps - 1), 0)
    late = lambda t: (jnp.maximum(t - lag, 0), 0)
    fixed = lambda t: (0, 0)
    once = pl.Buffered(1)
    return pl.pallas_call(
        functools.partial(branch_kernel, ways, steps),
        out_shape=[
            jax.ShapeDtypeStruct((rows, width), jnp.bfloat16),
            jax.ShapeDtypeStruct((ffn, D), jnp.bfloat16),
            jax.ShapeDtypeStruct((width, D), jnp.bfloat16),
        ],
        grid=(steps + lag,),
        in_specs=[
            pl.BlockSpec((RB, width), now),
            pl.BlockSpec((RB, ffn), now),
            pl.BlockSpec((RB, D), now),
            pl.BlockSpec((RB, width), late),
            pl.BlockSpec((D, width), lambda t: (0, 3), pipeline_mode=once),
            pl.BlockSpec((ffn, D), fixed, pipeline_mode=once),
        ],
        out_specs=[
            pl.BlockSpec((RB, width), late),
            pl.BlockSpec((ffn, D), fixed, pipeline_mode=once),
            pl.BlockSpec((width, D), fixed, pipeline_mode=once),
        ],
        scratch_shapes=[
            *reducer_scratch(ways, rows, width),
            pltpu.VMEM((ffn, D), jnp.float32),
            pltpu.VMEM((width, D), jnp.float32),
        ],
        compiler_params=pltpu.CompilerParams(
            collective_id=1,
            has_side_effects=True,
            dimension_semantics=("arbitrary",),
            vmem_limit_bytes=60 << 20,
        ),
        cost_estimate=pl.CostEstimate(
            flops=8 * rows * D * (2 * ffn + width), bytes_accessed=4 * rows * D, transcendentals=0
        ),
        name="branches",
    )(att, hidden, grad, tokens, weights, wd)


def back_kernel(
    ways,
    lines,
    steps,
    gp_ref,
    gg_ref,
    gu_ref,
    x_ref,
    token_ref,
    cot_ref,
    stat_ref,
    w_ref,
    wgu_ref,
    vectors_ref,
    gain_ref,
    wqkv_ref,
    out_ref,
    vgrad_ref,
    qkv_ref,
    parts,
    inbox,
    send_sem,
    recv_sem,
    sums,
    ssend_sem,
    srecv_sem,
    acc,
    vsend_sem,
    vrecv_sem,
):
    f32, bf16 = jnp.float32, jnp.bfloat16
    t = pl.program_id(0)
    me, width = lax.axis_index("col"), D // ways
    line = lax.axis_index("row")
    lags = lags_of(ways)
    ring = Reducer(ways, parts, inbox, send_sem, recv_sem)

    @pl.when(t == 0)
    def _():
        acc[...] = jnp.zeros_like(acc)
        meet(
            [{"col": flip(me, k)} for k in range(1, ways)]
            + [{"row": (line + k) % lines} for k in range(1, lines)]
        )

    def sum_copies(group):
        rows = pl.ds(pl.multiple_of(group * RB, RB), RB)
        for k in range(1, ways):
            yield pltpu.make_async_remote_copy(
                src_ref=sums.at[0, :, rows],
                dst_ref=sums.at[k, :, rows],
                send_sem=ssend_sem.at[group, k - 1],
                recv_sem=srecv_sem.at[group, k - 1],
                device_id={"col": flip(me, k)},
                device_id_type=MESH,
            )

    @pl.when(t < steps)
    def _():
        rows = pl.ds(pl.multiple_of(t * RB, RB), RB)
        gp, gg, gu = gp_ref[...], gg_ref[...], gu_ref[...]
        plain = jnp.zeros((RB, 1), f32)
        cross = jnp.zeros((RB, 1), f32)
        for o in range(ways):
            cols = pl.ds(pl.multiple_of(flip(me, o) * width, width), width)
            total = jnp.dot(gg, wgu_ref[0, :, cols], preferred_element_type=f32)
            total += jnp.dot(gu, wgu_ref[1, :, cols], preferred_element_type=f32)
            total += lax.dot_general(gp, w_ref[cols, :], NT, preferred_element_type=f32)
            parts[o, rows, :] = total.astype(bf16)
            scaled = x_ref[:, cols].astype(f32) - vectors_ref[1:2, cols]
            plain += jnp.sum(total * vectors_ref[0:1, cols], axis=1, keepdims=True)
            cross += jnp.sum(total * scaled, axis=1, keepdims=True)
        lane = lax.broadcasted_iota(jnp.int32, (RB, 128), 1)
        spot = 2 * (t % SUMS)
        pair = jnp.where(lane == spot, plain, jnp.where(lane == spot + 1, cross, 0.0))
        group = pl.ds(pl.multiple_of(t // SUMS * RB, RB), RB)
        before = jnp.where(jnp.broadcast_to(spot == 0, (8, RB)), 0.0, sums[0, :, group])
        sums[0, :, group] = before + pair.T[:8]
        for kind in range(3):
            qkv_ref[kind] = wqkv_ref[:, kind * width : (kind + 1) * width].astype(f32)

        @pl.when(t % SUMS == SUMS - 1)
        def _():
            for copy in sum_copies(t // SUMS):
                copy.start()

    ring.advance(t, steps, lags)
    s = t - lags[-1]

    @pl.when(s >= 0)
    def _():
        @pl.when(s % SUMS == 0)
        def _():
            for copy in sum_copies(s // SUMS):
                copy.wait_recv()

        group = pl.ds(pl.multiple_of(s // SUMS * RB, RB), RB)
        both = sum(sums[k, :, group] for k in range(ways)).T
        lane = lax.broadcasted_iota(jnp.int32, (RB, 8), 1)
        spot = 2 * (s % SUMS)
        plain = jnp.sum(jnp.where(lane == spot, both, 0.0), axis=1, keepdims=True) / D
        cross = jnp.sum(jnp.where(lane == spot + 1, both, 0.0), axis=1, keepdims=True) / D
        for k, value in enumerate(ring.absorb(s, ring.phases - 1)):
            half = slice(k * (RB // 2), (k + 1) * (RB // 2))
            inv = stat_ref[half, 1:]
            unit = (token_ref[half, :].astype(f32) - stat_ref[half, :1]) * inv
            scaled = value * gain_ref[0:1, :]
            out_ref[half, :] = cot_ref[half, :].astype(f32) + inv * (
                scaled - plain[half] - unit * cross[half]
            )
            acc[0, 0:1, :] += jnp.sum(value * unit, axis=0, keepdims=True)
            acc[0, 1:2, :] += jnp.sum(value, axis=0, keepdims=True)

        @pl.when(s % SUMS == 0)
        def _():
            for copy in sum_copies(s // SUMS):
                copy.wait_send()

        ring.finish(s)

    @pl.when(t == pl.num_programs(0) - 1)
    def _():
        copies = [
            pltpu.make_async_remote_copy(
                src_ref=acc.at[0],
                dst_ref=acc.at[k],
                send_sem=vsend_sem.at[k - 1],
                recv_sem=vrecv_sem.at[k - 1],
                device_id={"row": (line + k) % lines},
                device_id_type=MESH,
            )
            for k in range(1, lines)
        ]
        for copy in copies:
            copy.start()
        for copy in copies:
            copy.wait()
        vgrad_ref[...] = sum(acc[k] for k in range(lines))


def norm_back(
    gp, gg, gu, normed, tokens, cot, stats, weights, wgu, vectors, own, qkv, ways, lines
):
    rows, width = tokens.shape
    ffn = gg.shape[1]
    steps = rows // RB
    lag = lags_of(ways)[-1]
    deep = qkv.shape[0]
    slab = deep // steps
    now = lambda t: (jnp.minimum(t, steps - 1), 0)
    late = lambda t: (jnp.maximum(t - lag, 0), 0)
    fixed = lambda t: (0, 0)
    once = pl.Buffered(1)
    dma = pltpu.SemaphoreType.DMA
    return pl.pallas_call(
        functools.partial(back_kernel, ways, lines, steps),
        out_shape=[
            jax.ShapeDtypeStruct((rows, width), jnp.float32),
            jax.ShapeDtypeStruct((8, width), jnp.float32),
            jax.ShapeDtypeStruct((3, deep, width), jnp.float32),
        ],
        grid=(steps + lag,),
        in_specs=[
            pl.BlockSpec((RB, 3 * width), now),
            pl.BlockSpec((RB, ffn), now),
            pl.BlockSpec((RB, ffn), now),
            pl.BlockSpec((RB, D), now),
            pl.BlockSpec((RB, width), late),
            pl.BlockSpec((RB, width), late),
            pl.BlockSpec((RB, 2), late),
            pl.BlockSpec((D, 3 * width), fixed, pipeline_mode=once),
            pl.BlockSpec((2, ffn, D), lambda t: (0, 0, 0), pipeline_mode=once),
            pl.BlockSpec((8, D), fixed),
            pl.BlockSpec((8, width), fixed),
            pl.BlockSpec((slab, 3 * width), now),
        ],
        out_specs=[
            pl.BlockSpec((RB, width), late),
            pl.BlockSpec((8, width), fixed),
            pl.BlockSpec((3, slab, width), lambda t: (0, jnp.minimum(t, steps - 1), 0)),
        ],
        scratch_shapes=[
            *reducer_scratch(ways, rows, width),
            pltpu.VMEM((ways, 8, rows // SUMS), jnp.float32),
            dma((steps // SUMS, ways - 1)),
            dma((steps // SUMS, ways - 1)),
            pltpu.VMEM((lines, 8, width), jnp.float32),
            dma((lines - 1,)),
            dma((lines - 1,)),
        ],
        compiler_params=pltpu.CompilerParams(
            collective_id=2,
            has_side_effects=True,
            dimension_semantics=("arbitrary",),
            vmem_limit_bytes=61 << 20,
        ),
        cost_estimate=pl.CostEstimate(
            flops=4 * rows * D * (2 * ffn + 3 * width), bytes_accessed=6 * rows * D, transcendentals=0
        ),
        name="norm_back",
    )(gp, gg, gu, normed, tokens, cot, stats, weights, wgu, vectors, own, qkv)


def after(value, *others):
    return lax.optimization_barrier((value, others))[0]


def local(
    tokens,
    norm_gain,
    norm_bias,
    qkv_weight,
    gate_up_weight,
    out_weight,
    down_weight,
    image_start,
    doc_ids,
    out_grad,
):
    f32, bf16 = jnp.float32, jnp.bfloat16
    block_rows, width = tokens.shape
    ways = D // width
    lines = D // qkv_weight.shape[0]

    own = jnp.concatenate([qkv_weight[:, k] for k in range(3)] + [out_weight], axis=1)
    weights = lax.all_gather(own, "row", axis=0, tiled=True)
    full_gate_up = lax.all_gather(gate_up_weight, "row", axis=0, tiled=True)
    full_down = lax.all_gather(down_weight, "row", axis=0, tiled=True)
    wgu = jnp.transpose(full_gate_up, (1, 2, 0))
    wd = jnp.transpose(full_down, (1, 0))
    own_vectors = jnp.pad(jnp.stack([norm_gain, norm_bias]), ((0, 6), (0, 0)))

    half = block_rows // 2
    normed, grad, stats, vectors = gather_first(tokens, out_grad, own_vectors, half, ways)
    normed, grad, stats, *earlier = gather_rest(
        tokens, out_grad, vectors, weights, doc_ids, image_start, stats, normed, grad, ways
    )
    attended, grad_projected = attention(
        half // LEN, normed, grad, weights, image_start, doc_ids, earlier
    )

    def weight_sum(grad):
        return lax.psum_scatter(grad, "row", scatter_dimension=0, tiled=True)

    def weight_grad(left, right):
        return contract(left, right, 0, 0).astype(bf16)

    grad_qkv = weight_grad(normed, grad_projected)
    hidden, grad_gate, grad_up = feed_forward(after(normed, grad_qkv), grad, wgu, wd)
    weight_gate = weight_grad(normed, grad_gate)
    weight_up = weight_grad(normed, after(grad_up, weight_gate))
    qkv_sum = weight_sum(grad_qkv)
    gate_sum = weight_sum(weight_gate)
    outputs, weight_down, weight_out = branches(
        after(attended, weight_up, qkv_sum), hidden, grad, tokens, weights, wd, ways
    )
    input_grad, vector_grads, qkv_sum = norm_back(
        after(grad_projected, outputs, gate_sum),
        grad_gate,
        grad_up,
        normed,
        tokens,
        out_grad,
        stats,
        weights,
        wgu,
        vectors,
        own_vectors,
        qkv_sum,
        ways,
        lines,
    )
    qkv_sum = jnp.transpose(qkv_sum, (1, 0, 2))
    up_sum = after(weight_sum(weight_up), input_grad)
    down_sum = weight_sum(jnp.transpose(weight_down, (1, 0))).astype(f32)
    out_sum = weight_sum(jnp.transpose(weight_out, (1, 0))).astype(f32)
    gate_up_sum = jnp.stack([gate_sum.astype(f32), up_sum.astype(f32)], axis=1)
    return (
        outputs,
        input_grad,
        vector_grads[0],
        vector_grads[1],
        qkv_sum,
        gate_up_sum,
        out_sum,
        down_sum,
    )


def solution(mesh):
    placed = (
        P("row", "col"),
        P("col"),
        P("col"),
        P("row", None, "col"),
        P("row", None, "col"),
        P("row", "col"),
        P("row", "col"),
        P("row"),
        P("row", None),
        P("row", "col"),
    )
    return jax.shard_map(
        local,
        mesh=mesh,
        in_specs=placed,
        out_specs=(
            P("row", "col"),
            P("row", "col"),
            P("col"),
            P("col"),
            P("row", None, "col"),
            P("row", None, "col"),
            P("row", "col"),
            P("row", "col"),
        ),
        check_vma=False,
    )
```

```python
import functools

import jax
import jax.numpy as jnp
import numpy as np
from jax import lax
from jax.experimental import pallas as pl
from jax.experimental.pallas import tpu as pltpu
from jax.sharding import PartitionSpec as P

D = 2048
HD = 64
ROT = 16
LEN = 1024
IMG = 256
QB = 256
MB = 256
RB = 256
GB = 256
GA = 256
SUMS = 4


NORM_EPS = 1e-05
MESH = pl.DeviceIdType.MESH
MASKED_SCORE = -1e30
ROPE_BASE = 10000.0
NT = (((1,), (1,)), ((), ()))


def contract(left, right, left_dim, right_dim):
    return lax.dot_general(
        left, right, (((left_dim,), (right_dim,)), ((), ())), preferred_element_type=jnp.float32
    )


def rope_rows():
    half = ROT // 2
    inv_freq = np.float32(ROPE_BASE) ** (np.float32(-2.0 / ROT) * np.arange(half, dtype=np.float32))
    angles = np.arange(LEN, dtype=np.float32)[None, :] * inv_freq[:, None]
    wide = angles.astype(np.float64)
    return np.concatenate([np.cos(wide), np.sin(wide)]).astype(np.float32)


def fill_tables(rows_ref, tables):
    half = ROT // 2
    for i in range(LEN // QB):
        sl = pl.ds(i * QB, QB)
        cosines, sines = rows_ref[:half, sl], rows_ref[half:, sl]
        zero = jnp.zeros_like(sines)
        rest = [zero] * (HD // half - 2)
        ones = [jnp.ones_like(sines)] * (HD // half - 2)
        tables[0, sl, :] = jnp.concatenate([cosines, cosines, *ones] * (128 // HD), axis=0).T
        tables[1, sl, :] = jnp.concatenate([-sines, zero, *rest] * (128 // HD), axis=0).T
        tables[2, sl, :] = jnp.concatenate([zero, sines, *rest] * (128 // HD), axis=0).T


def turn(x, tables, sl, sign):
    width = x.shape[1]
    c, a, b = (jnp.concatenate([tables[k, sl, :]] * (width // 128), axis=1) for k in range(3))
    left = pltpu.roll(x, width - ROT // 2, 1)
    right = pltpu.roll(x, ROT // 2, 1)
    return x * c + (left * a + right * b) * sign


class Attention:
    def __init__(self, heads, scratch):
        self.heads, self.width = heads, heads * HD
        (
            self.tables,
            self.span,
            self.data,
            self.kt,
            self.vt,
            self.s,
            self.d,
            self.e,
            self.bias,
            self.m,
            self.l,
            self.ot,
            self.dqt,
            self.dk,
            self.dv,
        ) = scratch

    @staticmethod
    def scratch(heads):
        f32, bf16, blocks, width = jnp.float32, jnp.bfloat16, LEN // QB, heads * HD
        return [
            pltpu.VMEM((3, LEN, 128), f32),
            pltpu.VMEM((blocks, 8, QB), jnp.int32),
            pltpu.VMEM((LEN, 4 * width), bf16),
            pltpu.VMEM((blocks, width, QB), bf16),
            pltpu.VMEM((blocks, width, QB), bf16),
            pltpu.VMEM((blocks, heads, QB, QB), f32),
            pltpu.VMEM((blocks, heads, QB, QB), f32),
            pltpu.VMEM((blocks, heads, QB, QB), bf16),
            pltpu.VMEM((2, QB, QB), f32),
            pltpu.VMEM((heads, 8, QB), f32),
            pltpu.VMEM((heads, 8, QB), f32),
            pltpu.VMEM((width, QB), f32),
            pltpu.VMEM((width, QB), f32),
            pltpu.VMEM((LEN, width), f32),
            pltpu.VMEM((LEN, width), f32),
        ]

    def part(self, kind):
        return pl.ds(kind * self.width, self.width)

    def begin(self, doc_ref, seq, start, x_ref, g_ref, w_ref):
        f32, bf16, width = jnp.float32, jnp.bfloat16, self.width
        docs = doc_ref[pl.ds(seq, 1), :].astype(f32)
        down = jnp.broadcast_to(docs, (128, LEN)).T[:, :1]
        for i in range(LEN // QB):
            own = docs[:, i * QB : (i + 1) * QB]
            first = jnp.sum((down < own).astype(jnp.int32), axis=0, keepdims=True)
            last = jnp.sum((down <= own).astype(jnp.int32), axis=0, keepdims=True) - 1
            at = lax.broadcasted_iota(jnp.int32, (1, QB), 1) + i * QB
            inside = (at >= start) & (at < start + IMG)
            self.span[i, 0:1, :] = first
            self.span[i, 1:2, :] = jnp.where(inside, jnp.minimum(last, start + IMG - 1), at)

        def block(i, _):
            sl = pl.ds(pl.multiple_of(i * QB, QB), QB)
            x = x_ref[sl, :]
            q = jnp.dot(x, w_ref[:, :width], preferred_element_type=f32)
            k = jnp.dot(x, w_ref[:, width : 2 * width], preferred_element_type=f32)
            v = jnp.dot(x, w_ref[:, 2 * width : 3 * width], preferred_element_type=f32)
            g = jnp.dot(g_ref[sl, :], w_ref[:, 3 * width :], preferred_element_type=f32)
            q = turn(q, self.tables, sl, 1.0).astype(bf16).astype(f32) * HD**-0.5
            k = turn(k, self.tables, sl, 1.0).astype(bf16)
            self.data[sl, self.part(0)] = q.astype(bf16)
            self.data[sl, self.part(1)] = k
            self.data[sl, self.part(2)] = v.astype(bf16)
            self.data[sl, self.part(3)] = g.astype(bf16)
            self.kt[i] = k.astype(f32).T.astype(bf16)
            self.vt[i] = v.T.astype(bf16)
            return 0

        lax.fori_loop(0, LEN // QB, block, 0)
        self.dk[...] = jnp.zeros_like(self.dk)
        self.dv[...] = jnp.zeros_like(self.dv)

    def bounds(self, i):
        return jnp.min(self.span[i, 0:1, :]) // QB, jnp.max(self.span[i, 1:2, :]) // QB

    @staticmethod
    def sweep(low, high, body):
        def two(j, _):
            body(low + 2 * j)
            body(low + 2 * j + 1)
            return 0

        count = high + 1 - low
        lax.fori_loop(0, count // 2, two, 0)
        pl.when(count % 2 == 1)(lambda: body(high))

    def query_block(self, i, low, high, att_ref, gp_ref):
        f32, bf16, heads, width = jnp.float32, jnp.bfloat16, self.heads, self.width
        rows = pl.ds(pl.multiple_of(i * QB, QB), QB)
        lane = lax.broadcasted_iota(jnp.int32, (1, width), 1) // HD
        first, final = self.span[i, 0:1, :], self.span[i, 1:2, :]
        q, g = self.data[rows, self.part(0)], self.data[rows, self.part(3)]
        zero = jnp.zeros_like(q)
        q_own = [jnp.where(lane == h, q, zero) for h in range(heads)]
        g_own = [jnp.where(lane == h, g, zero) for h in range(heads)]
        self.m[...] = jnp.full_like(self.m, MASKED_SCORE)

        def fold(x, op):
            runs = [x[r : r + 8] for r in range(0, QB, 8)]
            lanes = runs[:8]
            for r, run in enumerate(runs[8:]):
                lanes[r % 8] = op(lanes[r % 8], run)
            while len(lanes) > 1:
                lanes = [op(a, b) for a, b in zip(lanes[::2], lanes[1::2])]
            return lanes[0]

        def score(kb):
            keys = pl.ds(pl.multiple_of(kb * QB, QB), QB)
            k, v = self.data[keys, self.part(1)], self.data[keys, self.part(2)]
            at = lax.broadcasted_iota(jnp.int32, (QB, QB), 0) + kb * QB
            bias = jnp.where((at >= first) & (at <= final), 0.0, MASKED_SCORE)
            self.bias[kb % 2] = bias
            for h in range(heads):
                s = lax.dot_general(k, q_own[h], NT, preferred_element_type=f32) + self.bias[kb % 2]
                self.s[kb, h] = s
                self.m[h] = jnp.maximum(self.m[h], fold(s, jnp.maximum))
                self.d[kb, h] = lax.dot_general(v, g_own[h], NT, preferred_element_type=f32)

        self.sweep(low, high, score)
        for h in range(heads):
            self.m[h] = jnp.broadcast_to(jnp.max(self.m[h], axis=0, keepdims=True), (8, QB))
        self.l[...] = jnp.zeros_like(self.l)
        self.ot[...] = jnp.zeros_like(self.ot)
        self.dqt[...] = jnp.zeros_like(self.dqt)

        def expo(kb):
            for h in range(heads):
                hs = slice(h * HD, (h + 1) * HD)
                e = jnp.exp(self.s[kb, h] - self.m[h, 0:1, :])
                self.l[h] += fold(e, jnp.add)
                e = e.astype(bf16)
                self.e[kb, h] = e
                self.ot[hs, :] += jnp.dot(self.vt[kb, hs, :], e, preferred_element_type=f32)

        self.sweep(low, high, expo)
        gt = g.astype(f32).T
        for h in range(heads):
            hs = slice(h * HD, (h + 1) * HD)
            inv = 1.0 / jnp.sum(self.l[h], axis=0, keepdims=True)
            self.l[h] = jnp.broadcast_to(inv, (8, QB))
            out = self.ot[hs, :] * inv
            self.ot[hs, :] = out
            delta = jnp.sum(out * gt[hs], axis=0, keepdims=True)
            self.m[h] = jnp.broadcast_to(delta, (8, QB))

        def back(kb):
            keys = pl.ds(pl.multiple_of(kb * QB, QB), QB)
            dk = self.dk[keys, :]
            dv = self.dv[keys, :]
            for h in range(heads):
                hs = slice(h * HD, (h + 1) * HD)
                p = self.e[kb, h].astype(f32) * self.l[h, 0:1, :]
                ds = (p * (self.d[kb, h] - self.m[h, 0:1, :])).astype(bf16)
                dv += jnp.dot(p.astype(bf16), g_own[h], preferred_element_type=f32)
                dk += jnp.dot(ds, q_own[h], preferred_element_type=f32)
                self.dqt[hs, :] += jnp.dot(self.kt[kb, hs, :], ds, preferred_element_type=f32)
            self.dk[keys, :] = dk
            self.dv[keys, :] = dv

        self.sweep(low, high, back)
        att_ref[rows, :] = self.ot[...].T.astype(bf16)
        dq = self.dqt[...].T * HD**-0.5
        gp_ref[rows, :width] = turn(dq, self.tables, rows, -1.0).astype(bf16)

    def finish(self, gp_ref):
        width = self.width

        def block(i, _):
            sl = pl.ds(pl.multiple_of(i * QB, QB), QB)
            dk = turn(self.dk[sl, :], self.tables, sl, -1.0)
            gp_ref[sl, width : 2 * width] = dk.astype(jnp.bfloat16)
            gp_ref[sl, 2 * width :] = self.dv[sl, :].astype(jnp.bfloat16)
            return 0

        lax.fori_loop(0, LEN // QB, block, 0)


def attention_kernel(
    heads, first, start_ref, x_ref, g_ref, w_ref, doc_ref, rope_ref, *refs
):
    att_ref, gp_ref = refs[2:4]
    seq = pl.program_id(0) + first
    attend = Attention(heads, refs[4:])

    @pl.when(pl.program_id(0) == 0)
    def _():
        fill_tables(rope_ref, attend.tables)

    attend.begin(doc_ref, seq, start_ref[seq], x_ref, g_ref, w_ref)

    def query_block(i, _):
        attend.query_block(i, *attend.bounds(i), att_ref, gp_ref)
        return 0

    lax.fori_loop(0, LEN // QB, query_block, 0)
    attend.finish(gp_ref)


def attention(first, normed, grad, weights, image_start, doc_ids, earlier):
    rows, width = normed.shape[0], weights.shape[1] // 4
    count, heads = rows // LEN, width // HD
    bf16 = jnp.bfloat16
    seq_rows = lambda s, *_: (s + first, 0)
    fixed = lambda s, *_: (0, 0)
    return pl.pallas_call(
        functools.partial(attention_kernel, heads, first),
        out_shape=[jax.ShapeDtypeStruct(e.shape, bf16) for e in earlier],
        grid_spec=pltpu.PrefetchScalarGridSpec(
            num_scalar_prefetch=1,
            grid=(count - first,),
            in_specs=[
                pl.BlockSpec((LEN, D), seq_rows),
                pl.BlockSpec((LEN, D), seq_rows),
                pl.BlockSpec((D, 4 * width), fixed, pipeline_mode=pl.Buffered(1)),
                pl.BlockSpec((count, LEN), fixed),
                pl.BlockSpec((ROT, LEN), fixed),
                pl.BlockSpec(memory_space=pl.ANY),
                pl.BlockSpec(memory_space=pl.ANY),
            ],
            out_specs=[
                pl.BlockSpec((LEN, width), seq_rows),
                pl.BlockSpec((LEN, 3 * width), seq_rows),
            ],
            scratch_shapes=Attention.scratch(heads),
        ),
        input_output_aliases={6: 0, 7: 1},
        compiler_params=pltpu.CompilerParams(
            dimension_semantics=("arbitrary",), vmem_limit_bytes=56 << 20
        ),
        cost_estimate=pl.CostEstimate(
            flops=(count - first) * LEN * (36 * 640 * width + 8 * D * width),
            bytes_accessed=(count - first) * LEN * (width * 8 + 4 * D) + 8 * D * width,
            transcendentals=(count - first) * LEN * 640 * heads,
        ),
        name="attention",
    )(image_start, normed, grad, weights, doc_ids, jnp.asarray(rope_rows()), *earlier)


def ffn_kernel(x_ref, g_ref, wgu_ref, wd_ref, hidden_ref, gg_ref, gu_ref):
    f32, bf16 = jnp.float32, jnp.bfloat16
    x = x_ref[...]
    gate = lax.dot_general(x, wgu_ref[0], NT, preferred_element_type=f32)
    up = lax.dot_general(x, wgu_ref[1], NT, preferred_element_type=f32)
    grad = lax.dot_general(g_ref[...], wd_ref[...], NT, preferred_element_type=f32)
    sigma = jax.nn.sigmoid(gate)
    silu = gate * sigma
    hidden_ref[...] = (silu * up).astype(bf16)
    gg_ref[...] = (grad * up * (sigma + silu * (1.0 - sigma))).astype(bf16)
    gu_ref[...] = (grad * silu).astype(bf16)


def feed_forward(normed, grad, wgu, wd):
    rows, ffn = normed.shape[0], wd.shape[0]
    block = lambda i: (i, 0)
    return pl.pallas_call(
        ffn_kernel,
        out_shape=[jax.ShapeDtypeStruct((rows, ffn), jnp.bfloat16)] * 3,
        grid=(rows // MB,),
        in_specs=[
            pl.BlockSpec((MB, D), block),
            pl.BlockSpec((MB, D), block),
            pl.BlockSpec((2, ffn, D), lambda i: (0, 0, 0), pipeline_mode=pl.Buffered(1)),
            pl.BlockSpec((ffn, D), lambda i: (0, 0), pipeline_mode=pl.Buffered(1)),
        ],
        out_specs=[pl.BlockSpec((MB, ffn), block)] * 3,
        compiler_params=pltpu.CompilerParams(
            dimension_semantics=("arbitrary",), vmem_limit_bytes=56 << 20
        ),
        cost_estimate=pl.CostEstimate(
            flops=6 * rows * D * ffn,
            bytes_accessed=rows * (4 * D + 6 * ffn) + 6 * D * ffn,
            transcendentals=rows * ffn,
        ),
        name="feed_forward",
    )(normed, grad, wgu, wd)


def flip(index, bits):
    bit = 1
    while bit <= bits:
        if bits & bit:
            index = index + bit - 2 * bit * ((index // bit) % 2)
        bit *= 2
    return index


def chip_orders(ways):
    bits = [1 << k for k in range(1, ways.bit_length() - 1)]
    return bits, bits[::-1]


def held(bits):
    found = [0]
    for bit in bits:
        found += [o ^ bit for o in found]
    return found


def meet(peers):
    barrier = pltpu.get_barrier_semaphore()
    for peer in peers:
        pl.semaphore_signal(barrier, inc=1, device_id=peer, device_id_type=MESH)
    pl.semaphore_wait(barrier, len(peers))


def gather_kernel(ways, base, attended, count, *refs):
    f32, bf16 = jnp.float32, jnp.bfloat16
    me = lax.axis_index("col")
    if attended:
        (token_ref, cot_ref, vectors_ref, w_ref, rope_ref, doc_ref, image_ref, old_ref) = refs[:8]
        (old_normed, old_grad, normed_ref, full_ref, stat_ref, att_ref, gp_ref) = refs[8:15]
        refs = refs[15:]
    else:
        (token_ref, cot_ref, vector_ref, normed_ref, full_ref, stat_ref, vectors_ref) = refs[:7]
        refs = refs[7:]
    (both, load_sem, store_sem, full_sem, send_sem, recv_sem) = refs[:6]
    refs = refs[6:]
    width = token_ref.shape[1]
    rows = both.shape[1]
    pairs = rows // count
    orders = chip_orders(ways)
    phases = len(orders[0])
    mine = pl.ds(pl.multiple_of(me * width, width), width)
    source = pl.ds(base, rows)
    loads = [
        pltpu.make_async_copy(token_ref.at[source], both.at[me, :, pl.ds(0, width)], load_sem.at[0]),
        pltpu.make_async_copy(cot_ref.at[source], both.at[me, :, pl.ds(width, width)], load_sem.at[1]),
    ]
    for load in loads:
        load.start()
    peers = [flip(me, k) for k in range(1, ways)]
    if attended:
        meet([{"col": flip(me, 1 << k)} for k in range(ways.bit_length() - 1)])
    else:
        vectors_ref[:, mine] = vector_ref[...]
        meet([{"col": peer} for peer in peers])

    def vector_copy(k):
        return pltpu.make_async_remote_copy(
            src_ref=vectors_ref.at[:, mine],
            dst_ref=vectors_ref.at[:, mine],
            send_sem=refs[0].at[k],
            recv_sem=refs[1].at[k],
            device_id={"col": peers[k]},
            device_id_type=MESH,
        )

    def copies(p, phase):
        for k, order in enumerate(orders):
            bit = order[phase] if phase < phases else 1
            place = pl.ds(pl.multiple_of(p * count + k * (count // 2), count // 2), count // 2)
            for o in held(order[:phase]):
                index = k * ways + (o ^ bit)
                owner = flip(me, o)
                yield pltpu.make_async_remote_copy(
                    src_ref=both.at[owner, place],
                    dst_ref=both.at[owner, place],
                    send_sem=send_sem.at[p, index],
                    recv_sem=recv_sem.at[p, index],
                    device_id={"col": flip(me, bit)},
                    device_id_type=MESH,
                )

    def start(p, phase):
        for copy in copies(p, phase):
            copy.start()

    def arrive(p, phase):
        for copy in copies(p, phase):
            copy.wait_recv()

    def filed(p, first, out_ref, sem):
        place = pl.ds(pl.multiple_of(p * count, count), count)
        goal = pl.ds(pl.multiple_of(base + p * count, count), count)
        for b in range(ways):
            pltpu.make_async_copy(
                both.at[b, place, pl.ds(first, width)],
                out_ref.at[goal, pl.ds(b * width, width)],
                sem.at[p],
            ).start()

    def filed_wait(p, out_ref, sem):
        place = out_ref.at[pl.ds(base + p * count, count)]
        pltpu.make_async_copy(place, place, sem.at[p]).wait()

    def norm(p):
        filed(p, width, full_ref, full_sem)
        for phase in range(phases + 1):
            for copy in copies(p, phase):
                copy.wait_send()

        def block(j, _):
            at = pl.ds(pl.multiple_of(p * count + j * QB, QB), QB)
            goal = pl.ds(pl.multiple_of(base + p * count + j * QB, QB), QB)
            sums = sum(both[b, at, :width].astype(f32) for b in range(ways))
            mean = jnp.sum(sums, axis=1, keepdims=True) / D
            squares = jnp.zeros((QB, width), f32)
            for b in range(ways):
                x = both[b, at, :width].astype(f32) - mean
                squares += x * x
            inv = lax.rsqrt(jnp.sum(squares, axis=1, keepdims=True) / D + NORM_EPS)
            stat_ref[goal, :1] = mean
            stat_ref[goal, 1:] = inv
            for b in range(ways):
                cols = slice(b * width, (b + 1) * width)
                x = (both[b, at, :width].astype(f32) - mean) * inv
                x = x * vectors_ref[0:1, cols] + vectors_ref[1:2, cols]
                both[b, at, :width] = x.astype(bf16)
            return 0

        lax.fori_loop(0, count // QB, block, 0)
        filed(p, 0, normed_ref, store_sem)

    if attended:
        x_scr, g_scr, att_scr, gp_scr, in_sem, out_sem = refs[:6]
        attend = Attention(width // HD, refs[6:])
        stat_ref[pl.ds(0, base), :] = old_ref[pl.ds(0, base), :]

        def fetch(seq):
            place = pl.ds(pl.multiple_of(seq * LEN, LEN), LEN)
            return [
                pltpu.make_async_copy(old_normed.at[place], x_scr, in_sem.at[seq, 0]),
                pltpu.make_async_copy(old_grad.at[place], g_scr, in_sem.at[seq, 1]),
            ]

        def give(seq):
            place = pl.ds(pl.multiple_of(seq * LEN, LEN), LEN)
            return [
                pltpu.make_async_copy(att_scr.at[seq], att_ref.at[place], out_sem.at[seq, 0]),
                pltpu.make_async_copy(gp_scr.at[seq], gp_ref.at[place], out_sem.at[seq, 1]),
            ]

        for move in fetch(0):
            move.start()

    for load in loads:
        load.wait()
    start(0, 0)
    start(1, 0)
    if attended:
        fill_tables(rope_ref, attend.tables)
    else:
        for k in range(ways - 1):
            vector_copy(k).start()
        for k in range(ways - 1):
            vector_copy(k).wait_recv()
    blocks = LEN // QB
    turns = attended * blocks // pairs if attended else 0

    def step(p, _):
        for phase in range(phases):
            if phase or attended:
                arrive(p, phase)
                start(p, phase + 1)
            if phase == 0:
                if attended:
                    pl.when(p + 2 < pairs)(lambda: start(p + 2, 0))
                else:

                    @pl.when(p + 1 < pairs)
                    def _():
                        arrive(p + 1, 0)
                        start(p + 1, 1)

                    pl.when(p + 3 < pairs)(lambda: start(p + 3, 0))

                @pl.when(p >= 1)
                def _():
                    arrive(p - 1, phases)
                    norm(p - 1)

                if attended:
                    seq = p * turns // blocks
                    spot = p * turns % blocks

                    @pl.when(spot == 0)
                    def _():
                        for move in fetch(seq):
                            move.wait()
                        attend.begin(doc_ref, seq, image_ref[seq], x_scr, g_scr, w_ref)

                        @pl.when(seq + 1 < attended)
                        def _():
                            for move in fetch(seq + 1):
                                move.start()

                    def query_block(i, _):
                        low = i // (blocks - 1)
                        attend.query_block(i, low, i + 1 - low, att_scr.at[seq], gp_scr.at[seq])
                        return 0

                    lax.fori_loop(spot, spot + turns, query_block, 0)

                    @pl.when(spot + turns == blocks)
                    def _():
                        attend.finish(gp_scr.at[seq])
                        for move in give(seq):
                            move.start()
        return 0

    if not attended:
        arrive(0, 0)
        start(0, 1)
        start(2, 0)
    lax.fori_loop(0, pairs, step, 0)
    arrive(pairs - 1, phases)
    norm(pairs - 1)
    for p in range(pairs):
        filed_wait(p, full_ref, full_sem)
        filed_wait(p, normed_ref, store_sem)
    if attended:
        for seq in range(attended):
            for move in give(seq):
                move.wait()
    else:
        for k in range(ways - 1):
            vector_copy(k).wait_send()


def gather_scratch(ways, rows, width, count):
    dma = pltpu.SemaphoreType.DMA
    pairs = rows // count
    return [
        pltpu.VMEM((ways, rows, 2 * width), jnp.bfloat16),
        dma((2,)),
        dma((pairs,)),
        dma((pairs,)),
        dma((pairs, 2 * ways)),
        dma((pairs, 2 * ways)),
    ]


def gather_first(tokens, out_grad, vectors, count, ways):
    rows, width = tokens.shape
    bf16, f32 = jnp.bfloat16, jnp.float32
    anywhere = pl.BlockSpec(memory_space=pl.ANY)
    vmem = pl.BlockSpec(memory_space=pltpu.VMEM)
    dma = pltpu.SemaphoreType.DMA
    return pl.pallas_call(
        functools.partial(gather_kernel, ways, 0, 0, GB),
        out_shape=[
            jax.ShapeDtypeStruct((rows, D), bf16),
            jax.ShapeDtypeStruct((rows, D), bf16),
            jax.ShapeDtypeStruct((rows, 2), f32),
            jax.ShapeDtypeStruct((8, D), f32),
        ],
        in_specs=[anywhere, anywhere, vmem],
        out_specs=[anywhere, anywhere, vmem, vmem],
        scratch_shapes=[*gather_scratch(ways, count, width, GB), dma((ways - 1,)), dma((ways - 1,))],
        compiler_params=pltpu.CompilerParams(
            collective_id=0, has_side_effects=True, vmem_limit_bytes=63 << 20
        ),
        cost_estimate=pl.CostEstimate(
            flops=100 * count * D * D // ways, bytes_accessed=count * D * 8, transcendentals=0
        ),
        name="gather_first",
    )(tokens, out_grad, vectors)


def gather_rest(tokens, out_grad, vectors, weights, doc_ids, image_start, stats, normed, grad, ways):
    rows, width = tokens.shape
    count = rows // 2
    bf16, f32 = jnp.bfloat16, jnp.float32
    anywhere = pl.BlockSpec(memory_space=pl.ANY)
    vmem = pl.BlockSpec(memory_space=pltpu.VMEM)
    dma = pltpu.SemaphoreType.DMA
    seqs = count // LEN
    return pl.pallas_call(
        functools.partial(gather_kernel, ways, count, seqs, GA),
        out_shape=[
            jax.ShapeDtypeStruct((rows, D), bf16),
            jax.ShapeDtypeStruct((rows, D), bf16),
            jax.ShapeDtypeStruct((rows, 2), f32),
            jax.ShapeDtypeStruct((rows, width), bf16),
            jax.ShapeDtypeStruct((rows, 3 * width), bf16),
        ],
        in_specs=[
            anywhere,
            anywhere,
            vmem,
            vmem,
            vmem,
            vmem,
            pl.BlockSpec(memory_space=pltpu.SMEM),
            vmem,
            anywhere,
            anywhere,
        ],
        out_specs=[anywhere, anywhere, vmem, anywhere, anywhere],
        input_output_aliases={8: 0, 9: 1},
        scratch_shapes=[
            *gather_scratch(ways, rows - count, width, GA),
            pltpu.VMEM((LEN, D), bf16),
            pltpu.VMEM((LEN, D), bf16),
            pltpu.VMEM((seqs, LEN, width), bf16),
            pltpu.VMEM((seqs, LEN, 3 * width), bf16),
            dma((seqs, 2)),
            dma((seqs, 2)),
            *Attention.scratch(width // HD),
        ],
        compiler_params=pltpu.CompilerParams(
            collective_id=3, has_side_effects=True, vmem_limit_bytes=63 << 20
        ),
        cost_estimate=pl.CostEstimate(
            flops=100 * count * D * D // ways, bytes_accessed=count * D * 8, transcendentals=0
        ),
        name="gather_rest",
    )(tokens, out_grad, vectors, weights, jnp.asarray(rope_rows()), doc_ids, image_start, stats, normed, grad)


class Reducer:
    def __init__(self, ways, parts, inbox, send_sem, recv_sem):
        self.ways, self.parts, self.inbox = ways, parts, inbox
        self.send_sem, self.recv_sem = send_sem, recv_sem
        self.me = lax.axis_index("col")
        self.orders = chip_orders(ways)
        self.phases = 1 + len(self.orders[0])

    def moves(self, step, phase):
        halves = [None] if phase == 0 else [0, 1]
        for k in halves:
            order = [1] if phase == 0 else [1, *self.orders[k]]
            bit = order[phase]
            done = sum(order[:phase])
            count = RB if k is None else RB // 2
            rows = pl.ds(pl.multiple_of(step * RB + (k or 0) * count, count), count)
            for o in range(self.ways):
                if o & done or not o & bit:
                    continue
                goal = o ^ bit
                slot = slot_of(self.ways, self.orders, phase, k, goal)
                sem = 2 * slot + (k or 0)
                copy = pltpu.make_async_remote_copy(
                    src_ref=self.parts.at[o, rows],
                    dst_ref=self.inbox.at[slot, rows],
                    send_sem=self.send_sem.at[step, sem],
                    recv_sem=self.recv_sem.at[step, sem],
                    device_id={"col": flip(self.me, bit)},
                    device_id_type=MESH,
                )
                yield copy, goal, slot, rows

    def send(self, step, phase):
        for copy, *_ in self.moves(step, phase):
            copy.start()

    def absorb(self, step, phase):
        out = []
        for copy, goal, slot, rows in self.moves(step, phase):
            copy.wait_recv()
            value = self.parts[goal, rows, :].astype(jnp.float32)
            value += self.inbox[slot, rows, :].astype(jnp.float32)
            if phase == self.phases - 1:
                out.append(value)
            else:
                self.parts[goal, rows, :] = value.astype(jnp.bfloat16)
        return out

    def finish(self, step):
        for phase in range(self.phases):
            for copy, *_ in self.moves(step, phase):
                copy.wait_send()

    def advance(self, t, steps, lags):
        pl.when(t < steps)(lambda: self.send(t, 0))
        for phase in range(self.phases - 1):
            s = t - lags[phase]

            @pl.when((s >= 0) & (s < steps))
            def _():
                self.absorb(s, phase)
                self.send(s, phase + 1)


def slot_of(ways, orders, phase, half, goal):
    if phase == 0:
        return goal // 2
    order = [1, *orders[half]]
    base = ways // 2
    for p in range(1, phase):
        base += ways >> (p + 1)
    goals = [g for g in range(ways) if not g & sum(order[: phase + 1])]
    return base + goals.index(goal)


def lags_of(ways):
    return [1 + 2 * p for p in range(len(chip_orders(ways)[0]) + 1)]


def reducer_scratch(ways, rows, width):
    steps = rows // RB
    return [
        pltpu.VMEM((ways, rows, width), jnp.bfloat16),
        pltpu.VMEM((ways - 1, rows, width), jnp.bfloat16),
        pltpu.SemaphoreType.DMA((steps, 2 * ways)),
        pltpu.SemaphoreType.DMA((steps, 2 * ways)),
    ]


def branch_kernel(
    ways,
    steps,
    att_ref,
    hidden_ref,
    grad_ref,
    token_ref,
    wout_ref,
    wd_ref,
    out_ref,
    wgrad_ref,
    parts,
    inbox,
    send_sem,
    recv_sem,
    acc,
    acc_out,
):
    f32, bf16 = jnp.float32, jnp.bfloat16
    t = pl.program_id(0)
    me, width = lax.axis_index("col"), D // ways
    lags = lags_of(ways)
    ring = Reducer(ways, parts, inbox, send_sem, recv_sem)

    @pl.when(t == 0)
    def _():
        acc[...] = jnp.zeros_like(acc)
        acc_out[...] = jnp.zeros_like(acc_out)
        meet([{"col": flip(me, 1 << k)} for k in range(ways.bit_length() - 1)])

    @pl.when(t < steps)
    def _():
        rows = pl.ds(pl.multiple_of(t * RB, RB), RB)
        att, hidden = att_ref[...], hidden_ref[...]
        for o in range(ways):
            cols = pl.ds(pl.multiple_of(flip(me, o) * width, width), width)
            total = lax.dot_general(att, wout_ref[cols, :], NT, preferred_element_type=f32)
            total += jnp.dot(hidden, wd_ref[:, cols], preferred_element_type=f32)
            parts[o, rows, :] = total.astype(bf16)

    ring.advance(t, steps, lags)

    @pl.when(t < steps)
    def _():
        acc[...] += contract(hidden_ref[...], grad_ref[...], 0, 0)
        acc_out[...] += contract(att_ref[...], grad_ref[...], 0, 0)

    @pl.when(t == steps)
    def _():
        ffn = acc.shape[0]
        wgrad_ref[:ffn, :] = acc[...].astype(bf16)
        wgrad_ref[ffn:, :] = acc_out[...].astype(bf16)

    s = t - lags[-1]

    @pl.when(s >= 0)
    def _():
        for k, value in enumerate(ring.absorb(s, ring.phases - 1)):
            half = slice(k * (RB // 2), (k + 1) * (RB // 2))
            out_ref[half, :] = (token_ref[half, :].astype(f32) + value).astype(bf16)
        ring.finish(s)


def branches(att, hidden, grad, tokens, weights, wd, ways):
    rows, width = tokens.shape
    ffn = wd.shape[0]
    steps = rows // RB
    lag = lags_of(ways)[-1]
    now = lambda t: (jnp.minimum(t, steps - 1), 0)
    late = lambda t: (jnp.maximum(t - lag, 0), 0)
    fixed = lambda t: (0, 0)
    once = pl.Buffered(1)
    return pl.pallas_call(
        functools.partial(branch_kernel, ways, steps),
        out_shape=[
            jax.ShapeDtypeStruct((rows, width), jnp.bfloat16),
            jax.ShapeDtypeStruct((ffn + width, D), jnp.bfloat16),
        ],
        grid=(steps + lag,),
        in_specs=[
            pl.BlockSpec((RB, width), now),
            pl.BlockSpec((RB, ffn), now),
            pl.BlockSpec((RB, D), now),
            pl.BlockSpec((RB, width), late),
            pl.BlockSpec((D, width), lambda t: (0, 3), pipeline_mode=once),
            pl.BlockSpec((ffn, D), fixed, pipeline_mode=once),
        ],
        out_specs=[
            pl.BlockSpec((RB, width), late),
            pl.BlockSpec((ffn + width, D), fixed, pipeline_mode=once),
        ],
        scratch_shapes=[
            *reducer_scratch(ways, rows, width),
            pltpu.VMEM((ffn, D), jnp.float32),
            pltpu.VMEM((width, D), jnp.float32),
        ],
        compiler_params=pltpu.CompilerParams(
            collective_id=1,
            has_side_effects=True,
            dimension_semantics=("arbitrary",),
            vmem_limit_bytes=60 << 20,
        ),
        cost_estimate=pl.CostEstimate(
            flops=8 * rows * D * (2 * ffn + width), bytes_accessed=4 * rows * D, transcendentals=0
        ),
        name="branches",
    )(att, hidden, grad, tokens, weights, wd)


def back_kernel(
    ways,
    lines,
    steps,
    gp_ref,
    gg_ref,
    gu_ref,
    x_ref,
    token_ref,
    cot_ref,
    stat_ref,
    w_ref,
    wgu_ref,
    vectors_ref,
    gain_ref,
    wqkv_ref,
    out_ref,
    vgrad_ref,
    qkv_ref,
    parts,
    inbox,
    send_sem,
    recv_sem,
    sums,
    ssend_sem,
    srecv_sem,
    acc,
    vsend_sem,
    vrecv_sem,
):
    f32, bf16 = jnp.float32, jnp.bfloat16
    t = pl.program_id(0)
    me, width = lax.axis_index("col"), D // ways
    line = lax.axis_index("row")
    lags = lags_of(ways)
    ring = Reducer(ways, parts, inbox, send_sem, recv_sem)

    @pl.when(t == 0)
    def _():
        acc[...] = jnp.zeros_like(acc)
        meet(
            [{"col": flip(me, k)} for k in range(1, ways)]
            + [{"row": (line + k) % lines} for k in range(1, lines)]
        )

    def sum_copies(group):
        rows = pl.ds(pl.multiple_of(group * RB, RB), RB)
        for k in range(1, ways):
            yield pltpu.make_async_remote_copy(
                src_ref=sums.at[0, :, rows],
                dst_ref=sums.at[k, :, rows],
                send_sem=ssend_sem.at[group, k - 1],
                recv_sem=srecv_sem.at[group, k - 1],
                device_id={"col": flip(me, k)},
                device_id_type=MESH,
            )

    @pl.when(t < steps)
    def _():
        rows = pl.ds(pl.multiple_of(t * RB, RB), RB)
        gp, gg, gu = gp_ref[...], gg_ref[...], gu_ref[...]
        plain = jnp.zeros((RB, 1), f32)
        cross = jnp.zeros((RB, 1), f32)
        for o in range(ways):
            cols = pl.ds(pl.multiple_of(flip(me, o) * width, width), width)
            total = jnp.dot(gg, wgu_ref[0, :, cols], preferred_element_type=f32)
            total += jnp.dot(gu, wgu_ref[1, :, cols], preferred_element_type=f32)
            total += lax.dot_general(gp, w_ref[cols, :], NT, preferred_element_type=f32)
            parts[o, rows, :] = total.astype(bf16)
            scaled = x_ref[:, cols].astype(f32) - vectors_ref[1:2, cols]
            plain += jnp.sum(total * vectors_ref[0:1, cols], axis=1, keepdims=True)
            cross += jnp.sum(total * scaled, axis=1, keepdims=True)
        lane = lax.broadcasted_iota(jnp.int32, (RB, 128), 1)
        spot = 2 * (t % SUMS)
        pair = jnp.where(lane == spot, plain, jnp.where(lane == spot + 1, cross, 0.0))
        group = pl.ds(pl.multiple_of(t // SUMS * RB, RB), RB)
        before = jnp.where(jnp.broadcast_to(spot == 0, (8, RB)), 0.0, sums[0, :, group])
        sums[0, :, group] = before + pair.T[:8]
        for kind in range(3):
            qkv_ref[kind] = wqkv_ref[:, kind * width : (kind + 1) * width].astype(f32)

        @pl.when(t % SUMS == SUMS - 1)
        def _():
            for copy in sum_copies(t // SUMS):
                copy.start()

    ring.advance(t, steps, lags)
    s = t - lags[-1]

    @pl.when(s >= 0)
    def _():
        @pl.when(s % SUMS == 0)
        def _():
            for copy in sum_copies(s // SUMS):
                copy.wait_recv()

        group = pl.ds(pl.multiple_of(s // SUMS * RB, RB), RB)
        both = sum(sums[k, :, group] for k in range(ways)).T
        lane = lax.broadcasted_iota(jnp.int32, (RB, 8), 1)
        spot = 2 * (s % SUMS)
        plain = jnp.sum(jnp.where(lane == spot, both, 0.0), axis=1, keepdims=True) / D
        cross = jnp.sum(jnp.where(lane == spot + 1, both, 0.0), axis=1, keepdims=True) / D
        for k, value in enumerate(ring.absorb(s, ring.phases - 1)):
            half = slice(k * (RB // 2), (k + 1) * (RB // 2))
            inv = stat_ref[half, 1:]
            unit = (token_ref[half, :].astype(f32) - stat_ref[half, :1]) * inv
            scaled = value * gain_ref[0:1, :]
            out_ref[half, :] = cot_ref[half, :].astype(f32) + inv * (
                scaled - plain[half] - unit * cross[half]
            )
            acc[0, 0:1, :] += jnp.sum(value * unit, axis=0, keepdims=True)
            acc[0, 1:2, :] += jnp.sum(value, axis=0, keepdims=True)

        @pl.when(s % SUMS == 0)
        def _():
            for copy in sum_copies(s // SUMS):
                copy.wait_send()

        ring.finish(s)

    @pl.when(t == pl.num_programs(0) - 1)
    def _():
        copies = [
            pltpu.make_async_remote_copy(
                src_ref=acc.at[0],
                dst_ref=acc.at[k],
                send_sem=vsend_sem.at[k - 1],
                recv_sem=vrecv_sem.at[k - 1],
                device_id={"row": (line + k) % lines},
                device_id_type=MESH,
            )
            for k in range(1, lines)
        ]
        for copy in copies:
            copy.start()
        for copy in copies:
            copy.wait()
        vgrad_ref[...] = sum(acc[k] for k in range(lines))


def norm_back(
    gp, gg, gu, normed, tokens, cot, stats, weights, wgu, vectors, own, qkv, ways, lines
):
    rows, width = tokens.shape
    ffn = gg.shape[1]
    steps = rows // RB
    lag = lags_of(ways)[-1]
    deep = qkv.shape[0]
    slab = deep // steps
    now = lambda t: (jnp.minimum(t, steps - 1), 0)
    late = lambda t: (jnp.maximum(t - lag, 0), 0)
    fixed = lambda t: (0, 0)
    once = pl.Buffered(1)
    dma = pltpu.SemaphoreType.DMA
    return pl.pallas_call(
        functools.partial(back_kernel, ways, lines, steps),
        out_shape=[
            jax.ShapeDtypeStruct((rows, width), jnp.float32),
            jax.ShapeDtypeStruct((8, width), jnp.float32),
            jax.ShapeDtypeStruct((3, deep, width), jnp.float32),
        ],
        grid=(steps + lag,),
        in_specs=[
            pl.BlockSpec((RB, 3 * width), now),
            pl.BlockSpec((RB, ffn), now),
            pl.BlockSpec((RB, ffn), now),
            pl.BlockSpec((RB, D), now),
            pl.BlockSpec((RB, width), late),
            pl.BlockSpec((RB, width), late),
            pl.BlockSpec((RB, 2), late),
            pl.BlockSpec((D, 3 * width), fixed, pipeline_mode=once),
            pl.BlockSpec((2, ffn, D), lambda t: (0, 0, 0), pipeline_mode=once),
            pl.BlockSpec((8, D), fixed),
            pl.BlockSpec((8, width), fixed),
            pl.BlockSpec((slab, 3 * width), now),
        ],
        out_specs=[
            pl.BlockSpec((RB, width), late),
            pl.BlockSpec((8, width), fixed),
            pl.BlockSpec((3, slab, width), lambda t: (0, jnp.minimum(t, steps - 1), 0)),
        ],
        scratch_shapes=[
            *reducer_scratch(ways, rows, width),
            pltpu.VMEM((ways, 8, rows // SUMS), jnp.float32),
            dma((steps // SUMS, ways - 1)),
            dma((steps // SUMS, ways - 1)),
            pltpu.VMEM((lines, 8, width), jnp.float32),
            dma((lines - 1,)),
            dma((lines - 1,)),
        ],
        compiler_params=pltpu.CompilerParams(
            collective_id=2,
            has_side_effects=True,
            dimension_semantics=("arbitrary",),
            vmem_limit_bytes=61 << 20,
        ),
        cost_estimate=pl.CostEstimate(
            flops=4 * rows * D * (2 * ffn + 3 * width), bytes_accessed=6 * rows * D, transcendentals=0
        ),
        name="norm_back",
    )(gp, gg, gu, normed, tokens, cot, stats, weights, wgu, vectors, own, qkv)


def after(value, *others):
    return lax.optimization_barrier((value, others))[0]


def local(
    tokens,
    norm_gain,
    norm_bias,
    qkv_weight,
    gate_up_weight,
    out_weight,
    down_weight,
    image_start,
    doc_ids,
    out_grad,
):
    f32, bf16 = jnp.float32, jnp.bfloat16
    block_rows, width = tokens.shape
    ways = D // width
    lines = D // qkv_weight.shape[0]

    own = jnp.concatenate([qkv_weight[:, k] for k in range(3)] + [out_weight], axis=1)
    weights = lax.all_gather(own, "row", axis=0, tiled=True)
    full_gate_up = lax.all_gather(gate_up_weight, "row", axis=0, tiled=True)
    full_down = lax.all_gather(down_weight, "row", axis=0, tiled=True)
    wgu = jnp.transpose(full_gate_up, (1, 2, 0))
    wd = jnp.transpose(full_down, (1, 0))
    own_vectors = jnp.pad(jnp.stack([norm_gain, norm_bias]), ((0, 6), (0, 0)))

    half = block_rows // 2
    normed, grad, stats, vectors = gather_first(tokens, out_grad, own_vectors, half, ways)
    normed, grad, stats, *earlier = gather_rest(
        tokens, out_grad, vectors, weights, doc_ids, image_start, stats, normed, grad, ways
    )
    attended, grad_projected = attention(
        half // LEN, normed, grad, weights, image_start, doc_ids, earlier
    )

    def weight_sum(grad):
        return lax.psum_scatter(grad, "row", scatter_dimension=0, tiled=True)

    def weight_grad(left, right):
        return contract(left, right, 0, 0).astype(bf16)

    grad_qkv = weight_grad(normed, grad_projected)
    hidden, grad_gate, grad_up = feed_forward(after(normed, grad_qkv), grad, wgu, wd)
    weight_gate = weight_grad(normed, grad_gate)
    weight_up = weight_grad(normed, after(grad_up, weight_gate))
    qkv_sum = weight_sum(grad_qkv)
    gate_sum = weight_sum(weight_gate)
    outputs, weight_rest = branches(
        after(attended, weight_up, qkv_sum), hidden, grad, tokens, weights, wd, ways
    )
    input_grad, vector_grads, qkv_sum = norm_back(
        after(grad_projected, outputs, gate_sum),
        grad_gate,
        grad_up,
        normed,
        tokens,
        out_grad,
        stats,
        weights,
        wgu,
        vectors,
        own_vectors,
        qkv_sum,
        ways,
        lines,
    )
    qkv_sum = jnp.transpose(qkv_sum, (1, 0, 2))
    up_sum = after(weight_sum(weight_up), input_grad)
    rest = weight_sum(jnp.transpose(weight_rest, (1, 0))).astype(f32)
    down_sum, out_sum = rest[:, :-width], rest[:, -width:]
    gate_up_sum = jnp.stack([gate_sum.astype(f32), up_sum.astype(f32)], axis=1)
    return (
        outputs,
        input_grad,
        vector_grads[0],
        vector_grads[1],
        qkv_sum,
        gate_up_sum,
        out_sum,
        down_sum,
    )


def solution(mesh):
    placed = (
        P("row", "col"),
        P("col"),
        P("col"),
        P("row", None, "col"),
        P("row", None, "col"),
        P("row", "col"),
        P("row", "col"),
        P("row"),
        P("row", None),
        P("row", "col"),
    )
    return jax.shard_map(
        local,
        mesh=mesh,
        in_specs=placed,
        out_specs=(
            P("row", "col"),
            P("row", "col"),
            P("col"),
            P("col"),
            P("row", None, "col"),
            P("row", None, "col"),
            P("row", "col"),
            P("row", "col"),
        ),
        check_vma=False,
    )
```

```python
import functools

import jax
import jax.numpy as jnp
import numpy as np
from jax import lax
from jax.experimental import pallas as pl
from jax.experimental.pallas import tpu as pltpu
from jax.sharding import PartitionSpec as P

D = 2048
HD = 64
ROT = 16
LEN = 1024
IMG = 256
QB = 256
MB = 256
RB = 256
GB = 256
GA = 256
SUMS = 4


NORM_EPS = 1e-05
MESH = pl.DeviceIdType.MESH
MASKED_SCORE = -1e30
ROPE_BASE = 10000.0
NT = (((1,), (1,)), ((), ()))


def contract(left, right, left_dim, right_dim):
    return lax.dot_general(
        left, right, (((left_dim,), (right_dim,)), ((), ())), preferred_element_type=jnp.float32
    )


def rope_rows():
    half = ROT // 2
    inv_freq = np.float32(ROPE_BASE) ** (np.float32(-2.0 / ROT) * np.arange(half, dtype=np.float32))
    angles = np.arange(LEN, dtype=np.float32)[None, :] * inv_freq[:, None]
    wide = angles.astype(np.float64)
    return np.concatenate([np.cos(wide), np.sin(wide)]).astype(np.float32)


def fill_tables(rows_ref, tables):
    half = ROT // 2
    for i in range(LEN // QB):
        sl = pl.ds(i * QB, QB)
        cosines, sines = rows_ref[:half, sl], rows_ref[half:, sl]
        zero = jnp.zeros_like(sines)
        rest = [zero] * (HD // half - 2)
        ones = [jnp.ones_like(sines)] * (HD // half - 2)
        tables[0, sl, :] = jnp.concatenate([cosines, cosines, *ones] * (128 // HD), axis=0).T
        tables[1, sl, :] = jnp.concatenate([-sines, zero, *rest] * (128 // HD), axis=0).T
        tables[2, sl, :] = jnp.concatenate([zero, sines, *rest] * (128 // HD), axis=0).T


def turn(x, tables, sl, sign):
    width = x.shape[1]
    c, a, b = (jnp.concatenate([tables[k, sl, :]] * (width // 128), axis=1) for k in range(3))
    left = pltpu.roll(x, width - ROT // 2, 1)
    right = pltpu.roll(x, ROT // 2, 1)
    return x * c + (left * a + right * b) * sign


class Attention:
    def __init__(self, heads, scratch):
        self.heads, self.width = heads, heads * HD
        (
            self.tables,
            self.span,
            self.data,
            self.kt,
            self.vt,
            self.s,
            self.d,
            self.e,
            self.bias,
            self.m,
            self.l,
            self.ot,
            self.dqt,
            self.dk,
            self.dv,
        ) = scratch

    @staticmethod
    def scratch(heads):
        f32, bf16, blocks, width = jnp.float32, jnp.bfloat16, LEN // QB, heads * HD
        return [
            pltpu.VMEM((3, LEN, 128), f32),
            pltpu.VMEM((blocks, 8, QB), jnp.int32),
            pltpu.VMEM((LEN, 4 * width), bf16),
            pltpu.VMEM((blocks, width, QB), bf16),
            pltpu.VMEM((blocks, width, QB), bf16),
            pltpu.VMEM((blocks, heads, QB, QB), f32),
            pltpu.VMEM((blocks, heads, QB, QB), f32),
            pltpu.VMEM((blocks, heads, QB, QB), bf16),
            pltpu.VMEM((2, QB, QB), f32),
            pltpu.VMEM((heads, 8, QB), f32),
            pltpu.VMEM((heads, 8, QB), f32),
            pltpu.VMEM((width, QB), f32),
            pltpu.VMEM((width, QB), f32),
            pltpu.VMEM((LEN, width), f32),
            pltpu.VMEM((LEN, width), f32),
        ]

    def part(self, kind):
        return pl.ds(kind * self.width, self.width)

    def begin(self, doc_ref, seq, start, x_ref, g_ref, w_ref, arrive=None):
        f32, bf16, width = jnp.float32, jnp.bfloat16, self.width
        docs = doc_ref[pl.ds(seq, 1), :].astype(f32)
        down = jnp.broadcast_to(docs, (128, LEN)).T[:, :1]
        for i in range(LEN // QB):
            own = docs[:, i * QB : (i + 1) * QB]
            first = jnp.sum((down < own).astype(jnp.int32), axis=0, keepdims=True)
            last = jnp.sum((down <= own).astype(jnp.int32), axis=0, keepdims=True) - 1
            at = lax.broadcasted_iota(jnp.int32, (1, QB), 1) + i * QB
            inside = (at >= start) & (at < start + IMG)
            self.span[i, 0:1, :] = first
            self.span[i, 1:2, :] = jnp.where(inside, jnp.minimum(last, start + IMG - 1), at)

        def block(i, _):
            sl = pl.ds(pl.multiple_of(i * QB, QB), QB)
            if arrive:
                arrive(i)
            x = x_ref[sl, :]
            q = jnp.dot(x, w_ref[:, :width], preferred_element_type=f32)
            k = jnp.dot(x, w_ref[:, width : 2 * width], preferred_element_type=f32)
            v = jnp.dot(x, w_ref[:, 2 * width : 3 * width], preferred_element_type=f32)
            g = jnp.dot(g_ref[sl, :], w_ref[:, 3 * width :], preferred_element_type=f32)
            q = turn(q, self.tables, sl, 1.0).astype(bf16).astype(f32) * HD**-0.5
            k = turn(k, self.tables, sl, 1.0).astype(bf16)
            self.data[sl, self.part(0)] = q.astype(bf16)
            self.data[sl, self.part(1)] = k
            self.data[sl, self.part(2)] = v.astype(bf16)
            self.data[sl, self.part(3)] = g.astype(bf16)
            self.kt[i] = k.astype(f32).T.astype(bf16)
            self.vt[i] = v.T.astype(bf16)
            return 0

        lax.fori_loop(0, LEN // QB, block, 0)
        self.dk[...] = jnp.zeros_like(self.dk)
        self.dv[...] = jnp.zeros_like(self.dv)

    def bounds(self, i):
        return jnp.min(self.span[i, 0:1, :]) // QB, jnp.max(self.span[i, 1:2, :]) // QB

    @staticmethod
    def sweep(low, high, body):
        def two(j, _):
            body(low + 2 * j)
            body(low + 2 * j + 1)
            return 0

        count = high + 1 - low
        lax.fori_loop(0, count // 2, two, 0)
        pl.when(count % 2 == 1)(lambda: body(high))

    def query_block(self, i, low, high, att_ref, gp_ref):
        f32, bf16, heads, width = jnp.float32, jnp.bfloat16, self.heads, self.width
        rows = pl.ds(pl.multiple_of(i * QB, QB), QB)
        lane = lax.broadcasted_iota(jnp.int32, (1, width), 1) // HD
        first, final = self.span[i, 0:1, :], self.span[i, 1:2, :]
        q, g = self.data[rows, self.part(0)], self.data[rows, self.part(3)]
        zero = jnp.zeros_like(q)
        q_own = [jnp.where(lane == h, q, zero) for h in range(heads)]
        g_own = [jnp.where(lane == h, g, zero) for h in range(heads)]
        self.m[...] = jnp.full_like(self.m, MASKED_SCORE)

        def fold(x, op):
            runs = [x[r : r + 8] for r in range(0, QB, 8)]
            lanes = runs[:8]
            for r, run in enumerate(runs[8:]):
                lanes[r % 8] = op(lanes[r % 8], run)
            while len(lanes) > 1:
                lanes = [op(a, b) for a, b in zip(lanes[::2], lanes[1::2])]
            return lanes[0]

        def score(kb):
            keys = pl.ds(pl.multiple_of(kb * QB, QB), QB)
            k, v = self.data[keys, self.part(1)], self.data[keys, self.part(2)]
            at = lax.broadcasted_iota(jnp.int32, (QB, QB), 0) + kb * QB
            bias = jnp.where((at >= first) & (at <= final), 0.0, MASKED_SCORE)
            self.bias[kb % 2] = bias
            for h in range(heads):
                s = lax.dot_general(k, q_own[h], NT, preferred_element_type=f32) + self.bias[kb % 2]
                self.s[kb, h] = s
                self.m[h] = jnp.maximum(self.m[h], fold(s, jnp.maximum))
                self.d[kb, h] = lax.dot_general(v, g_own[h], NT, preferred_element_type=f32)

        self.sweep(low, high, score)
        for h in range(heads):
            self.m[h] = jnp.broadcast_to(jnp.max(self.m[h], axis=0, keepdims=True), (8, QB))
        self.l[...] = jnp.zeros_like(self.l)
        self.ot[...] = jnp.zeros_like(self.ot)
        self.dqt[...] = jnp.zeros_like(self.dqt)

        def expo(kb):
            for h in range(heads):
                hs = slice(h * HD, (h + 1) * HD)
                e = jnp.exp(self.s[kb, h] - self.m[h, 0:1, :])
                self.l[h] += fold(e, jnp.add)
                e = e.astype(bf16)
                self.e[kb, h] = e
                self.ot[hs, :] += jnp.dot(self.vt[kb, hs, :], e, preferred_element_type=f32)

        self.sweep(low, high, expo)
        gt = g.astype(f32).T
        for h in range(heads):
            hs = slice(h * HD, (h + 1) * HD)
            inv = 1.0 / jnp.sum(self.l[h], axis=0, keepdims=True)
            self.l[h] = jnp.broadcast_to(inv, (8, QB))
            out = self.ot[hs, :] * inv
            self.ot[hs, :] = out
            delta = jnp.sum(out * gt[hs], axis=0, keepdims=True)
            self.m[h] = jnp.broadcast_to(delta, (8, QB))

        def back(kb):
            keys = pl.ds(pl.multiple_of(kb * QB, QB), QB)
            dk = self.dk[keys, :]
            dv = self.dv[keys, :]
            for h in range(heads):
                hs = slice(h * HD, (h + 1) * HD)
                p = self.e[kb, h].astype(f32) * self.l[h, 0:1, :]
                ds = (p * (self.d[kb, h] - self.m[h, 0:1, :])).astype(bf16)
                dv += jnp.dot(p.astype(bf16), g_own[h], preferred_element_type=f32)
                dk += jnp.dot(ds, q_own[h], preferred_element_type=f32)
                self.dqt[hs, :] += jnp.dot(self.kt[kb, hs, :], ds, preferred_element_type=f32)
            self.dk[keys, :] = dk
            self.dv[keys, :] = dv

        self.sweep(low, high, back)
        att_ref[rows, :] = self.ot[...].T.astype(bf16)
        dq = self.dqt[...].T * HD**-0.5
        gp_ref[rows, :width] = turn(dq, self.tables, rows, -1.0).astype(bf16)

    def finish(self, gp_ref):
        width = self.width

        def block(i, _):
            sl = pl.ds(pl.multiple_of(i * QB, QB), QB)
            dk = turn(self.dk[sl, :], self.tables, sl, -1.0)
            gp_ref[sl, width : 2 * width] = dk.astype(jnp.bfloat16)
            gp_ref[sl, 2 * width :] = self.dv[sl, :].astype(jnp.bfloat16)
            return 0

        lax.fori_loop(0, LEN // QB, block, 0)


def attention_kernel(
    heads, first, start_ref, x_ref, g_ref, w_ref, doc_ref, rope_ref, *refs
):
    att_ref, gp_ref, x_scr, g_scr, sem = refs[2:7]
    seq = pl.program_id(0) + first
    attend = Attention(heads, refs[7:])

    def fetch(seq, i):
        here = pl.ds(pl.multiple_of(i * QB, QB), QB)
        there = pl.ds(pl.multiple_of(seq * LEN + i * QB, QB), QB)
        return [
            pltpu.make_async_copy(x_ref.at[there], x_scr.at[here], sem.at[0, i]),
            pltpu.make_async_copy(g_ref.at[there], g_scr.at[here], sem.at[1, i]),
        ]

    def fetch_all(seq):
        for i in range(LEN // QB):
            for move in fetch(seq, i):
                move.start()

    def arrive(i):
        for move in fetch(seq, i):
            move.wait()

    @pl.when(pl.program_id(0) == 0)
    def _():
        fetch_all(seq)
        fill_tables(rope_ref, attend.tables)

    attend.begin(doc_ref, seq, start_ref[seq], x_scr, g_scr, w_ref, arrive)
    pl.when(pl.program_id(0) + 1 < pl.num_programs(0))(lambda: fetch_all(seq + 1))

    def query_block(i, _):
        attend.query_block(i, *attend.bounds(i), att_ref, gp_ref)
        return 0

    lax.fori_loop(0, LEN // QB, query_block, 0)
    attend.finish(gp_ref)


def attention(first, normed, grad, weights, image_start, doc_ids, earlier):
    rows, width = normed.shape[0], weights.shape[1] // 4
    count, heads = rows // LEN, width // HD
    bf16 = jnp.bfloat16
    seq_rows = lambda s, *_: (s + first, 0)
    fixed = lambda s, *_: (0, 0)
    return pl.pallas_call(
        functools.partial(attention_kernel, heads, first),
        out_shape=[jax.ShapeDtypeStruct(e.shape, bf16) for e in earlier],
        grid_spec=pltpu.PrefetchScalarGridSpec(
            num_scalar_prefetch=1,
            grid=(count - first,),
            in_specs=[
                pl.BlockSpec(memory_space=pl.ANY),
                pl.BlockSpec(memory_space=pl.ANY),
                pl.BlockSpec((D, 4 * width), fixed, pipeline_mode=pl.Buffered(1)),
                pl.BlockSpec((count, LEN), fixed),
                pl.BlockSpec((ROT, LEN), fixed),
                pl.BlockSpec(memory_space=pl.ANY),
                pl.BlockSpec(memory_space=pl.ANY),
            ],
            out_specs=[
                pl.BlockSpec((LEN, width), seq_rows),
                pl.BlockSpec((LEN, 3 * width), seq_rows),
            ],
            scratch_shapes=[
                pltpu.VMEM((LEN, D), bf16),
                pltpu.VMEM((LEN, D), bf16),
                pltpu.SemaphoreType.DMA((2, LEN // QB)),
                *Attention.scratch(heads),
            ],
        ),
        input_output_aliases={6: 0, 7: 1},
        compiler_params=pltpu.CompilerParams(
            dimension_semantics=("arbitrary",), vmem_limit_bytes=56 << 20
        ),
        cost_estimate=pl.CostEstimate(
            flops=(count - first) * LEN * (36 * 640 * width + 8 * D * width),
            bytes_accessed=(count - first) * LEN * (width * 8 + 4 * D) + 8 * D * width,
            transcendentals=(count - first) * LEN * 640 * heads,
        ),
        name="attention",
    )(image_start, normed, grad, weights, doc_ids, jnp.asarray(rope_rows()), *earlier)


def ffn_kernel(x_ref, g_ref, wgu_ref, wd_ref, hidden_ref, gg_ref, gu_ref):
    f32, bf16 = jnp.float32, jnp.bfloat16
    x = x_ref[...]
    ffn = wd_ref.shape[0]
    gate = lax.dot_general(x, wgu_ref[:ffn], NT, preferred_element_type=f32)
    up = lax.dot_general(x, wgu_ref[ffn:], NT, preferred_element_type=f32)
    grad = lax.dot_general(g_ref[...], wd_ref[...], NT, preferred_element_type=f32)
    sigma = jax.nn.sigmoid(gate)
    silu = gate * sigma
    hidden_ref[...] = (silu * up).astype(bf16)
    gg_ref[...] = (grad * up * (sigma + silu * (1.0 - sigma))).astype(bf16)
    gu_ref[...] = (grad * silu).astype(bf16)


def feed_forward(normed, grad, wffn):
    rows, ffn = normed.shape[0], wffn.shape[0] // 3
    block = lambda i: (i, 0)
    return pl.pallas_call(
        ffn_kernel,
        out_shape=[jax.ShapeDtypeStruct((rows, ffn), jnp.bfloat16)] * 3,
        grid=(rows // MB,),
        in_specs=[
            pl.BlockSpec((MB, D), block),
            pl.BlockSpec((MB, D), block),
            pl.BlockSpec((2 * ffn, D), lambda i: (0, 0), pipeline_mode=pl.Buffered(1)),
            pl.BlockSpec((ffn, D), lambda i: (2, 0), pipeline_mode=pl.Buffered(1)),
        ],
        out_specs=[pl.BlockSpec((MB, ffn), block)] * 3,
        compiler_params=pltpu.CompilerParams(
            dimension_semantics=("arbitrary",), vmem_limit_bytes=56 << 20
        ),
        cost_estimate=pl.CostEstimate(
            flops=6 * rows * D * ffn,
            bytes_accessed=rows * (4 * D + 6 * ffn) + 6 * D * ffn,
            transcendentals=rows * ffn,
        ),
        name="feed_forward",
    )(normed, grad, wffn, wffn)


def flip(index, bits):
    bit = 1
    while bit <= bits:
        if bits & bit:
            index = index + bit - 2 * bit * ((index // bit) % 2)
        bit *= 2
    return index


def chip_orders(ways):
    bits = [1 << k for k in range(1, ways.bit_length() - 1)]
    return bits, bits[::-1]


def held(bits):
    found = [0]
    for bit in bits:
        found += [o ^ bit for o in found]
    return found


def meet(peers):
    barrier = pltpu.get_barrier_semaphore()
    for peer in peers:
        pl.semaphore_signal(barrier, inc=1, device_id=peer, device_id_type=MESH)
    pl.semaphore_wait(barrier, len(peers))


def gather_kernel(ways, base, attended, count, *refs):
    f32, bf16 = jnp.float32, jnp.bfloat16
    me = lax.axis_index("col")
    if attended:
        (token_ref, cot_ref, vectors_ref, w_ref, rope_ref, doc_ref, image_ref, old_ref) = refs[:8]
        (old_normed, old_grad, normed_ref, full_ref, stat_ref, att_ref, gp_ref) = refs[8:15]
        refs = refs[15:]
    else:
        (token_ref, cot_ref, vector_ref, gate_ref, down_ref) = refs[:5]
        (normed_ref, full_ref, stat_ref, vectors_ref, ffn_ref) = refs[5:10]
        refs = refs[10:]
    (both, load_sem, store_sem, full_sem, send_sem, recv_sem) = refs[:6]
    refs = refs[6:]
    width = token_ref.shape[1]
    rows = both.shape[1]
    pairs = rows // count
    orders = chip_orders(ways)
    phases = len(orders[0])
    mine = pl.ds(pl.multiple_of(me * width, width), width)
    source = pl.ds(base, rows)
    loads = [
        pltpu.make_async_copy(token_ref.at[source], both.at[me, :, pl.ds(0, width)], load_sem.at[0]),
        pltpu.make_async_copy(cot_ref.at[source], both.at[me, :, pl.ds(width, width)], load_sem.at[1]),
    ]
    for load in loads:
        load.start()
    peers = [flip(me, k) for k in range(1, ways)]
    if attended:
        meet([{"col": flip(me, 1 << k)} for k in range(ways.bit_length() - 1)])
    else:
        vectors_ref[:, mine] = vector_ref[...]
        meet([{"col": peer} for peer in peers])

    def vector_copy(k):
        return pltpu.make_async_remote_copy(
            src_ref=vectors_ref.at[:, mine],
            dst_ref=vectors_ref.at[:, mine],
            send_sem=refs[0].at[k],
            recv_sem=refs[1].at[k],
            device_id={"col": peers[k]},
            device_id_type=MESH,
        )

    def copies(p, phase):
        for k, order in enumerate(orders):
            bit = order[phase] if phase < phases else 1
            place = pl.ds(pl.multiple_of(p * count + k * (count // 2), count // 2), count // 2)
            for o in held(order[:phase]):
                index = k * ways + (o ^ bit)
                owner = flip(me, o)
                yield pltpu.make_async_remote_copy(
                    src_ref=both.at[owner, place],
                    dst_ref=both.at[owner, place],
                    send_sem=send_sem.at[p, index],
                    recv_sem=recv_sem.at[p, index],
                    device_id={"col": flip(me, bit)},
                    device_id_type=MESH,
                )

    def start(p, phase):
        for copy in copies(p, phase):
            copy.start()

    def arrive(p, phase):
        for copy in copies(p, phase):
            copy.wait_recv()

    def filed(p, first, out_ref, sem):
        place = pl.ds(pl.multiple_of(p * count, count), count)
        goal = pl.ds(pl.multiple_of(base + p * count, count), count)
        for b in range(ways):
            pltpu.make_async_copy(
                both.at[b, place, pl.ds(first, width)],
                out_ref.at[goal, pl.ds(b * width, width)],
                sem.at[p],
            ).start()

    def filed_wait(p, out_ref, sem):
        place = out_ref.at[pl.ds(base + p * count, count)]
        pltpu.make_async_copy(place, place, sem.at[p]).wait()

    def norm(p):
        filed(p, width, full_ref, full_sem)
        for phase in range(phases + 1):
            for copy in copies(p, phase):
                copy.wait_send()

        def block(j, _):
            at = pl.ds(pl.multiple_of(p * count + j * QB, QB), QB)
            goal = pl.ds(pl.multiple_of(base + p * count + j * QB, QB), QB)
            sums = sum(both[b, at, :width].astype(f32) for b in range(ways))
            mean = jnp.sum(sums, axis=1, keepdims=True) / D
            squares = jnp.zeros((QB, width), f32)
            for b in range(ways):
                x = both[b, at, :width].astype(f32) - mean
                squares += x * x
            inv = lax.rsqrt(jnp.sum(squares, axis=1, keepdims=True) / D + NORM_EPS)
            stat_ref[goal, :1] = mean
            stat_ref[goal, 1:] = inv
            for b in range(ways):
                cols = slice(b * width, (b + 1) * width)
                x = (both[b, at, :width].astype(f32) - mean) * inv
                x = x * vectors_ref[0:1, cols] + vectors_ref[1:2, cols]
                both[b, at, :width] = x.astype(bf16)
            return 0

        lax.fori_loop(0, count // QB, block, 0)
        filed(p, 0, normed_ref, store_sem)

    if attended:
        x_scr, g_scr, att_scr, gp_scr, in_sem, out_sem = refs[:6]
        attend = Attention(width // HD, refs[6:])
        stat_ref[pl.ds(0, base), :] = old_ref[pl.ds(0, base), :]

        def fetch(seq):
            place = pl.ds(pl.multiple_of(seq * LEN, LEN), LEN)
            return [
                pltpu.make_async_copy(old_normed.at[place], x_scr, in_sem.at[seq, 0]),
                pltpu.make_async_copy(old_grad.at[place], g_scr, in_sem.at[seq, 1]),
            ]

        def give(seq):
            place = pl.ds(pl.multiple_of(seq * LEN, LEN), LEN)
            return [
                pltpu.make_async_copy(att_scr.at[seq], att_ref.at[place], out_sem.at[seq, 0]),
                pltpu.make_async_copy(gp_scr.at[seq], gp_ref.at[place], out_sem.at[seq, 1]),
            ]

        for move in fetch(0):
            move.start()

    for load in loads:
        load.wait()
    start(0, 0)
    start(1, 0)
    if attended:
        fill_tables(rope_ref, attend.tables)
    else:
        ffn_scr, ffn_sem = refs[2:4]
        split = gate_ref.shape[0]
        moves = [
            pltpu.make_async_copy(gate_ref, ffn_scr.at[pl.ds(0, split)], ffn_sem.at[0]),
            pltpu.make_async_copy(down_ref, ffn_scr.at[pl.ds(split, split // 2)], ffn_sem.at[1]),
        ]
        for move in moves:
            move.start()
        for move in moves:
            move.wait()
        laid = pltpu.make_async_copy(ffn_scr, ffn_ref, ffn_sem.at[2])
        laid.start()
        for k in range(ways - 1):
            vector_copy(k).start()
        for k in range(ways - 1):
            vector_copy(k).wait_recv()
    blocks = LEN // QB
    turns = attended * blocks // pairs if attended else 0

    def step(p, _):
        for phase in range(phases):
            if phase or attended:
                arrive(p, phase)
                start(p, phase + 1)
            if phase == 0:
                if attended:
                    pl.when(p + 2 < pairs)(lambda: start(p + 2, 0))
                else:

                    @pl.when(p + 1 < pairs)
                    def _():
                        arrive(p + 1, 0)
                        start(p + 1, 1)

                    pl.when(p + 3 < pairs)(lambda: start(p + 3, 0))

                @pl.when(p >= 1)
                def _():
                    arrive(p - 1, phases)
                    norm(p - 1)

                if attended:
                    seq = p * turns // blocks
                    spot = p * turns % blocks

                    @pl.when(spot == 0)
                    def _():
                        for move in fetch(seq):
                            move.wait()
                        attend.begin(doc_ref, seq, image_ref[seq], x_scr, g_scr, w_ref)

                        @pl.when(seq + 1 < attended)
                        def _():
                            for move in fetch(seq + 1):
                                move.start()

                    def query_block(i, _):
                        low = i // (blocks - 1)
                        attend.query_block(i, low, i + 1 - low, att_scr.at[seq], gp_scr.at[seq])
                        return 0

                    lax.fori_loop(spot, spot + turns, query_block, 0)

                    @pl.when(spot + turns == blocks)
                    def _():
                        attend.finish(gp_scr.at[seq])
                        for move in give(seq):
                            move.start()
        return 0

    if not attended:
        arrive(0, 0)
        start(0, 1)
        start(2, 0)
    lax.fori_loop(0, pairs, step, 0)
    arrive(pairs - 1, phases)
    norm(pairs - 1)
    for p in range(pairs):
        filed_wait(p, full_ref, full_sem)
        filed_wait(p, normed_ref, store_sem)
    if attended:
        for seq in range(attended):
            for move in give(seq):
                move.wait()
    else:
        laid.wait()
        for k in range(ways - 1):
            vector_copy(k).wait_send()


def gather_scratch(ways, rows, width, count):
    dma = pltpu.SemaphoreType.DMA
    pairs = rows // count
    return [
        pltpu.VMEM((ways, rows, 2 * width), jnp.bfloat16),
        dma((2,)),
        dma((pairs,)),
        dma((pairs,)),
        dma((pairs, 2 * ways)),
        dma((pairs, 2 * ways)),
    ]


def gather_first(tokens, out_grad, vectors, gate_up, down, count, ways):
    rows, width = tokens.shape
    bf16, f32 = jnp.bfloat16, jnp.float32
    anywhere = pl.BlockSpec(memory_space=pl.ANY)
    vmem = pl.BlockSpec(memory_space=pltpu.VMEM)
    dma = pltpu.SemaphoreType.DMA
    return pl.pallas_call(
        functools.partial(gather_kernel, ways, 0, 0, GB),
        out_shape=[
            jax.ShapeDtypeStruct((rows, D), bf16),
            jax.ShapeDtypeStruct((rows, D), bf16),
            jax.ShapeDtypeStruct((rows, 2), f32),
            jax.ShapeDtypeStruct((8, D), f32),
            jax.ShapeDtypeStruct((3 * down.shape[0], down.shape[1]), bf16),
        ],
        in_specs=[anywhere, anywhere, vmem, anywhere, anywhere],
        out_specs=[anywhere, anywhere, vmem, vmem, anywhere],
        scratch_shapes=[
            *gather_scratch(ways, count, width, GB),
            dma((ways - 1,)),
            dma((ways - 1,)),
            pltpu.VMEM((3 * down.shape[0], down.shape[1]), bf16),
            dma((3,)),
        ],
        compiler_params=pltpu.CompilerParams(
            collective_id=0, has_side_effects=True, vmem_limit_bytes=63 << 20
        ),
        cost_estimate=pl.CostEstimate(
            flops=100 * count * D * D // ways, bytes_accessed=count * D * 8, transcendentals=0
        ),
        name="gather_first",
    )(tokens, out_grad, vectors, gate_up, down)


def gather_rest(tokens, out_grad, vectors, weights, doc_ids, image_start, stats, normed, grad, ways):
    rows, width = tokens.shape
    count = rows // 2
    bf16, f32 = jnp.bfloat16, jnp.float32
    anywhere = pl.BlockSpec(memory_space=pl.ANY)
    vmem = pl.BlockSpec(memory_space=pltpu.VMEM)
    dma = pltpu.SemaphoreType.DMA
    seqs = count // LEN
    return pl.pallas_call(
        functools.partial(gather_kernel, ways, count, seqs, GA),
        out_shape=[
            jax.ShapeDtypeStruct((rows, D), bf16),
            jax.ShapeDtypeStruct((rows, D), bf16),
            jax.ShapeDtypeStruct((rows, 2), f32),
            jax.ShapeDtypeStruct((rows, width), bf16),
            jax.ShapeDtypeStruct((rows, 3 * width), bf16),
        ],
        in_specs=[
            anywhere,
            anywhere,
            vmem,
            vmem,
            vmem,
            vmem,
            pl.BlockSpec(memory_space=pltpu.SMEM),
            vmem,
            anywhere,
            anywhere,
        ],
        out_specs=[anywhere, anywhere, vmem, anywhere, anywhere],
        input_output_aliases={8: 0, 9: 1},
        scratch_shapes=[
            *gather_scratch(ways, rows - count, width, GA),
            pltpu.VMEM((LEN, D), bf16),
            pltpu.VMEM((LEN, D), bf16),
            pltpu.VMEM((seqs, LEN, width), bf16),
            pltpu.VMEM((seqs, LEN, 3 * width), bf16),
            dma((seqs, 2)),
            dma((seqs, 2)),
            *Attention.scratch(width // HD),
        ],
        compiler_params=pltpu.CompilerParams(
            collective_id=3, has_side_effects=True, vmem_limit_bytes=63 << 20
        ),
        cost_estimate=pl.CostEstimate(
            flops=100 * count * D * D // ways, bytes_accessed=count * D * 8, transcendentals=0
        ),
        name="gather_rest",
    )(tokens, out_grad, vectors, weights, jnp.asarray(rope_rows()), doc_ids, image_start, stats, normed, grad)


class Reducer:
    def __init__(self, ways, parts, inbox, send_sem, recv_sem):
        self.ways, self.parts, self.inbox = ways, parts, inbox
        self.send_sem, self.recv_sem = send_sem, recv_sem
        self.me = lax.axis_index("col")
        self.orders = chip_orders(ways)
        self.phases = 1 + len(self.orders[0])

    def moves(self, step, phase):
        halves = [None] if phase == 0 else [0, 1]
        for k in halves:
            order = [1] if phase == 0 else [1, *self.orders[k]]
            bit = order[phase]
            done = sum(order[:phase])
            count = RB if k is None else RB // 2
            rows = pl.ds(pl.multiple_of(step * RB + (k or 0) * count, count), count)
            for o in range(self.ways):
                if o & done or not o & bit:
                    continue
                goal = o ^ bit
                slot = slot_of(self.ways, self.orders, phase, k, goal)
                sem = 2 * slot + (k or 0)
                copy = pltpu.make_async_remote_copy(
                    src_ref=self.parts.at[o, rows],
                    dst_ref=self.inbox.at[slot, rows],
                    send_sem=self.send_sem.at[step, sem],
                    recv_sem=self.recv_sem.at[step, sem],
                    device_id={"col": flip(self.me, bit)},
                    device_id_type=MESH,
                )
                yield copy, goal, slot, rows

    def send(self, step, phase):
        for copy, *_ in self.moves(step, phase):
            copy.start()

    def absorb(self, step, phase):
        out = []
        for copy, goal, slot, rows in self.moves(step, phase):
            copy.wait_recv()
            value = self.parts[goal, rows, :].astype(jnp.float32)
            value += self.inbox[slot, rows, :].astype(jnp.float32)
            if phase == self.phases - 1:
                out.append(value)
            else:
                self.parts[goal, rows, :] = value.astype(jnp.bfloat16)
        return out

    def finish(self, step):
        for phase in range(self.phases):
            for copy, *_ in self.moves(step, phase):
                copy.wait_send()

    def advance(self, t, steps, lags):
        pl.when(t < steps)(lambda: self.send(t, 0))
        for phase in range(self.phases - 1):
            s = t - lags[phase]

            @pl.when((s >= 0) & (s < steps))
            def _():
                self.absorb(s, phase)
                self.send(s, phase + 1)


def slot_of(ways, orders, phase, half, goal):
    if phase == 0:
        return goal // 2
    order = [1, *orders[half]]
    base = ways // 2
    for p in range(1, phase):
        base += ways >> (p + 1)
    goals = [g for g in range(ways) if not g & sum(order[: phase + 1])]
    return base + goals.index(goal)


def lags_of(ways):
    return [1 + 2 * p for p in range(len(chip_orders(ways)[0]) + 1)]


def reducer_scratch(ways, rows, width):
    steps = rows // RB
    return [
        pltpu.VMEM((ways, rows, width), jnp.bfloat16),
        pltpu.VMEM((ways - 1, rows, width), jnp.bfloat16),
        pltpu.SemaphoreType.DMA((steps, 2 * ways)),
        pltpu.SemaphoreType.DMA((steps, 2 * ways)),
    ]


def branch_kernel(
    ways,
    steps,
    att_ref,
    hidden_ref,
    grad_ref,
    token_ref,
    wout_ref,
    wd_ref,
    out_ref,
    wgrad_ref,
    parts,
    inbox,
    send_sem,
    recv_sem,
    acc,
    acc_out,
):
    f32, bf16 = jnp.float32, jnp.bfloat16
    t = pl.program_id(0)
    me, width = lax.axis_index("col"), D // ways
    lags = lags_of(ways)
    ring = Reducer(ways, parts, inbox, send_sem, recv_sem)

    @pl.when(t == 0)
    def _():
        acc[...] = jnp.zeros_like(acc)
        acc_out[...] = jnp.zeros_like(acc_out)
        meet([{"col": flip(me, 1 << k)} for k in range(ways.bit_length() - 1)])

    @pl.when(t < steps)
    def _():
        rows = pl.ds(pl.multiple_of(t * RB, RB), RB)
        att, hidden = att_ref[...], hidden_ref[...]
        total = jnp.dot(hidden, wd_ref[...], preferred_element_type=f32)
        total += lax.dot_general(att, wout_ref[...], NT, preferred_element_type=f32)
        for b in range(ways):
            parts[flip(me, b), rows, :] = total[:, b * width : (b + 1) * width].astype(bf16)

    ring.advance(t, steps, lags)

    @pl.when(t < steps)
    def _():
        acc[...] += contract(hidden_ref[...], grad_ref[...], 0, 0)
        acc_out[...] += contract(att_ref[...], grad_ref[...], 0, 0)

    @pl.when(t == steps)
    def _():
        ffn = acc.shape[0]
        wgrad_ref[:ffn, :] = acc[...].astype(bf16)
        wgrad_ref[ffn:, :] = acc_out[...].astype(bf16)

    s = t - lags[-1]

    @pl.when(s >= 0)
    def _():
        for k, value in enumerate(ring.absorb(s, ring.phases - 1)):
            half = slice(k * (RB // 2), (k + 1) * (RB // 2))
            out_ref[half, :] = (token_ref[half, :].astype(f32) + value).astype(bf16)
        ring.finish(s)


def branches(att, hidden, grad, tokens, weights, wffn, ways):
    rows, width = tokens.shape
    ffn = wffn.shape[0] // 3
    steps = rows // RB
    lag = lags_of(ways)[-1]
    now = lambda t: (jnp.minimum(t, steps - 1), 0)
    late = lambda t: (jnp.maximum(t - lag, 0), 0)
    fixed = lambda t: (0, 0)
    once = pl.Buffered(1)
    return pl.pallas_call(
        functools.partial(branch_kernel, ways, steps),
        out_shape=[
            jax.ShapeDtypeStruct((rows, width), jnp.bfloat16),
            jax.ShapeDtypeStruct((ffn + width, D), jnp.bfloat16),
        ],
        grid=(steps + lag,),
        in_specs=[
            pl.BlockSpec((RB, width), now),
            pl.BlockSpec((RB, ffn), now),
            pl.BlockSpec((RB, D), now),
            pl.BlockSpec((RB, width), late),
            pl.BlockSpec((D, width), lambda t: (0, 3), pipeline_mode=once),
            pl.BlockSpec((ffn, D), lambda t: (2, 0), pipeline_mode=once),
        ],
        out_specs=[
            pl.BlockSpec((RB, width), late),
            pl.BlockSpec((ffn + width, D), fixed, pipeline_mode=once),
        ],
        scratch_shapes=[
            *reducer_scratch(ways, rows, width),
            pltpu.VMEM((ffn, D), jnp.float32),
            pltpu.VMEM((width, D), jnp.float32),
        ],
        compiler_params=pltpu.CompilerParams(
            collective_id=1,
            has_side_effects=True,
            dimension_semantics=("arbitrary",),
            vmem_limit_bytes=60 << 20,
        ),
        cost_estimate=pl.CostEstimate(
            flops=8 * rows * D * (2 * ffn + width), bytes_accessed=4 * rows * D, transcendentals=0
        ),
        name="branches",
    )(att, hidden, grad, tokens, weights, wffn)


def back_kernel(
    ways,
    lines,
    steps,
    gp_ref,
    gg_ref,
    gu_ref,
    x_ref,
    token_ref,
    cot_ref,
    stat_ref,
    w_ref,
    wgu_ref,
    vectors_ref,
    gain_ref,
    wqkv_ref,
    out_ref,
    vgrad_ref,
    qkv_ref,
    parts,
    inbox,
    send_sem,
    recv_sem,
    sums,
    ssend_sem,
    srecv_sem,
    acc,
    vsend_sem,
    vrecv_sem,
):
    f32, bf16 = jnp.float32, jnp.bfloat16
    t = pl.program_id(0)
    me, width = lax.axis_index("col"), D // ways
    line = lax.axis_index("row")
    lags = lags_of(ways)
    ring = Reducer(ways, parts, inbox, send_sem, recv_sem)

    @pl.when(t == 0)
    def _():
        acc[...] = jnp.zeros_like(acc)
        meet(
            [{"col": flip(me, k)} for k in range(1, ways)]
            + [{"row": (line + k) % lines} for k in range(1, lines)]
        )

    def sum_copies(group):
        rows = pl.ds(pl.multiple_of(group * RB, RB), RB)
        for k in range(1, ways):
            yield pltpu.make_async_remote_copy(
                src_ref=sums.at[0, :, rows],
                dst_ref=sums.at[k, :, rows],
                send_sem=ssend_sem.at[group, k - 1],
                recv_sem=srecv_sem.at[group, k - 1],
                device_id={"col": flip(me, k)},
                device_id_type=MESH,
            )

    @pl.when(t < steps)
    def _():
        rows = pl.ds(pl.multiple_of(t * RB, RB), RB)
        gp, gg, gu = gp_ref[...], gg_ref[...], gu_ref[...]
        total = jnp.dot(gg, wgu_ref[: gg.shape[1]], preferred_element_type=f32)
        total += jnp.dot(gu, wgu_ref[gg.shape[1] :], preferred_element_type=f32)
        total += lax.dot_general(gp, w_ref[...], NT, preferred_element_type=f32)
        for b in range(ways):
            parts[flip(me, b), rows, :] = total[:, b * width : (b + 1) * width].astype(bf16)
        scaled = x_ref[...].astype(f32) - vectors_ref[1:2, :]
        plain = jnp.sum(total * vectors_ref[0:1, :], axis=1, keepdims=True)
        cross = jnp.sum(total * scaled, axis=1, keepdims=True)
        lane = lax.broadcasted_iota(jnp.int32, (RB, 128), 1)
        spot = 2 * (t % SUMS)
        pair = jnp.where(lane == spot, plain, jnp.where(lane == spot + 1, cross, 0.0))
        group = pl.ds(pl.multiple_of(t // SUMS * RB, RB), RB)
        before = jnp.where(jnp.broadcast_to(spot == 0, (8, RB)), 0.0, sums[0, :, group])
        sums[0, :, group] = before + pair.T[:8]
        for kind in range(3):
            qkv_ref[kind] = wqkv_ref[:, kind * width : (kind + 1) * width].astype(f32)

        @pl.when(t % SUMS == SUMS - 1)
        def _():
            for copy in sum_copies(t // SUMS):
                copy.start()

    ring.advance(t, steps, lags)
    s = t - lags[-1]

    @pl.when(s >= 0)
    def _():
        @pl.when(s % SUMS == 0)
        def _():
            for copy in sum_copies(s // SUMS):
                copy.wait_recv()

        group = pl.ds(pl.multiple_of(s // SUMS * RB, RB), RB)
        both = sum(sums[k, :, group] for k in range(ways)).T
        lane = lax.broadcasted_iota(jnp.int32, (RB, 8), 1)
        spot = 2 * (s % SUMS)
        plain = jnp.sum(jnp.where(lane == spot, both, 0.0), axis=1, keepdims=True) / D
        cross = jnp.sum(jnp.where(lane == spot + 1, both, 0.0), axis=1, keepdims=True) / D
        for k, value in enumerate(ring.absorb(s, ring.phases - 1)):
            half = slice(k * (RB // 2), (k + 1) * (RB // 2))
            inv = stat_ref[half, 1:]
            unit = (token_ref[half, :].astype(f32) - stat_ref[half, :1]) * inv
            scaled = value * gain_ref[0:1, :]
            out_ref[half, :] = cot_ref[half, :].astype(f32) + inv * (
                scaled - plain[half] - unit * cross[half]
            )
            acc[0, 0:1, :] += jnp.sum(value * unit, axis=0, keepdims=True)
            acc[0, 1:2, :] += jnp.sum(value, axis=0, keepdims=True)

        @pl.when(s % SUMS == 0)
        def _():
            for copy in sum_copies(s // SUMS):
                copy.wait_send()

        ring.finish(s)

    @pl.when(t == pl.num_programs(0) - 1)
    def _():
        copies = [
            pltpu.make_async_remote_copy(
                src_ref=acc.at[0],
                dst_ref=acc.at[k],
                send_sem=vsend_sem.at[k - 1],
                recv_sem=vrecv_sem.at[k - 1],
                device_id={"row": (line + k) % lines},
                device_id_type=MESH,
            )
            for k in range(1, lines)
        ]
        for copy in copies:
            copy.start()
        for copy in copies:
            copy.wait()
        vgrad_ref[...] = sum(acc[k] for k in range(lines))


def norm_back(
    gp, gg, gu, normed, tokens, cot, stats, weights, wffn, vectors, own, qkv, ways, lines
):
    rows, width = tokens.shape
    ffn = gg.shape[1]
    steps = rows // RB
    lag = lags_of(ways)[-1]
    deep = qkv.shape[0]
    slab = deep // steps
    now = lambda t: (jnp.minimum(t, steps - 1), 0)
    late = lambda t: (jnp.maximum(t - lag, 0), 0)
    fixed = lambda t: (0, 0)
    once = pl.Buffered(1)
    dma = pltpu.SemaphoreType.DMA
    return pl.pallas_call(
        functools.partial(back_kernel, ways, lines, steps),
        out_shape=[
            jax.ShapeDtypeStruct((rows, width), jnp.float32),
            jax.ShapeDtypeStruct((8, width), jnp.float32),
            jax.ShapeDtypeStruct((3, deep, width), jnp.float32),
        ],
        grid=(steps + lag,),
        in_specs=[
            pl.BlockSpec((RB, 3 * width), now),
            pl.BlockSpec((RB, ffn), now),
            pl.BlockSpec((RB, ffn), now),
            pl.BlockSpec((RB, D), now),
            pl.BlockSpec((RB, width), late),
            pl.BlockSpec((RB, width), late),
            pl.BlockSpec((RB, 2), late),
            pl.BlockSpec((D, 3 * width), fixed, pipeline_mode=once),
            pl.BlockSpec((2 * ffn, D), fixed, pipeline_mode=once),
            pl.BlockSpec((8, D), fixed),
            pl.BlockSpec((8, width), fixed),
            pl.BlockSpec((slab, 3 * width), now),
        ],
        out_specs=[
            pl.BlockSpec((RB, width), late),
            pl.BlockSpec((8, width), fixed),
            pl.BlockSpec((3, slab, width), lambda t: (0, jnp.minimum(t, steps - 1), 0)),
        ],
        scratch_shapes=[
            *reducer_scratch(ways, rows, width),
            pltpu.VMEM((ways, 8, rows // SUMS), jnp.float32),
            dma((steps // SUMS, ways - 1)),
            dma((steps // SUMS, ways - 1)),
            pltpu.VMEM((lines, 8, width), jnp.float32),
            dma((lines - 1,)),
            dma((lines - 1,)),
        ],
        compiler_params=pltpu.CompilerParams(
            collective_id=2,
            has_side_effects=True,
            dimension_semantics=("arbitrary",),
            vmem_limit_bytes=61 << 20,
        ),
        cost_estimate=pl.CostEstimate(
            flops=4 * rows * D * (2 * ffn + 3 * width), bytes_accessed=6 * rows * D, transcendentals=0
        ),
        name="norm_back",
    )(gp, gg, gu, normed, tokens, cot, stats, weights, wffn, vectors, own, qkv)


def after(value, *others):
    return lax.optimization_barrier((value, others))[0]


def local(
    tokens,
    norm_gain,
    norm_bias,
    qkv_weight,
    gate_up_weight,
    out_weight,
    down_weight,
    image_start,
    doc_ids,
    out_grad,
):
    f32, bf16 = jnp.float32, jnp.bfloat16
    block_rows, width = tokens.shape
    ways = D // width
    lines = D // qkv_weight.shape[0]

    own = jnp.concatenate([qkv_weight[:, k] for k in range(3)] + [out_weight], axis=1)
    weights = lax.all_gather(own, "row", axis=0, tiled=True)
    own_vectors = jnp.pad(jnp.stack([norm_gain, norm_bias]), ((0, 6), (0, 0)))

    half = block_rows // 2
    normed, grad, stats, vectors, own_ffn = gather_first(
        tokens,
        out_grad,
        own_vectors,
        jnp.transpose(gate_up_weight, (1, 2, 0)).reshape(-1, D // lines),
        jnp.transpose(down_weight, (1, 0)),
        half,
        ways,
    )
    wffn = lax.all_gather(own_ffn, "row", axis=1, tiled=True)
    normed, grad, stats, *earlier = gather_rest(
        tokens, out_grad, vectors, weights, doc_ids, image_start, stats, normed, grad, ways
    )
    attended, grad_projected = attention(
        half // LEN, normed, grad, weights, image_start, doc_ids, earlier
    )

    def weight_sum(grad):
        return lax.psum_scatter(grad, "row", scatter_dimension=0, tiled=True)

    def weight_grad(left, right):
        return contract(left, right, 0, 0).astype(bf16)

    grad_qkv = weight_grad(normed, grad_projected)
    hidden, grad_gate, grad_up = feed_forward(after(normed, grad_qkv), grad, wffn)
    weight_gate = weight_grad(normed, grad_gate)
    weight_up = weight_grad(normed, after(grad_up, weight_gate))
    qkv_sum = weight_sum(grad_qkv)
    gate_sum = weight_sum(weight_gate)
    outputs, weight_rest = branches(
        after(attended, weight_up, qkv_sum), hidden, grad, tokens, weights, wffn, ways
    )
    input_grad, vector_grads, qkv_sum = norm_back(
        after(grad_projected, outputs, gate_sum),
        grad_gate,
        grad_up,
        normed,
        tokens,
        out_grad,
        stats,
        weights,
        wffn,
        vectors,
        own_vectors,
        qkv_sum,
        ways,
        lines,
    )
    qkv_sum = jnp.transpose(qkv_sum, (1, 0, 2))
    up_sum = after(weight_sum(weight_up), input_grad)
    rest = weight_sum(jnp.transpose(weight_rest, (1, 0)))
    down_sum, out_sum = rest[:, :-width].astype(f32), rest[:, -width:].astype(f32)
    gate_up_sum = jnp.stack([gate_sum.astype(f32), up_sum.astype(f32)], axis=1)
    return (
        outputs,
        input_grad,
        vector_grads[0],
        vector_grads[1],
        qkv_sum,
        gate_up_sum,
        out_sum,
        down_sum,
    )


def solution(mesh):
    placed = (
        P("row", "col"),
        P("col"),
        P("col"),
        P("row", None, "col"),
        P("row", None, "col"),
        P("row", "col"),
        P("row", "col"),
        P("row"),
        P("row", None),
        P("row", "col"),
    )
    return jax.shard_map(
        local,
        mesh=mesh,
        in_specs=placed,
        out_specs=(
            P("row", "col"),
            P("row", "col"),
            P("col"),
            P("col"),
            P("row", None, "col"),
            P("row", None, "col"),
            P("row", "col"),
            P("row", "col"),
        ),
        check_vma=False,
    )
```

```python
import functools

import jax
import jax.numpy as jnp
import numpy as np
from jax import lax
from jax.experimental import pallas as pl
from jax.experimental.pallas import tpu as pltpu
from jax.sharding import PartitionSpec as P

D = 2048
HD = 64
ROT = 16
LEN = 1024
IMG = 256
QB = 256
MB = 256
RB = 256
GB = 256
GA = 256
SUMS = 4


NORM_EPS = 1e-05
MESH = pl.DeviceIdType.MESH
MASKED_SCORE = -1e30
ROPE_BASE = 10000.0
NT = (((1,), (1,)), ((), ()))


def contract(left, right, left_dim, right_dim):
    return lax.dot_general(
        left, right, (((left_dim,), (right_dim,)), ((), ())), preferred_element_type=jnp.float32
    )


def rope_rows():
    half = ROT // 2
    inv_freq = np.float32(ROPE_BASE) ** (np.float32(-2.0 / ROT) * np.arange(half, dtype=np.float32))
    angles = np.arange(LEN, dtype=np.float32)[None, :] * inv_freq[:, None]
    wide = angles.astype(np.float64)
    return np.concatenate([np.cos(wide), np.sin(wide)]).astype(np.float32)


def fill_tables(rows_ref, tables):
    half = ROT // 2
    for i in range(LEN // QB):
        sl = pl.ds(i * QB, QB)
        cosines, sines = rows_ref[:half, sl], rows_ref[half:, sl]
        zero = jnp.zeros_like(sines)
        rest = [zero] * (HD // half - 2)
        ones = [jnp.ones_like(sines)] * (HD // half - 2)
        tables[0, sl, :] = jnp.concatenate([cosines, cosines, *ones] * (128 // HD), axis=0).T
        tables[1, sl, :] = jnp.concatenate([-sines, zero, *rest] * (128 // HD), axis=0).T
        tables[2, sl, :] = jnp.concatenate([zero, sines, *rest] * (128 // HD), axis=0).T


def turn(x, tables, sl, sign):
    width = x.shape[1]
    c, a, b = (jnp.concatenate([tables[k, sl, :]] * (width // 128), axis=1) for k in range(3))
    left = pltpu.roll(x, width - ROT // 2, 1)
    right = pltpu.roll(x, ROT // 2, 1)
    return x * c + (left * a + right * b) * sign


class Attention:
    def __init__(self, heads, scratch):
        self.heads, self.width = heads, heads * HD
        (
            self.tables,
            self.span,
            self.data,
            self.kt,
            self.vt,
            self.s,
            self.d,
            self.e,
            self.bias,
            self.m,
            self.l,
            self.ot,
            self.dqt,
            self.dk,
            self.dv,
        ) = scratch

    @staticmethod
    def scratch(heads):
        f32, bf16, blocks, width = jnp.float32, jnp.bfloat16, LEN // QB, heads * HD
        return [
            pltpu.VMEM((3, LEN, 128), f32),
            pltpu.VMEM((blocks, 8, QB), jnp.int32),
            pltpu.VMEM((LEN, 4 * width), bf16),
            pltpu.VMEM((blocks, width, QB), bf16),
            pltpu.VMEM((blocks, width, QB), bf16),
            pltpu.VMEM((blocks, heads, QB, QB), f32),
            pltpu.VMEM((blocks, heads, QB, QB), f32),
            pltpu.VMEM((blocks, heads, QB, QB), bf16),
            pltpu.VMEM((2, QB, QB), f32),
            pltpu.VMEM((heads, 8, QB), f32),
            pltpu.VMEM((heads, 8, QB), f32),
            pltpu.VMEM((width, QB), f32),
            pltpu.VMEM((width, QB), f32),
            pltpu.VMEM((LEN, width), f32),
            pltpu.VMEM((LEN, width), f32),
        ]

    def part(self, kind):
        return pl.ds(kind * self.width, self.width)

    def begin(self, doc_ref, seq, start, x_ref, g_ref, w_ref, arrive=None):
        f32, bf16, width = jnp.float32, jnp.bfloat16, self.width
        docs = doc_ref[pl.ds(seq, 1), :].astype(f32)
        down = jnp.broadcast_to(docs, (128, LEN)).T[:, :1]
        for i in range(LEN // QB):
            own = docs[:, i * QB : (i + 1) * QB]
            first = jnp.sum((down < own).astype(jnp.int32), axis=0, keepdims=True)
            last = jnp.sum((down <= own).astype(jnp.int32), axis=0, keepdims=True) - 1
            at = lax.broadcasted_iota(jnp.int32, (1, QB), 1) + i * QB
            inside = (at >= start) & (at < start + IMG)
            self.span[i, 0:1, :] = first
            self.span[i, 1:2, :] = jnp.where(inside, jnp.minimum(last, start + IMG - 1), at)

        def block(i, _):
            sl = pl.ds(pl.multiple_of(i * QB, QB), QB)
            if arrive:
                arrive(i)
            x = x_ref[sl, :]
            q = jnp.dot(x, w_ref[0], preferred_element_type=f32)
            k = jnp.dot(x, w_ref[1], preferred_element_type=f32)
            v = jnp.dot(x, w_ref[2], preferred_element_type=f32)
            g = jnp.dot(g_ref[sl, :], w_ref[3], preferred_element_type=f32)
            q = turn(q, self.tables, sl, 1.0).astype(bf16).astype(f32) * HD**-0.5
            k = turn(k, self.tables, sl, 1.0).astype(bf16)
            self.data[sl, self.part(0)] = q.astype(bf16)
            self.data[sl, self.part(1)] = k
            self.data[sl, self.part(2)] = v.astype(bf16)
            self.data[sl, self.part(3)] = g.astype(bf16)
            self.kt[i] = k.astype(f32).T.astype(bf16)
            self.vt[i] = v.T.astype(bf16)
            return 0

        lax.fori_loop(0, LEN // QB, block, 0)
        self.dk[...] = jnp.zeros_like(self.dk)
        self.dv[...] = jnp.zeros_like(self.dv)

    def bounds(self, i):
        return jnp.min(self.span[i, 0:1, :]) // QB, jnp.max(self.span[i, 1:2, :]) // QB

    @staticmethod
    def sweep(low, high, body):
        def two(j, _):
            body(low + 2 * j)
            body(low + 2 * j + 1)
            return 0

        count = high + 1 - low
        lax.fori_loop(0, count // 2, two, 0)
        pl.when(count % 2 == 1)(lambda: body(high))

    def query_block(self, i, low, high, att_ref, gp_ref):
        f32, bf16, heads, width = jnp.float32, jnp.bfloat16, self.heads, self.width
        rows = pl.ds(pl.multiple_of(i * QB, QB), QB)
        lane = lax.broadcasted_iota(jnp.int32, (1, width), 1) // HD
        first, final = self.span[i, 0:1, :], self.span[i, 1:2, :]
        q, g = self.data[rows, self.part(0)], self.data[rows, self.part(3)]
        zero = jnp.zeros_like(q)
        q_own = [jnp.where(lane == h, q, zero) for h in range(heads)]
        g_own = [jnp.where(lane == h, g, zero) for h in range(heads)]
        self.m[...] = jnp.full_like(self.m, MASKED_SCORE)

        def fold(x, op):
            runs = [x[r : r + 8] for r in range(0, QB, 8)]
            lanes = runs[:8]
            for r, run in enumerate(runs[8:]):
                lanes[r % 8] = op(lanes[r % 8], run)
            while len(lanes) > 1:
                lanes = [op(a, b) for a, b in zip(lanes[::2], lanes[1::2])]
            return lanes[0]

        def score(kb):
            keys = pl.ds(pl.multiple_of(kb * QB, QB), QB)
            k, v = self.data[keys, self.part(1)], self.data[keys, self.part(2)]
            at = lax.broadcasted_iota(jnp.int32, (QB, QB), 0) + kb * QB
            bias = jnp.where((at >= first) & (at <= final), 0.0, MASKED_SCORE)
            self.bias[kb % 2] = bias
            for h in range(heads):
                s = lax.dot_general(k, q_own[h], NT, preferred_element_type=f32) + self.bias[kb % 2]
                self.s[kb, h] = s
                self.m[h] = jnp.maximum(self.m[h], fold(s, jnp.maximum))
                self.d[kb, h] = lax.dot_general(v, g_own[h], NT, preferred_element_type=f32)

        self.sweep(low, high, score)
        for h in range(heads):
            self.m[h] = jnp.broadcast_to(jnp.max(self.m[h], axis=0, keepdims=True), (8, QB))
        self.l[...] = jnp.zeros_like(self.l)
        self.ot[...] = jnp.zeros_like(self.ot)
        self.dqt[...] = jnp.zeros_like(self.dqt)

        def expo(kb):
            for h in range(heads):
                hs = slice(h * HD, (h + 1) * HD)
                e = jnp.exp(self.s[kb, h] - self.m[h, 0:1, :])
                self.l[h] += fold(e, jnp.add)
                e = e.astype(bf16)
                self.e[kb, h] = e
                self.ot[hs, :] += jnp.dot(self.vt[kb, hs, :], e, preferred_element_type=f32)

        self.sweep(low, high, expo)
        gt = g.astype(f32).T
        for h in range(heads):
            hs = slice(h * HD, (h + 1) * HD)
            inv = 1.0 / jnp.sum(self.l[h], axis=0, keepdims=True)
            self.l[h] = jnp.broadcast_to(inv, (8, QB))
            out = self.ot[hs, :] * inv
            self.ot[hs, :] = out
            delta = jnp.sum(out * gt[hs], axis=0, keepdims=True)
            self.m[h] = jnp.broadcast_to(delta, (8, QB))

        def back(kb):
            keys = pl.ds(pl.multiple_of(kb * QB, QB), QB)
            dk = self.dk[keys, :]
            dv = self.dv[keys, :]
            for h in range(heads):
                hs = slice(h * HD, (h + 1) * HD)
                p = self.e[kb, h].astype(f32) * self.l[h, 0:1, :]
                ds = (p * (self.d[kb, h] - self.m[h, 0:1, :])).astype(bf16)
                dv += jnp.dot(p.astype(bf16), g_own[h], preferred_element_type=f32)
                dk += jnp.dot(ds, q_own[h], preferred_element_type=f32)
                self.dqt[hs, :] += jnp.dot(self.kt[kb, hs, :], ds, preferred_element_type=f32)
            self.dk[keys, :] = dk
            self.dv[keys, :] = dv

        self.sweep(low, high, back)
        att_ref[rows, :] = self.ot[...].T.astype(bf16)
        dq = self.dqt[...].T * HD**-0.5
        gp_ref[rows, :width] = turn(dq, self.tables, rows, -1.0).astype(bf16)

    def finish(self, gp_ref):
        width = self.width

        def block(i, _):
            sl = pl.ds(pl.multiple_of(i * QB, QB), QB)
            dk = turn(self.dk[sl, :], self.tables, sl, -1.0)
            gp_ref[sl, width : 2 * width] = dk.astype(jnp.bfloat16)
            gp_ref[sl, 2 * width :] = self.dv[sl, :].astype(jnp.bfloat16)
            return 0

        lax.fori_loop(0, LEN // QB, block, 0)


def attention_kernel(
    heads, first, start_ref, x_ref, g_ref, w_ref, doc_ref, rope_ref, *refs
):
    att_ref, gp_ref, x_scr, g_scr, sem = refs[2:7]
    seq = pl.program_id(0) + first
    attend = Attention(heads, refs[7:])

    def fetch(seq, i):
        here = pl.ds(pl.multiple_of(i * QB, QB), QB)
        there = pl.ds(pl.multiple_of(seq * LEN + i * QB, QB), QB)
        return [
            pltpu.make_async_copy(x_ref.at[there], x_scr.at[here], sem.at[0, i]),
            pltpu.make_async_copy(g_ref.at[there], g_scr.at[here], sem.at[1, i]),
        ]

    def fetch_all(seq):
        for i in range(LEN // QB):
            for move in fetch(seq, i):
                move.start()

    def arrive(i):
        for move in fetch(seq, i):
            move.wait()

    @pl.when(pl.program_id(0) == 0)
    def _():
        fetch_all(seq)
        fill_tables(rope_ref, attend.tables)

    attend.begin(doc_ref, seq, start_ref[seq], x_scr, g_scr, w_ref, arrive)
    pl.when(pl.program_id(0) + 1 < pl.num_programs(0))(lambda: fetch_all(seq + 1))

    def query_block(i, _):
        attend.query_block(i, *attend.bounds(i), att_ref, gp_ref)
        return 0

    lax.fori_loop(0, LEN // QB, query_block, 0)
    attend.finish(gp_ref)


def attention(first, normed, grad, weights, image_start, doc_ids, earlier):
    rows, width = normed.shape[0], weights.shape[2]
    count, heads = rows // LEN, width // HD
    bf16 = jnp.bfloat16
    seq_rows = lambda s, *_: (s + first, 0)
    fixed = lambda s, *_: (0, 0)
    return pl.pallas_call(
        functools.partial(attention_kernel, heads, first),
        out_shape=[jax.ShapeDtypeStruct(e.shape, bf16) for e in earlier],
        grid_spec=pltpu.PrefetchScalarGridSpec(
            num_scalar_prefetch=1,
            grid=(count - first,),
            in_specs=[
                pl.BlockSpec(memory_space=pl.ANY),
                pl.BlockSpec(memory_space=pl.ANY),
                pl.BlockSpec((4, D, width), lambda s, *_: (0, 0, 0), pipeline_mode=pl.Buffered(1)),
                pl.BlockSpec((count, LEN), fixed),
                pl.BlockSpec((ROT, LEN), fixed),
                pl.BlockSpec(memory_space=pl.ANY),
                pl.BlockSpec(memory_space=pl.ANY),
            ],
            out_specs=[
                pl.BlockSpec((LEN, width), seq_rows),
                pl.BlockSpec((LEN, 3 * width), seq_rows),
            ],
            scratch_shapes=[
                pltpu.VMEM((LEN, D), bf16),
                pltpu.VMEM((LEN, D), bf16),
                pltpu.SemaphoreType.DMA((2, LEN // QB)),
                *Attention.scratch(heads),
            ],
        ),
        input_output_aliases={6: 0, 7: 1},
        compiler_params=pltpu.CompilerParams(
            dimension_semantics=("arbitrary",), vmem_limit_bytes=56 << 20
        ),
        cost_estimate=pl.CostEstimate(
            flops=(count - first) * LEN * (36 * 640 * width + 8 * D * width),
            bytes_accessed=(count - first) * LEN * (width * 8 + 4 * D) + 8 * D * width,
            transcendentals=(count - first) * LEN * 640 * heads,
        ),
        name="attention",
    )(image_start, normed, grad, weights, doc_ids, jnp.asarray(rope_rows()), *earlier)


def ffn_kernel(x_ref, g_ref, wgu_ref, wd_ref, hidden_ref, gg_ref, gu_ref):
    f32, bf16 = jnp.float32, jnp.bfloat16
    x = x_ref[...]
    ffn = wd_ref.shape[0]
    gate = lax.dot_general(x, wgu_ref[:ffn], NT, preferred_element_type=f32)
    up = lax.dot_general(x, wgu_ref[ffn:], NT, preferred_element_type=f32)
    grad = lax.dot_general(g_ref[...], wd_ref[...], NT, preferred_element_type=f32)
    sigma = jax.nn.sigmoid(gate)
    silu = gate * sigma
    hidden_ref[...] = (silu * up).astype(bf16)
    gg_ref[...] = (grad * up * (sigma + silu * (1.0 - sigma))).astype(bf16)
    gu_ref[...] = (grad * silu).astype(bf16)


def feed_forward(normed, grad, wffn):
    rows, ffn = normed.shape[0], wffn.shape[0] // 3
    block = lambda i: (i, 0)
    return pl.pallas_call(
        ffn_kernel,
        out_shape=[jax.ShapeDtypeStruct((rows, ffn), jnp.bfloat16)] * 3,
        grid=(rows // MB,),
        in_specs=[
            pl.BlockSpec((MB, D), block),
            pl.BlockSpec((MB, D), block),
            pl.BlockSpec((2 * ffn, D), lambda i: (0, 0), pipeline_mode=pl.Buffered(1)),
            pl.BlockSpec((ffn, D), lambda i: (2, 0), pipeline_mode=pl.Buffered(1)),
        ],
        out_specs=[pl.BlockSpec((MB, ffn), block)] * 3,
        compiler_params=pltpu.CompilerParams(
            dimension_semantics=("arbitrary",), vmem_limit_bytes=56 << 20
        ),
        cost_estimate=pl.CostEstimate(
            flops=6 * rows * D * ffn,
            bytes_accessed=rows * (4 * D + 6 * ffn) + 6 * D * ffn,
            transcendentals=rows * ffn,
        ),
        name="feed_forward",
    )(normed, grad, wffn, wffn)


def flip(index, bits):
    bit = 1
    while bit <= bits:
        if bits & bit:
            index = index + bit - 2 * bit * ((index // bit) % 2)
        bit *= 2
    return index


def chip_orders(ways):
    bits = [1 << k for k in range(1, ways.bit_length() - 1)]
    return bits, bits[::-1]


def held(bits):
    found = [0]
    for bit in bits:
        found += [o ^ bit for o in found]
    return found


def meet(peers):
    barrier = pltpu.get_barrier_semaphore()
    for peer in peers:
        pl.semaphore_signal(barrier, inc=1, device_id=peer, device_id_type=MESH)
    pl.semaphore_wait(barrier, len(peers))


def gather_kernel(ways, base, attended, count, *refs):
    f32, bf16 = jnp.float32, jnp.bfloat16
    me = lax.axis_index("col")
    if attended:
        (token_ref, cot_ref, vectors_ref, w_ref, rope_ref, doc_ref, image_ref, old_ref) = refs[:8]
        (old_normed, old_grad, normed_ref, full_ref, stat_ref, att_ref, gp_ref) = refs[8:15]
        refs = refs[15:]
    else:
        (token_ref, cot_ref, vector_ref, gate_ref, down_ref) = refs[:5]
        (normed_ref, full_ref, stat_ref, vectors_ref, ffn_ref) = refs[5:10]
        refs = refs[10:]
    (both, load_sem, store_sem, full_sem, send_sem, recv_sem) = refs[:6]
    refs = refs[6:]
    width = token_ref.shape[1]
    rows = both.shape[1]
    pairs = rows // count
    orders = chip_orders(ways)
    phases = len(orders[0])
    mine = pl.ds(pl.multiple_of(me * width, width), width)
    source = pl.ds(base, rows)
    loads = [
        pltpu.make_async_copy(token_ref.at[source], both.at[me, :, pl.ds(0, width)], load_sem.at[0]),
        pltpu.make_async_copy(cot_ref.at[source], both.at[me, :, pl.ds(width, width)], load_sem.at[1]),
    ]
    for load in loads:
        load.start()
    peers = [flip(me, k) for k in range(1, ways)]
    if attended:
        meet([{"col": flip(me, 1 << k)} for k in range(ways.bit_length() - 1)])
    else:
        vectors_ref[:, mine] = vector_ref[...]
        meet([{"col": peer} for peer in peers])

    def vector_copy(k):
        return pltpu.make_async_remote_copy(
            src_ref=vectors_ref.at[:, mine],
            dst_ref=vectors_ref.at[:, mine],
            send_sem=refs[0].at[k],
            recv_sem=refs[1].at[k],
            device_id={"col": peers[k]},
            device_id_type=MESH,
        )

    def copies(p, phase):
        for k, order in enumerate(orders):
            bit = order[phase] if phase < phases else 1
            place = pl.ds(pl.multiple_of(p * count + k * (count // 2), count // 2), count // 2)
            for o in held(order[:phase]):
                index = k * ways + (o ^ bit)
                owner = flip(me, o)
                yield pltpu.make_async_remote_copy(
                    src_ref=both.at[owner, place],
                    dst_ref=both.at[owner, place],
                    send_sem=send_sem.at[p, index],
                    recv_sem=recv_sem.at[p, index],
                    device_id={"col": flip(me, bit)},
                    device_id_type=MESH,
                )

    def start(p, phase):
        for copy in copies(p, phase):
            copy.start()

    def arrive(p, phase):
        for copy in copies(p, phase):
            copy.wait_recv()

    def filed(p, first, out_ref, sem):
        place = pl.ds(pl.multiple_of(p * count, count), count)
        goal = pl.ds(pl.multiple_of(base + p * count, count), count)
        for b in range(ways):
            pltpu.make_async_copy(
                both.at[b, place, pl.ds(first, width)],
                out_ref.at[goal, pl.ds(b * width, width)],
                sem.at[p],
            ).start()

    def filed_wait(p, out_ref, sem):
        place = out_ref.at[pl.ds(base + p * count, count)]
        pltpu.make_async_copy(place, place, sem.at[p]).wait()

    def norm(p):
        filed(p, width, full_ref, full_sem)
        for phase in range(phases + 1):
            for copy in copies(p, phase):
                copy.wait_send()

        def block(j, _):
            at = pl.ds(pl.multiple_of(p * count + j * QB, QB), QB)
            goal = pl.ds(pl.multiple_of(base + p * count + j * QB, QB), QB)
            sums = sum(both[b, at, :width].astype(f32) for b in range(ways))
            mean = jnp.sum(sums, axis=1, keepdims=True) / D
            squares = jnp.zeros((QB, width), f32)
            for b in range(ways):
                x = both[b, at, :width].astype(f32) - mean
                squares += x * x
            inv = lax.rsqrt(jnp.sum(squares, axis=1, keepdims=True) / D + NORM_EPS)
            stat_ref[goal, :1] = mean
            stat_ref[goal, 1:] = inv
            for b in range(ways):
                cols = slice(b * width, (b + 1) * width)
                x = (both[b, at, :width].astype(f32) - mean) * inv
                x = x * vectors_ref[0:1, cols] + vectors_ref[1:2, cols]
                both[b, at, :width] = x.astype(bf16)
            return 0

        lax.fori_loop(0, count // QB, block, 0)
        filed(p, 0, normed_ref, store_sem)

    if attended:
        x_scr, g_scr, att_scr, gp_scr, in_sem, out_sem = refs[:6]
        attend = Attention(width // HD, refs[6:])
        stat_ref[pl.ds(0, base), :] = old_ref[pl.ds(0, base), :]

        def fetch(seq):
            place = pl.ds(pl.multiple_of(seq * LEN, LEN), LEN)
            return [
                pltpu.make_async_copy(old_normed.at[place], x_scr, in_sem.at[seq, 0]),
                pltpu.make_async_copy(old_grad.at[place], g_scr, in_sem.at[seq, 1]),
            ]

        def give(seq):
            place = pl.ds(pl.multiple_of(seq * LEN, LEN), LEN)
            return [
                pltpu.make_async_copy(att_scr.at[seq], att_ref.at[place], out_sem.at[seq, 0]),
                pltpu.make_async_copy(gp_scr.at[seq], gp_ref.at[place], out_sem.at[seq, 1]),
            ]

        for move in fetch(0):
            move.start()

    for load in loads:
        load.wait()
    start(0, 0)
    start(1, 0)
    if attended:
        fill_tables(rope_ref, attend.tables)
    else:
        ffn_scr, ffn_sem = refs[2:4]
        split = gate_ref.shape[0]
        moves = [
            pltpu.make_async_copy(gate_ref, ffn_scr.at[pl.ds(0, split)], ffn_sem.at[0]),
            pltpu.make_async_copy(down_ref, ffn_scr.at[pl.ds(split, split // 2)], ffn_sem.at[1]),
        ]
        for move in moves:
            move.start()
        for move in moves:
            move.wait()
        laid = pltpu.make_async_copy(ffn_scr, ffn_ref, ffn_sem.at[2])
        laid.start()
        for k in range(ways - 1):
            vector_copy(k).start()
        for k in range(ways - 1):
            vector_copy(k).wait_recv()
    blocks = LEN // QB
    turns = attended * blocks // pairs if attended else 0

    def step(p, _):
        for phase in range(phases):
            if phase or attended:
                arrive(p, phase)
                start(p, phase + 1)
            if phase == 0:
                if attended:
                    pl.when(p + 2 < pairs)(lambda: start(p + 2, 0))
                else:

                    @pl.when(p + 1 < pairs)
                    def _():
                        arrive(p + 1, 0)
                        start(p + 1, 1)

                    pl.when(p + 3 < pairs)(lambda: start(p + 3, 0))

                @pl.when(p >= 1)
                def _():
                    arrive(p - 1, phases)
                    norm(p - 1)

                if attended:
                    seq = p * turns // blocks
                    spot = p * turns % blocks

                    @pl.when(spot == 0)
                    def _():
                        for move in fetch(seq):
                            move.wait()
                        attend.begin(doc_ref, seq, image_ref[seq], x_scr, g_scr, w_ref)

                        @pl.when(seq + 1 < attended)
                        def _():
                            for move in fetch(seq + 1):
                                move.start()

                    def query_block(i, _):
                        low = i // (blocks - 1)
                        attend.query_block(i, low, i + 1 - low, att_scr.at[seq], gp_scr.at[seq])
                        return 0

                    lax.fori_loop(spot, spot + turns, query_block, 0)

                    @pl.when(spot + turns == blocks)
                    def _():
                        attend.finish(gp_scr.at[seq])
                        for move in give(seq):
                            move.start()
        return 0

    if not attended:
        arrive(0, 0)
        start(0, 1)
        start(2, 0)
    lax.fori_loop(0, pairs, step, 0)
    arrive(pairs - 1, phases)
    norm(pairs - 1)
    for p in range(pairs):
        filed_wait(p, full_ref, full_sem)
        filed_wait(p, normed_ref, store_sem)
    if attended:
        for seq in range(attended):
            for move in give(seq):
                move.wait()
    else:
        laid.wait()
        for k in range(ways - 1):
            vector_copy(k).wait_send()


def gather_scratch(ways, rows, width, count):
    dma = pltpu.SemaphoreType.DMA
    pairs = rows // count
    return [
        pltpu.VMEM((ways, rows, 2 * width), jnp.bfloat16),
        dma((2,)),
        dma((pairs,)),
        dma((pairs,)),
        dma((pairs, 2 * ways)),
        dma((pairs, 2 * ways)),
    ]


def gather_first(tokens, out_grad, vectors, gate_up, down, count, ways):
    rows, width = tokens.shape
    bf16, f32 = jnp.bfloat16, jnp.float32
    anywhere = pl.BlockSpec(memory_space=pl.ANY)
    vmem = pl.BlockSpec(memory_space=pltpu.VMEM)
    dma = pltpu.SemaphoreType.DMA
    return pl.pallas_call(
        functools.partial(gather_kernel, ways, 0, 0, GB),
        out_shape=[
            jax.ShapeDtypeStruct((rows, D), bf16),
            jax.ShapeDtypeStruct((rows, D), bf16),
            jax.ShapeDtypeStruct((rows, 2), f32),
            jax.ShapeDtypeStruct((8, D), f32),
            jax.ShapeDtypeStruct((3 * down.shape[0], down.shape[1]), bf16),
        ],
        in_specs=[anywhere, anywhere, vmem, anywhere, anywhere],
        out_specs=[anywhere, anywhere, vmem, vmem, anywhere],
        scratch_shapes=[
            *gather_scratch(ways, count, width, GB),
            dma((ways - 1,)),
            dma((ways - 1,)),
            pltpu.VMEM((3 * down.shape[0], down.shape[1]), bf16),
            dma((3,)),
        ],
        compiler_params=pltpu.CompilerParams(
            collective_id=0, has_side_effects=True, vmem_limit_bytes=63 << 20
        ),
        cost_estimate=pl.CostEstimate(
            flops=100 * count * D * D // ways, bytes_accessed=count * D * 8, transcendentals=0
        ),
        name="gather_first",
    )(tokens, out_grad, vectors, gate_up, down)


def gather_rest(tokens, out_grad, vectors, weights, doc_ids, image_start, stats, normed, grad, ways):
    rows, width = tokens.shape
    count = rows // 2
    bf16, f32 = jnp.bfloat16, jnp.float32
    anywhere = pl.BlockSpec(memory_space=pl.ANY)
    vmem = pl.BlockSpec(memory_space=pltpu.VMEM)
    dma = pltpu.SemaphoreType.DMA
    seqs = count // LEN
    return pl.pallas_call(
        functools.partial(gather_kernel, ways, count, seqs, GA),
        out_shape=[
            jax.ShapeDtypeStruct((rows, D), bf16),
            jax.ShapeDtypeStruct((rows, D), bf16),
            jax.ShapeDtypeStruct((rows, 2), f32),
            jax.ShapeDtypeStruct((rows, width), bf16),
            jax.ShapeDtypeStruct((rows, 3 * width), bf16),
        ],
        in_specs=[
            anywhere,
            anywhere,
            vmem,
            vmem,
            vmem,
            vmem,
            pl.BlockSpec(memory_space=pltpu.SMEM),
            vmem,
            anywhere,
            anywhere,
        ],
        out_specs=[anywhere, anywhere, vmem, anywhere, anywhere],
        input_output_aliases={8: 0, 9: 1},
        scratch_shapes=[
            *gather_scratch(ways, rows - count, width, GA),
            pltpu.VMEM((LEN, D), bf16),
            pltpu.VMEM((LEN, D), bf16),
            pltpu.VMEM((seqs, LEN, width), bf16),
            pltpu.VMEM((seqs, LEN, 3 * width), bf16),
            dma((seqs, 2)),
            dma((seqs, 2)),
            *Attention.scratch(width // HD),
        ],
        compiler_params=pltpu.CompilerParams(
            collective_id=3, has_side_effects=True, vmem_limit_bytes=63 << 20
        ),
        cost_estimate=pl.CostEstimate(
            flops=100 * count * D * D // ways, bytes_accessed=count * D * 8, transcendentals=0
        ),
        name="gather_rest",
    )(tokens, out_grad, vectors, weights, jnp.asarray(rope_rows()), doc_ids, image_start, stats, normed, grad)


class Reducer:
    def __init__(self, ways, parts, inbox, send_sem, recv_sem):
        self.ways, self.parts, self.inbox = ways, parts, inbox
        self.send_sem, self.recv_sem = send_sem, recv_sem
        self.me = lax.axis_index("col")
        self.orders = chip_orders(ways)
        self.phases = 1 + len(self.orders[0])

    def moves(self, step, phase):
        halves = [None] if phase == 0 else [0, 1]
        for k in halves:
            order = [1] if phase == 0 else [1, *self.orders[k]]
            bit = order[phase]
            done = sum(order[:phase])
            count = RB if k is None else RB // 2
            rows = pl.ds(pl.multiple_of(step * RB + (k or 0) * count, count), count)
            for o in range(self.ways):
                if o & done or not o & bit:
                    continue
                goal = o ^ bit
                slot = slot_of(self.ways, self.orders, phase, k, goal)
                sem = 2 * slot + (k or 0)
                copy = pltpu.make_async_remote_copy(
                    src_ref=self.parts.at[o, rows],
                    dst_ref=self.inbox.at[slot, rows],
                    send_sem=self.send_sem.at[step, sem],
                    recv_sem=self.recv_sem.at[step, sem],
                    device_id={"col": flip(self.me, bit)},
                    device_id_type=MESH,
                )
                yield copy, goal, slot, rows

    def send(self, step, phase):
        for copy, *_ in self.moves(step, phase):
            copy.start()

    def absorb(self, step, phase):
        out = []
        for copy, goal, slot, rows in self.moves(step, phase):
            copy.wait_recv()
            value = self.parts[goal, rows, :].astype(jnp.float32)
            value += self.inbox[slot, rows, :].astype(jnp.float32)
            if phase == self.phases - 1:
                out.append(value)
            else:
                self.parts[goal, rows, :] = value.astype(jnp.bfloat16)
        return out

    def finish(self, step):
        for phase in range(self.phases):
            for copy, *_ in self.moves(step, phase):
                copy.wait_send()

    def advance(self, t, steps, lags):
        pl.when(t < steps)(lambda: self.send(t, 0))
        for phase in range(self.phases - 1):
            s = t - lags[phase]

            @pl.when((s >= 0) & (s < steps))
            def _():
                self.absorb(s, phase)
                self.send(s, phase + 1)


def slot_of(ways, orders, phase, half, goal):
    if phase == 0:
        return goal // 2
    order = [1, *orders[half]]
    base = ways // 2
    for p in range(1, phase):
        base += ways >> (p + 1)
    goals = [g for g in range(ways) if not g & sum(order[: phase + 1])]
    return base + goals.index(goal)


def lags_of(ways):
    return [1 + 2 * p for p in range(len(chip_orders(ways)[0]) + 1)]


def reducer_scratch(ways, rows, width):
    steps = rows // RB
    return [
        pltpu.VMEM((ways, rows, width), jnp.bfloat16),
        pltpu.VMEM((ways - 1, rows, width), jnp.bfloat16),
        pltpu.SemaphoreType.DMA((steps, 2 * ways)),
        pltpu.SemaphoreType.DMA((steps, 2 * ways)),
    ]


def branch_kernel(
    ways,
    steps,
    att_ref,
    hidden_ref,
    grad_ref,
    token_ref,
    wout_ref,
    wd_ref,
    out_ref,
    wgrad_ref,
    parts,
    inbox,
    send_sem,
    recv_sem,
    acc,
    acc_out,
):
    f32, bf16 = jnp.float32, jnp.bfloat16
    t = pl.program_id(0)
    me, width = lax.axis_index("col"), D // ways
    lags = lags_of(ways)
    ring = Reducer(ways, parts, inbox, send_sem, recv_sem)

    @pl.when(t == 0)
    def _():
        acc[...] = jnp.zeros_like(acc)
        acc_out[...] = jnp.zeros_like(acc_out)
        meet([{"col": flip(me, 1 << k)} for k in range(ways.bit_length() - 1)])

    @pl.when(t < steps)
    def _():
        rows = pl.ds(pl.multiple_of(t * RB, RB), RB)
        att, hidden = att_ref[...], hidden_ref[...]
        total = jnp.dot(hidden, wd_ref[...], preferred_element_type=f32)
        total += lax.dot_general(att, wout_ref[...], NT, preferred_element_type=f32)
        for b in range(ways):
            parts[flip(me, b), rows, :] = total[:, b * width : (b + 1) * width].astype(bf16)

    ring.advance(t, steps, lags)

    @pl.when(t < steps)
    def _():
        acc[...] += contract(hidden_ref[...], grad_ref[...], 0, 0)
        acc_out[...] += contract(att_ref[...], grad_ref[...], 0, 0)

    @pl.when(t == steps)
    def _():
        ffn = acc.shape[0]
        wgrad_ref[:ffn, :] = acc[...].astype(bf16)
        wgrad_ref[ffn:, :] = acc_out[...].astype(bf16)

    s = t - lags[-1]

    @pl.when(s >= 0)
    def _():
        for k, value in enumerate(ring.absorb(s, ring.phases - 1)):
            half = slice(k * (RB // 2), (k + 1) * (RB // 2))
            out_ref[half, :] = (token_ref[half, :].astype(f32) + value).astype(bf16)
        ring.finish(s)


def branches(att, hidden, grad, tokens, weights, wffn, ways):
    rows, width = tokens.shape
    ffn = wffn.shape[0] // 3
    steps = rows // RB
    lag = lags_of(ways)[-1]
    now = lambda t: (jnp.minimum(t, steps - 1), 0)
    late = lambda t: (jnp.maximum(t - lag, 0), 0)
    fixed = lambda t: (0, 0)
    once = pl.Buffered(1)
    return pl.pallas_call(
        functools.partial(branch_kernel, ways, steps),
        out_shape=[
            jax.ShapeDtypeStruct((rows, width), jnp.bfloat16),
            jax.ShapeDtypeStruct((ffn + width, D), jnp.bfloat16),
        ],
        grid=(steps + lag,),
        in_specs=[
            pl.BlockSpec((RB, width), now),
            pl.BlockSpec((RB, ffn), now),
            pl.BlockSpec((RB, D), now),
            pl.BlockSpec((RB, width), late),
            pl.BlockSpec((None, D, width), lambda t: (3, 0, 0), pipeline_mode=once),
            pl.BlockSpec((ffn, D), lambda t: (2, 0), pipeline_mode=once),
        ],
        out_specs=[
            pl.BlockSpec((RB, width), late),
            pl.BlockSpec((ffn + width, D), fixed, pipeline_mode=once),
        ],
        scratch_shapes=[
            *reducer_scratch(ways, rows, width),
            pltpu.VMEM((ffn, D), jnp.float32),
            pltpu.VMEM((width, D), jnp.float32),
        ],
        compiler_params=pltpu.CompilerParams(
            collective_id=1,
            has_side_effects=True,
            dimension_semantics=("arbitrary",),
            vmem_limit_bytes=60 << 20,
        ),
        cost_estimate=pl.CostEstimate(
            flops=8 * rows * D * (2 * ffn + width), bytes_accessed=4 * rows * D, transcendentals=0
        ),
        name="branches",
    )(att, hidden, grad, tokens, weights, wffn)


def back_kernel(
    ways,
    lines,
    steps,
    gp_ref,
    gg_ref,
    gu_ref,
    x_ref,
    token_ref,
    cot_ref,
    stat_ref,
    w_ref,
    wgu_ref,
    vectors_ref,
    gain_ref,
    wqkv_ref,
    out_ref,
    vgrad_ref,
    qkv_ref,
    parts,
    inbox,
    send_sem,
    recv_sem,
    sums,
    ssend_sem,
    srecv_sem,
    acc,
    vsend_sem,
    vrecv_sem,
):
    f32, bf16 = jnp.float32, jnp.bfloat16
    t = pl.program_id(0)
    me, width = lax.axis_index("col"), D // ways
    line = lax.axis_index("row")
    lags = lags_of(ways)
    ring = Reducer(ways, parts, inbox, send_sem, recv_sem)

    @pl.when(t == 0)
    def _():
        acc[...] = jnp.zeros_like(acc)
        meet(
            [{"col": flip(me, k)} for k in range(1, ways)]
            + [{"row": (line + k) % lines} for k in range(1, lines)]
        )

    def sum_copies(group):
        rows = pl.ds(pl.multiple_of(group * RB, RB), RB)
        for k in range(1, ways):
            yield pltpu.make_async_remote_copy(
                src_ref=sums.at[0, :, rows],
                dst_ref=sums.at[k, :, rows],
                send_sem=ssend_sem.at[group, k - 1],
                recv_sem=srecv_sem.at[group, k - 1],
                device_id={"col": flip(me, k)},
                device_id_type=MESH,
            )

    @pl.when(t < steps)
    def _():
        rows = pl.ds(pl.multiple_of(t * RB, RB), RB)
        gp, gg, gu = gp_ref[...], gg_ref[...], gu_ref[...]
        total = jnp.dot(gg, wgu_ref[: gg.shape[1]], preferred_element_type=f32)
        total += jnp.dot(gu, wgu_ref[gg.shape[1] :], preferred_element_type=f32)
        for kind in range(3):
            part = gp[:, kind * width : (kind + 1) * width]
            total += lax.dot_general(part, w_ref[kind], NT, preferred_element_type=f32)
        for b in range(ways):
            parts[flip(me, b), rows, :] = total[:, b * width : (b + 1) * width].astype(bf16)
        scaled = x_ref[...].astype(f32) - vectors_ref[1:2, :]
        plain = jnp.sum(total * vectors_ref[0:1, :], axis=1, keepdims=True)
        cross = jnp.sum(total * scaled, axis=1, keepdims=True)
        lane = lax.broadcasted_iota(jnp.int32, (RB, 128), 1)
        spot = 2 * (t % SUMS)
        pair = jnp.where(lane == spot, plain, jnp.where(lane == spot + 1, cross, 0.0))
        group = pl.ds(pl.multiple_of(t // SUMS * RB, RB), RB)
        before = jnp.where(jnp.broadcast_to(spot == 0, (8, RB)), 0.0, sums[0, :, group])
        sums[0, :, group] = before + pair.T[:8]
        for kind in range(3):
            qkv_ref[kind] = wqkv_ref[:, kind * width : (kind + 1) * width].astype(f32)

        @pl.when(t % SUMS == SUMS - 1)
        def _():
            for copy in sum_copies(t // SUMS):
                copy.start()

    ring.advance(t, steps, lags)
    s = t - lags[-1]

    @pl.when(s >= 0)
    def _():
        @pl.when(s % SUMS == 0)
        def _():
            for copy in sum_copies(s // SUMS):
                copy.wait_recv()

        group = pl.ds(pl.multiple_of(s // SUMS * RB, RB), RB)
        both = sum(sums[k, :, group] for k in range(ways)).T
        lane = lax.broadcasted_iota(jnp.int32, (RB, 8), 1)
        spot = 2 * (s % SUMS)
        plain = jnp.sum(jnp.where(lane == spot, both, 0.0), axis=1, keepdims=True) / D
        cross = jnp.sum(jnp.where(lane == spot + 1, both, 0.0), axis=1, keepdims=True) / D
        for k, value in enumerate(ring.absorb(s, ring.phases - 1)):
            half = slice(k * (RB // 2), (k + 1) * (RB // 2))
            inv = stat_ref[half, 1:]
            unit = (token_ref[half, :].astype(f32) - stat_ref[half, :1]) * inv
            scaled = value * gain_ref[0:1, :]
            out_ref[half, :] = cot_ref[half, :].astype(f32) + inv * (
                scaled - plain[half] - unit * cross[half]
            )
            acc[0, 0:1, :] += jnp.sum(value * unit, axis=0, keepdims=True)
            acc[0, 1:2, :] += jnp.sum(value, axis=0, keepdims=True)

        @pl.when(s % SUMS == 0)
        def _():
            for copy in sum_copies(s // SUMS):
                copy.wait_send()

        ring.finish(s)

    @pl.when(t == pl.num_programs(0) - 1)
    def _():
        copies = [
            pltpu.make_async_remote_copy(
                src_ref=acc.at[0],
                dst_ref=acc.at[k],
                send_sem=vsend_sem.at[k - 1],
                recv_sem=vrecv_sem.at[k - 1],
                device_id={"row": (line + k) % lines},
                device_id_type=MESH,
            )
            for k in range(1, lines)
        ]
        for copy in copies:
            copy.start()
        for copy in copies:
            copy.wait()
        vgrad_ref[...] = sum(acc[k] for k in range(lines))


def norm_back(
    gp, gg, gu, normed, tokens, cot, stats, weights, wffn, vectors, own, qkv, ways, lines
):
    rows, width = tokens.shape
    ffn = gg.shape[1]
    steps = rows // RB
    lag = lags_of(ways)[-1]
    deep = qkv.shape[0]
    slab = deep // steps
    now = lambda t: (jnp.minimum(t, steps - 1), 0)
    late = lambda t: (jnp.maximum(t - lag, 0), 0)
    fixed = lambda t: (0, 0)
    once = pl.Buffered(1)
    dma = pltpu.SemaphoreType.DMA
    return pl.pallas_call(
        functools.partial(back_kernel, ways, lines, steps),
        out_shape=[
            jax.ShapeDtypeStruct((rows, width), jnp.float32),
            jax.ShapeDtypeStruct((8, width), jnp.float32),
            jax.ShapeDtypeStruct((3, deep, width), jnp.float32),
        ],
        grid=(steps + lag,),
        in_specs=[
            pl.BlockSpec((RB, 3 * width), now),
            pl.BlockSpec((RB, ffn), now),
            pl.BlockSpec((RB, ffn), now),
            pl.BlockSpec((RB, D), now),
            pl.BlockSpec((RB, width), late),
            pl.BlockSpec((RB, width), late),
            pl.BlockSpec((RB, 2), late),
            pl.BlockSpec((3, D, width), lambda t: (0, 0, 0), pipeline_mode=once),
            pl.BlockSpec((2 * ffn, D), fixed, pipeline_mode=once),
            pl.BlockSpec((8, D), fixed),
            pl.BlockSpec((8, width), fixed),
            pl.BlockSpec((slab, 3 * width), now),
        ],
        out_specs=[
            pl.BlockSpec((RB, width), late),
            pl.BlockSpec((8, width), fixed),
            pl.BlockSpec((3, slab, width), lambda t: (0, jnp.minimum(t, steps - 1), 0)),
        ],
        scratch_shapes=[
            *reducer_scratch(ways, rows, width),
            pltpu.VMEM((ways, 8, rows // SUMS), jnp.float32),
            dma((steps // SUMS, ways - 1)),
            dma((steps // SUMS, ways - 1)),
            pltpu.VMEM((lines, 8, width), jnp.float32),
            dma((lines - 1,)),
            dma((lines - 1,)),
        ],
        compiler_params=pltpu.CompilerParams(
            collective_id=2,
            has_side_effects=True,
            dimension_semantics=("arbitrary",),
            vmem_limit_bytes=61 << 20,
        ),
        cost_estimate=pl.CostEstimate(
            flops=4 * rows * D * (2 * ffn + 3 * width), bytes_accessed=6 * rows * D, transcendentals=0
        ),
        name="norm_back",
    )(gp, gg, gu, normed, tokens, cot, stats, weights, wffn, vectors, own, qkv)


def after(value, *others):
    return lax.optimization_barrier((value, others))[0]


def local(
    tokens,
    norm_gain,
    norm_bias,
    qkv_weight,
    gate_up_weight,
    out_weight,
    down_weight,
    image_start,
    doc_ids,
    out_grad,
):
    f32, bf16 = jnp.float32, jnp.bfloat16
    block_rows, width = tokens.shape
    ways = D // width
    lines = D // qkv_weight.shape[0]

    own = jnp.concatenate([jnp.transpose(qkv_weight, (1, 0, 2)), out_weight[None]], axis=0)
    weights = lax.all_gather(own, "row", axis=1, tiled=True)
    own_vectors = jnp.pad(jnp.stack([norm_gain, norm_bias]), ((0, 6), (0, 0)))

    half = block_rows // 2
    normed, grad, stats, vectors, own_ffn = gather_first(
        tokens,
        out_grad,
        own_vectors,
        jnp.transpose(gate_up_weight, (1, 2, 0)).reshape(-1, D // lines),
        jnp.transpose(down_weight, (1, 0)),
        half,
        ways,
    )
    wffn = lax.all_gather(own_ffn, "row", axis=1, tiled=True)
    normed, grad, stats, *earlier = gather_rest(
        tokens, out_grad, vectors, weights, doc_ids, image_start, stats, normed, grad, ways
    )
    attended, grad_projected = attention(
        half // LEN, normed, grad, weights, image_start, doc_ids, earlier
    )

    def weight_sum(grad):
        return lax.psum_scatter(grad, "row", scatter_dimension=0, tiled=True)

    def weight_grad(left, right):
        return contract(left, right, 0, 0).astype(bf16)

    grad_qkv = weight_grad(normed, grad_projected)
    hidden, grad_gate, grad_up = feed_forward(after(normed, grad_qkv), grad, wffn)
    weight_gate = weight_grad(normed, grad_gate)
    weight_up = weight_grad(normed, after(grad_up, weight_gate))
    qkv_sum = weight_sum(grad_qkv)
    gate_sum = weight_sum(weight_gate)
    outputs, weight_rest = branches(
        after(attended, weight_up, qkv_sum), hidden, grad, tokens, weights, wffn, ways
    )
    input_grad, vector_grads, qkv_sum = norm_back(
        after(grad_projected, outputs, gate_sum),
        grad_gate,
        grad_up,
        normed,
        tokens,
        out_grad,
        stats,
        weights,
        wffn,
        vectors,
        own_vectors,
        qkv_sum,
        ways,
        lines,
    )
    qkv_sum = jnp.transpose(qkv_sum, (1, 0, 2))
    up_sum = after(weight_sum(weight_up), input_grad)
    rest = weight_sum(jnp.transpose(weight_rest, (1, 0)))
    down_sum, out_sum = rest[:, :-width].astype(f32), rest[:, -width:].astype(f32)
    gate_up_sum = jnp.stack([gate_sum.astype(f32), up_sum.astype(f32)], axis=1)
    return (
        outputs,
        input_grad,
        vector_grads[0],
        vector_grads[1],
        qkv_sum,
        gate_up_sum,
        out_sum,
        down_sum,
    )


def solution(mesh):
    placed = (
        P("row", "col"),
        P("col"),
        P("col"),
        P("row", None, "col"),
        P("row", None, "col"),
        P("row", "col"),
        P("row", "col"),
        P("row"),
        P("row", None),
        P("row", "col"),
    )
    return jax.shard_map(
        local,
        mesh=mesh,
        in_specs=placed,
        out_specs=(
            P("row", "col"),
            P("row", "col"),
            P("col"),
            P("col"),
            P("row", None, "col"),
            P("row", None, "col"),
            P("row", "col"),
            P("row", "col"),
        ),
        check_vma=False,
    )
```
